32 devices in a mesh: seq: 4 (over z), clip: 8 (over y, x, core).
Axes of the slice: x: 2, y: 2, z: 4, core: 2. Of those that a mesh axis runs over, the one named last changes fastest.
Arguments:
- clip_features: bfloat16 [8, 4, 8, 64, 384], P('clip', None, 'seq'), may hold values from -6 to 6
- enc_weight: bfloat16 [3, 3, 3, 384, 16], replicated, may hold values from -0.0625 to 0.0625
- noise_field: float32 [8, 4, 8, 64, 16], P('clip', None, 'seq'), may hold values from -6 to 6
- flow_times: int32 [8, 2], P('clip'), may hold values from 0 to 1000, as said below
- embed_weight: bfloat16 [64, 5120], replicated, may hold values from -0.75 to 0.75
- time_weight: bfloat16 [256, 5120], replicated, may hold values from -0.375 to 0.375
- norm_gain: float32 [5120], replicated, may hold values from 0.25 to 1.75
- qkv_weight: bfloat16 [5120, 3, 3072], P('clip', None, 'seq'), may hold values from -0.078125 to 0.078125
Outputs:
- attn_out: bfloat16 [8, 512, 3072], P('clip', 'seq')
- attn_tangent: bfloat16 [8, 512, 3072], P('clip', 'seq')
The draws below stay inside these ranges and needn't reach their ends.
Inputs may be any that keep to these rules, and one draw needn't show every extreme that they name: flow_times[c] = (index of r, index of t) with the index of r at most that of t; some clip has r index 0 and some t index 1000.
All inputs are finite; a program needn't handle non-finite values.
Results may differ from the reference program's by a relative error of at most 0.0044.
Values may be sent and summed in bfloat16 or wider, within the bound.
A program may use at most 128 MiB of HBM per device.

```python
import jax
import jax.numpy as jnp
from jax import lax

D = 5120
Z = 16
C = 384
HD = 128
HEADS = 24
TFEAT = 256
TGRID = 1000
FR = 4
WL = 64
INNER = 3072
PATCH = 64
HT = 8
CLIPS = 8


def draw_flow_times(key, part):
    key_one, key_two = jax.random.split(jax.random.fold_in(key, 17))
    draw_one = jax.random.randint(key_one, (CLIPS,), 0, TGRID + 1)
    draw_two = jax.random.randint(key_two, (CLIPS,), 0, TGRID + 1)
    start_idx = jnp.minimum(draw_one, draw_two).at[0].set(0)
    finish_idx = jnp.maximum(draw_one, draw_two).at[CLIPS - 1].set(TGRID)
    return jnp.stack([start_idx, finish_idx], axis=1).astype(jnp.int32)


def steps_of(key, shape, cuts, smallest, largest):
    def one(axis_at, blocks):
        steps = jax.random.uniform(jax.random.fold_in(jax.random.fold_in(key, 6), axis_at), (blocks,), jnp.float32, smallest / len(cuts), largest / len(cuts))
        return jnp.repeat(jnp.exp(steps), shape[axis_at] // blocks).reshape((-1,) + (1,) * (len(shape) - axis_at - 1))

    factor_of = one(*cuts[0])
    for cut in cuts[1:]:
        factor_of = factor_of * one(*cut)
    return factor_of


def scatter_about(own_key, shape, width, limit, pieces=(), kind=jnp.bfloat16):
    entries = jax.random.normal(own_key, shape, jnp.float32) * width
    if len(pieces) > 0:
        entries = steps_of(own_key, shape, pieces, -0.22, 0.18) * entries
    return jnp.clip(entries, min=-limit, max=limit).astype(kind)


def setup_inputs(seed: int = 0) -> dict:
    seeds = jax.random.split(jax.random.key(seed), 9)
    clip_features = scatter_about(seeds[0], (CLIPS, FR, HT, WL, C), 1.0, 6.0, ((0, 8), (2, 4)))
    enc_weight = scatter_about(seeds[1], (3, 3, 3, C, Z), (27 * C) ** -0.5, 0.0625)
    noise_field = scatter_about(seeds[2], (CLIPS, FR, HT, WL, Z), 1.0, 6.0, ((0, 8), (2, 4)), jnp.float32)
    flow_times = draw_flow_times(jax.random.fold_in(seeds[8], 71), 0)
    embed_weight = scatter_about(seeds[4], (PATCH, D), PATCH ** -0.5, 0.75)
    time_weight = scatter_about(seeds[5], (TFEAT, D), TFEAT ** -0.5, 0.375)
    norm_gain = jnp.clip(1.0 + 0.15 * jax.random.normal(seeds[6], (D,), jnp.float32), 0.25, 1.75)
    qkv_weight = scatter_about(seeds[7], (D, 3, INNER), D ** -0.5, 0.078125, ((0, 8), (2, 4)))
    return {"clip_features": clip_features, "enc_weight": enc_weight, "noise_field": noise_field, "flow_times": flow_times, "embed_weight": embed_weight, "time_weight": time_weight, "norm_gain": norm_gain, "qkv_weight": qkv_weight}


EPSILON = 1e-06

def time_features(flow_t, flow_h):
    quarter = TFEAT // 4
    freqs_omega = 8.0 * jnp.exp(-jnp.log(100.0) * jnp.arange(quarter, dtype=jnp.float32) / quarter)
    angle_t = freqs_omega * flow_t
    angle_h = freqs_omega * flow_h
    values = jnp.concatenate([jnp.sin(angle_t), jnp.cos(angle_t), jnp.sin(angle_h), jnp.cos(angle_h)])
    tangent = jnp.concatenate([freqs_omega * jnp.cos(angle_t), -freqs_omega * jnp.sin(angle_t), freqs_omega * jnp.cos(angle_h), -freqs_omega * jnp.sin(angle_h)])
    return (values[None, :], tangent[None, :])

def encode(padded, enc_weight):
    frames = padded.shape[0] - 2
    rows = padded.shape[1] - 2
    columns = padded.shape[2] - 2
    latent = jnp.zeros((frames, rows, columns, enc_weight.shape[4]), jnp.float32)
    for tap_time in range(3):
        for tap_row in range(3):
            for tap_col in range(3):
                window = padded[tap_time:tap_time + frames, tap_row:tap_row + rows, tap_col:tap_col + columns]
                latent = latent + jnp.einsum('fhwc,cz->fhwz', window.astype(jnp.float32), enc_weight[tap_time, tap_row, tap_col].astype(jnp.float32))
    return latent

def patchify(field):
    frames, rows, columns, chans = field.shape
    shaped = field.reshape(frames, rows // 2, 2, columns // 2, 2, chans)
    return shaped.transpose(1, 0, 3, 2, 4, 5).reshape(-1, 4 * chans)

def embed(patches, patch_tangent, values, tangent, embed_weight, time_weight, norm_gain):
    high = lax.Precision.HIGHEST
    embed_full = embed_weight.astype(jnp.float32)
    time_full = time_weight.astype(jnp.float32)
    hidden = jnp.dot(patches, embed_full, precision=high) + jnp.dot(values, time_full, precision=high)
    hidden_t = jnp.dot(patch_tangent, embed_full, precision=high) + jnp.dot(tangent, time_full, precision=high)
    inv_rms = lax.rsqrt(lax.optimization_barrier(jnp.mean(hidden * hidden, axis=-1, keepdims=True)) + EPSILON)
    cross = lax.optimization_barrier(jnp.mean(hidden * hidden_t, axis=-1, keepdims=True))
    normed = (hidden * inv_rms * norm_gain).astype(jnp.bfloat16)
    normed_t = (norm_gain * (hidden_t * inv_rms - hidden * inv_rms ** 3 * cross)).astype(jnp.bfloat16)
    return (normed, normed_t)

def attend(query, keys, vals, query_t, keys_t, vals_t):
    score_scale = query.shape[-1] ** (-0.5)
    qf, kf, vf = (query.astype(jnp.float32), keys.astype(jnp.float32), vals.astype(jnp.float32))
    qtf, ktf, vtf = (query_t.astype(jnp.float32), keys_t.astype(jnp.float32), vals_t.astype(jnp.float32))
    scores = jnp.einsum('hqd,hkd->hqk', qf, kf) * score_scale
    score_t = (jnp.einsum('hqd,hkd->hqk', qtf, kf) + jnp.einsum('hqd,hkd->hqk', qf, ktf)) * score_scale
    peak = lax.optimization_barrier(jnp.max(scores, axis=-1, keepdims=True))
    expo = jnp.exp(scores - peak)
    probs = expo / lax.optimization_barrier(jnp.sum(expo, axis=-1, keepdims=True))
    prob_t = probs * (score_t - lax.optimization_barrier(jnp.sum(probs * score_t, axis=-1, keepdims=True)))
    probs_b = probs.astype(jnp.bfloat16).astype(jnp.float32)
    prob_tb = prob_t.astype(jnp.bfloat16).astype(jnp.float32)
    output = jnp.einsum('hqk,hkd->hqd', probs_b, vf).astype(jnp.bfloat16)
    output_t = (jnp.einsum('hqk,hkd->hqd', prob_tb, vf) + jnp.einsum('hqk,hkd->hqd', probs_b, vtf)).astype(jnp.bfloat16)
    return (output, output_t)

def reference(clip_features, enc_weight, noise_field, flow_times, embed_weight, time_weight, norm_gain, qkv_weight):
    weight_flat = qkv_weight.reshape(D, 3 * HEADS * HD)

    def one_clip(inputs):
        feature_map, noise_one, pair = inputs
        padded = jnp.pad(feature_map, ((2, 0), (1, 1), (1, 1), (0, 0)))
        latent = encode(padded, enc_weight)
        start_t = pair[0].astype(jnp.float32) / TGRID
        flow_t = pair[1].astype(jnp.float32) / TGRID
        noisy = (1.0 - flow_t) * latent + flow_t * noise_one
        velocity = noise_one - latent
        values, tangent = time_features(flow_t, flow_t - start_t)
        normed, normed_t = embed(patchify(noisy), patchify(velocity), values, tangent, embed_weight, time_weight, norm_gain)
        projected = jnp.dot(normed, weight_flat, preferred_element_type=jnp.float32).astype(jnp.bfloat16)
        projected_t = jnp.dot(normed_t, weight_flat, preferred_element_type=jnp.float32).astype(jnp.bfloat16)
        tokens_all = normed.shape[0]
        heads_p = projected.reshape(tokens_all, 3, HEADS, HD).transpose(1, 2, 0, 3)
        heads_t = projected_t.reshape(tokens_all, 3, HEADS, HD).transpose(1, 2, 0, 3)
        output, output_t = attend(heads_p[0], heads_p[1], heads_p[2], heads_t[0], heads_t[1], heads_t[2])
        return (output.transpose(1, 0, 2).reshape(tokens_all, HEADS * HD), output_t.transpose(1, 0, 2).reshape(tokens_all, HEADS * HD))
    return lax.map(one_clip, (clip_features, noise_field, flow_times))
```

```python
import functools

import jax
import jax.numpy as jnp
import numpy as np
from jax import lax
from jax.experimental import pallas as pl
from jax.experimental.pallas import tpu as pltpu
from jax.sharding import PartitionSpec as P

HD = 128
TFEAT = 256
TGRID = 1000
EPSILON = 1e-06
LANES = 128
F32 = jnp.float32
BF16 = jnp.bfloat16


def split(value, parts):
    terms = []
    for _ in range(parts):
        term = value.astype(BF16)
        terms.append(term)
        value = value - term.astype(F32)
    return terms


def dot(a, b):
    return jnp.dot(a, b, preferred_element_type=F32)


def dot_nt(a, b):
    return lax.dot_general(a, b, (((1,), (1,)), ((), ())), preferred_element_type=F32)


def conv_part(features, weight, frames, width, chans):
    pixels = features.shape[1]
    taps = [dot_nt(weight[...], features[f]) for f in range(frames)]
    lane = lax.broadcasted_iota(jnp.int32, (chans, pixels), 1)
    column = lax.rem(lane, width)
    block = 9 * chans
    own, edge = [], []
    for f in range(frames):
        acc = taps[f][2 * block : 3 * block]
        if f >= 1:
            acc = acc + taps[f - 1][block : 2 * block]
        if f >= 2:
            acc = acc + taps[f - 2][:block]
        rows = []
        for b in range(3):
            part = [acc[(b * 3 + e) * chans : (b * 3 + e + 1) * chans] for e in range(3)]
            total = part[1]
            total = total + jnp.where(column > 0, pltpu.roll(part[0], 1, 1), 0.0)
            total = total + jnp.where(column < width - 1, pltpu.roll(part[2], pixels - 1, 1), 0.0)
            rows.append(total)
        down = pltpu.roll(rows[0], width, 1)
        up = pltpu.roll(rows[2], pixels - width, 1)
        here = rows[1] + jnp.where(lane >= width, down, 0.0)
        own.append(here + jnp.where(lane < pixels - width, up, 0.0))
        edge.append(jnp.where(lane < width, down, up))
    return jnp.concatenate(own, axis=1), jnp.concatenate(edge, axis=1)


def tokens_part(latent, noise, pick, flow_t, chans):
    tokens = pick.shape[1] // 4
    terms = split(latent, 3) + split(noise, 3)
    moved = dot(jnp.concatenate(terms, axis=0), pick)
    lat = moved[:chans] + moved[chans : 2 * chans] + moved[2 * chans : 3 * chans]
    noi = moved[3 * chans : 4 * chans] + moved[4 * chans : 5 * chans] + moved[5 * chans :]
    noisy = (1.0 - flow_t) * lat + flow_t * noi
    velocity = noi - lat
    stacked = jnp.concatenate(
        [noisy[:, k * tokens : (k + 1) * tokens] for k in range(4)]
        + [velocity[:, k * tokens : (k + 1) * tokens] for k in range(4)],
        axis=0,
    )
    flipped = stacked.T
    return flipped[:, : 4 * chans], flipped[:, 4 * chans :]


def norm_part(noisy, velocity, embed_ref, time_rows, chunk):
    tokens, patch = noisy.shape
    depth = embed_ref.shape[1]
    lhs = jnp.concatenate(
        [jnp.concatenate(split(noisy, 3), axis=1), jnp.concatenate(split(velocity, 3), axis=1)], axis=0
    )
    square = jnp.zeros((tokens, chunk), F32)
    cross = jnp.zeros((tokens, chunk), F32)
    for k in range(depth // chunk):
        piece = embed_ref[:, k * chunk : (k + 1) * chunk]
        both = dot(lhs, jnp.concatenate([piece, piece, piece], axis=0))
        hidden = both[:tokens] + time_rows[0:1, k * chunk : (k + 1) * chunk]
        hidden_t = both[tokens:] + time_rows[1:2, k * chunk : (k + 1) * chunk]
        square = square + hidden * hidden
        cross = cross + hidden * hidden_t
    mean_sq = jnp.sum(square, axis=1, keepdims=True) / depth
    mean_cr = jnp.sum(cross, axis=1, keepdims=True) / depth
    inv = lax.rsqrt(mean_sq + EPSILON)
    shift = -(inv * inv * inv) * mean_cr
    inv_hi, inv_lo = [v.astype(F32) for v in split(inv, 2)]
    sh_hi, sh_lo = [v.astype(F32) for v in split(shift, 2)]
    lane = lax.broadcasted_iota(jnp.int32, (tokens, LANES - patch), 1)

    def tail(*columns):
        out = jnp.zeros((tokens, LANES - patch), F32)
        for index, column in enumerate(columns):
            out = jnp.where(lane == index, column, out)
        return out

    rows = jnp.concatenate([noisy * inv, tail(inv_hi, inv_lo, inv_hi)], axis=1)
    rows_t = jnp.concatenate(
        [velocity * inv + noisy * shift, tail(sh_hi, sh_lo, sh_hi, inv_hi, inv_lo, inv_hi)], axis=1
    )
    return rows.astype(BF16), rows_t.astype(BF16)


MESH = pl.DeviceIdType.MESH


def front_kernel(
    dims,
    flow_ref, source_ref, w_hbm, ecut_hbm, gcut_hbm, tcut_hbm, f_hbm, enc_hbm, time_hbm, noise_hbm, embed_hbm,
    x_out, x_own, m_out,
    w_ref, ecut_ref, gcut_ref, tcut_ref, f_ref, enc_ref, time_ref, noise_ref, embed_ref, load_sem, feats_ref,
    feats_buf, feats_send, feats_recv,
    edge_buf, before_buf, after_buf, edge_send, edge_recv,
    e_send, e_recv, tau_send, tau_recv, e_ss, e_rs, t_ss, t_rs,
    x_buf, x_ss, x_rs,
    g_buf, tau_buf, b_ss, b_rs, bt_ss, bt_rs, a_ss, a_rs, c_ss, c_rs,
):
    frames, width, chans, peers, clips = dims
    seq, clip = lax.axis_index("seq"), lax.axis_index("clip")
    patch, depth = embed_ref.shape
    share = ecut_ref.shape[1]
    part = w_ref.shape[2]
    chunk = patch // clips
    on_seq = [{"seq": lax.rem(seq + k, peers)} for k in range(1, peers)]
    on_clip = [{"clip": lax.rem(clip + k, clips)} for k in range(1, clips)]
    mate = {"clip": clip + 1 - 2 * lax.rem(clip, 2)}

    def cut(ref):
        if ref.shape[-1] == share:
            return ref
        return ref.at[:, pl.ds(pl.multiple_of(clip * share, share), share)]

    pairs = (
        (w_hbm, w_ref), (cut(ecut_hbm), ecut_ref), (cut(gcut_hbm), gcut_ref), (cut(tcut_hbm), tcut_ref),
        (f_hbm, f_ref), (enc_hbm, enc_ref), (time_hbm, time_ref), (noise_hbm, noise_ref), (embed_hbm, embed_ref),
    )
    loads = [pltpu.make_async_copy(src, dst, load_sem.at[k]) for k, (src, dst) in enumerate(pairs)]
    for load in loads:
        load.start()
    flow_r = flow_ref[0, 0].astype(F32) / TGRID
    flow_t = flow_ref[0, 1].astype(F32) / TGRID
    quarter = TFEAT // 4
    order = lax.broadcasted_iota(jnp.int32, (8, TFEAT), 1)
    line = lax.broadcasted_iota(jnp.int32, (8, TFEAT), 0)
    omega = 8.0 * jnp.exp(-np.float32(np.log(100.0)) * lax.rem(order, quarter).astype(F32) / quarter)
    angle = omega * jnp.where(order < 2 * quarter, flow_t, flow_t - flow_r)
    sine, cosine = jnp.sin(angle), jnp.cos(angle)
    first = lax.rem(order // quarter, 2) == 0
    feats_ref[...] = jnp.where(
        line == 0,
        jnp.where(first, sine, cosine),
        jnp.where(line == 1, jnp.where(first, omega * cosine, -omega * sine), 0.0),
    )

    barrier = pltpu.get_barrier_semaphore()
    for who in on_seq + on_clip:
        pl.semaphore_signal(barrier, inc=1, device_id=who, device_id_type=MESH)
    pl.semaphore_wait(barrier, len(on_seq) + len(on_clip))
    sent = []

    def push(src, dst, ssem, rsem, who):
        copy = pltpu.make_async_remote_copy(
            src_ref=src, dst_ref=dst, send_sem=ssem, recv_sem=rsem, device_id=who, device_id_type=MESH
        )
        copy.start()
        sent.append(copy)
        return copy

    feats_in = [
        push(feats_ref, feats_buf.at[clip], feats_send.at[k], feats_recv.at[k], who) for k, who in enumerate(on_clip)
    ]
    feats_buf[clip] = feats_ref[...]

    loads[1].wait()
    loads[2].wait()
    gain = gcut_ref[...]
    left = jnp.concatenate(split(ecut_ref[...].astype(F32) * gain, 2), axis=0)
    loads[0].wait()
    for i in range(3):
        both = dot(left, w_ref[i])
        both = both[:patch] + both[patch:]
        for c in range(clips):
            e_send[c, :, i * part : (i + 1) * part] = both[c * chunk : (c + 1) * chunk].astype(BF16)
    e_in = [
        push(e_send.at[lax.rem(clip + k + 1, clips)], e_recv.at[k], e_ss.at[k], e_rs.at[k], who)
        for k, who in enumerate(on_clip)
    ]
    for copy in feats_in:
        copy.wait_recv()
    loads[3].wait()
    feats = feats_buf[...].reshape(clips * 8, feats_buf.shape[2])
    both = dot(jnp.concatenate(split(feats, 2), axis=0), tcut_ref[...])
    left = jnp.concatenate(split((both[: clips * 8] + both[clips * 8 :]) * gain, 2), axis=0)
    for i in range(3):
        both = dot(left, w_ref[i])
        both = both[: clips * 8] + both[clips * 8 :]
        for c in range(clips):
            tau_send[c, :, i * part : (i + 1) * part] = both[c * 8 : c * 8 + 2]
    tau_in = [
        push(tau_send.at[lax.rem(clip + k + 1, clips)], tau_recv.at[k], t_ss.at[k], t_rs.at[k], who)
        for k, who in enumerate(on_clip)
    ]

    loads[4].wait()
    loads[5].wait()
    own, edge = conv_part(f_ref, enc_ref, frames, width, chans)
    edge_buf[...] = edge

    def edge_copy(dst, k, step):
        return pltpu.make_async_remote_copy(
            src_ref=edge_buf, dst_ref=dst, send_sem=edge_send.at[k], recv_sem=edge_recv.at[k],
            device_id={"seq": lax.rem(seq + peers + step, peers)}, device_id_type=MESH,
        )

    to_next, to_last = edge_copy(before_buf, 0, 1), edge_copy(after_buf, 1, -1)

    @pl.when(seq < peers - 1)
    def _():
        to_next.start()

    @pl.when(seq > 0)
    def _():
        to_last.start()

    @pl.when(seq == 0)
    def _():
        before_buf[...] = jnp.zeros_like(before_buf)

    @pl.when(seq == peers - 1)
    def _():
        after_buf[...] = jnp.zeros_like(after_buf)

    loads[6].wait()
    mine = jnp.concatenate(split(feats_ref[...], 2), axis=0)
    times = dot(mine, time_ref[...])
    times = times[:8] + times[8:]

    for copy in e_in:
        copy.wait_recv()
    total = e_send[clip].astype(F32)
    for k in range(clips - 1):
        total = total + e_recv[k].astype(F32)
    g_buf[clip, seq] = total.astype(BF16)
    b_in = [
        push(g_buf.at[clip, seq], g_buf.at[clip, seq], b_ss.at[k], b_rs.at[k], who) for k, who in enumerate(on_seq)
    ]
    for copy in tau_in:
        copy.wait_recv()
    total = tau_send[clip]
    for k in range(clips - 1):
        total = total + tau_recv[k]
    tau_buf[seq] = total
    bt_in = [
        push(tau_buf.at[seq], tau_buf.at[seq], bt_ss.at[k], bt_rs.at[k], who) for k, who in enumerate(on_seq)
    ]
    @pl.when(seq > 0)
    def _():
        to_next.wait_recv()

    @pl.when(seq < peers - 1)
    def _():
        to_last.wait_recv()

    pixels = f_ref.shape[1]
    lane = lax.rem(lax.broadcasted_iota(jnp.int32, own.shape, 1), pixels)
    latent = own + jnp.where(lane < width, before_buf[...], 0.0)
    latent = latent + jnp.where(lane >= pixels - width, after_buf[...], 0.0)
    loads[7].wait()
    loads[8].wait()
    noise = jnp.concatenate(
        [noise_ref[f, r] for f in range(frames) for r in range(noise_ref.shape[1])], axis=1
    )
    places = lax.broadcasted_iota(jnp.int32, (own.shape[1], source_ref.shape[1]), 0)
    pick = (places == source_ref[...]).astype(F32).astype(BF16)
    noisy, velocity = tokens_part(latent, noise, pick, flow_t, chans)
    rows, rows_t = norm_part(noisy, velocity, embed_ref, times, 512)
    x_buf[seq, 0] = rows
    x_buf[seq, 1] = rows_t
    x_in = [push(x_buf.at[seq], x_buf.at[seq], x_ss.at[k], x_rs.at[k], who) for k, who in enumerate(on_seq)]

    for copy in b_in:
        copy.wait_recv()
    c_in = [push(g_buf.at[clip], g_buf.at[clip], c_ss.at[0], c_rs.at[0], mate)]
    a_in = [
        push(g_buf.at[clip], g_buf.at[clip], a_ss.at[k], a_rs.at[k], on_clip[2 * k + 1])
        for k in range(clips // 2 - 1)
    ]
    for k, copy in enumerate(a_in):
        copy.wait_recv()
        src = lax.rem(clip + clips - 2 * (k + 1), clips)
        c_in.append(push(g_buf.at[src], g_buf.at[src], c_ss.at[k + 1], c_rs.at[k + 1], mate))
    for copy in bt_in + x_in + c_in:
        copy.wait_recv()
    tokens = x_buf.shape[2]
    x_own[:tokens] = x_buf[seq, 0]
    x_own[tokens:] = x_buf[seq, 1]
    for p in range(peers):
        x_out[p * tokens : (p + 1) * tokens, :LANES] = x_buf[p, 0]
        x_out[p * tokens : (p + 1) * tokens, LANES:] = x_buf[p, 1]
        for c in range(clips):
            m_out[p, c * chunk : (c + 1) * chunk] = g_buf[c, p]
        hi = tau_buf[p].astype(BF16).astype(F32)
        lo = tau_buf[p] - hi
        extra = [hi[0:1], hi[0:1], lo[0:1], hi[1:2], hi[1:2], lo[1:2]]
        row = lax.broadcasted_iota(jnp.int32, (LANES - patch, 3 * part), 0)
        tail = jnp.zeros((LANES - patch, 3 * part), F32)
        for index, value in enumerate(extra):
            tail = jnp.where(row == index, value, tail)
        m_out[p, patch:] = tail.astype(BF16)
    for copy in sent:
        copy.wait_send()

    @pl.when(seq < peers - 1)
    def _():
        to_next.wait_send()

    @pl.when(seq > 0)
    def _():
        to_last.wait_send()


def attend_kernel(x_ref, own_ref, m_ref, out_ref, out_t_ref):
    peers, part = m_ref.shape[0], m_ref.shape[2] // 3
    per = peers * part // HD
    tokens = own_ref.shape[0] // 2
    fold = HD ** (-0.5) * np.log2(np.e).astype(np.float32)
    ln2 = np.log(2.0).astype(np.float32)
    zero = jnp.zeros((tokens, LANES), BF16)
    cuts = [slice(h * HD, (h + 1) * HD) for h in range(per)]
    each = part // HD

    def piece(h, g):
        return m_ref[h // each, :, g * part + h % each * HD : g * part + (h % each + 1) * HD]

    inner = [(dot_nt(piece(h, 0), piece(h, 1)) * fold).astype(BF16) for h in range(per)]
    u = dot(own_ref[...], jnp.concatenate(inner, axis=1)).astype(BF16)
    def scores_of(at):
        left = jnp.concatenate(
            [jnp.concatenate([u[:tokens, at], zero], axis=1), jnp.concatenate([u[tokens:, at], u[:tokens, at]], axis=1)],
            axis=0,
        )
        return dot_nt(left, x_ref[...])

    ys = []
    for h, at in enumerate(cuts):
        ahead = scores_of(at)
        scores, score_t = ahead[:tokens], ahead[tokens:]
        expo = jnp.exp2(scores - jnp.max(scores, axis=1, keepdims=True))
        inv = 1.0 / jnp.sum(expo, axis=1, keepdims=True)
        mean = jnp.sum(expo * score_t, axis=1, keepdims=True) * inv
        left = jnp.concatenate([expo.astype(BF16), (expo * (score_t - mean)).astype(BF16)], axis=0)
        both = dot(left, x_ref[...])
        y = both[:tokens, :LANES] * inv
        yt = both[tokens:, :LANES] * (inv * ln2) + both[:tokens, LANES:] * inv
        ys.append(jnp.concatenate(split(jnp.concatenate([y, yt], axis=0), 2), axis=1))
    for h, at in enumerate(cuts):
        v = piece(h, 2)
        o = dot(ys[h], jnp.concatenate([v, v], axis=0))
        out_ref[:, at] = o[:tokens].astype(BF16)
        out_t_ref[:, at] = o[tokens:].astype(BF16)


VMEM = pl.BlockSpec(memory_space=pltpu.VMEM)


def attend(rows, own, weights, inner):
    tokens = own.shape[0] // 2
    shape = jax.ShapeDtypeStruct((tokens, inner), BF16)
    return pl.pallas_call(
        attend_kernel,
        out_shape=(shape, shape),
        in_specs=[VMEM] * 3,
        out_specs=(VMEM, VMEM),
        name="attend",
    )(rows, own, weights)


def local(clip_features, enc_weight, noise_field, flow_times, embed_weight, time_weight, norm_gain, qkv_weight):
    _, frames, rows, width, depth_c = clip_features.shape
    chans = enc_weight.shape[4]
    patch, depth = embed_weight.shape
    peers, clips = lax.axis_size("seq"), lax.axis_size("clip")
    share = qkv_weight.shape[0]
    part = qkv_weight.shape[2]
    pixels = rows * width
    tokens = frames * pixels // 4

    gain, embed_cut, time_cut = norm_gain[None, :], embed_weight, time_weight
    if share % LANES:
        me = lax.axis_index("clip")
        gain, embed_cut, time_cut = (
            lax.dynamic_slice_in_dim(m, me * share, share, 1) for m in (gain, embed_weight, time_weight)
        )
    weight = qkv_weight.transpose(1, 0, 2)
    features = clip_features.reshape(frames, pixels, depth_c)
    enc = enc_weight.transpose(0, 1, 2, 4, 3).reshape(27 * chans, depth_c)
    noise = noise_field[0].transpose(0, 1, 3, 2)
    i, f, j = np.meshgrid(np.arange(rows // 2), np.arange(frames), np.arange(width // 2), indexing="ij")
    source = np.stack(
        [((f * rows + 2 * i + p) * width + 2 * j + q).reshape(-1) for p in range(2) for q in range(2)]
    ).reshape(1, -1)
    source = jnp.asarray(source.astype(np.int32))
    chunk = patch // clips
    dma = pltpu.SemaphoreType.DMA
    anywhere = pl.BlockSpec(memory_space=pl.ANY)
    edge = pltpu.VMEM((chans, frames * pixels), F32)
    x, x_own, weights = pl.pallas_call(
        functools.partial(front_kernel, (frames, width, chans, peers, clips)),
        out_shape=(
            jax.ShapeDtypeStruct((peers * tokens, 2 * LANES), BF16),
            jax.ShapeDtypeStruct((2 * tokens, LANES), BF16),
            jax.ShapeDtypeStruct((peers, LANES, 3 * part), BF16),
        ),
        in_specs=[pl.BlockSpec(memory_space=pltpu.SMEM), VMEM] + [anywhere] * 9,
        out_specs=(VMEM,) * 3,
        scratch_shapes=[
            pltpu.VMEM(weight.shape, BF16), pltpu.VMEM((patch, share), BF16), pltpu.VMEM((1, share), F32),
            pltpu.VMEM((TFEAT, share), BF16), pltpu.VMEM(features.shape, BF16), pltpu.VMEM(enc.shape, BF16),
            pltpu.VMEM(time_weight.shape, BF16), pltpu.VMEM(noise.shape, F32), pltpu.VMEM(embed_weight.shape, BF16),
            dma((9,)), pltpu.VMEM((8, TFEAT), F32),
            pltpu.VMEM((clips, 8, TFEAT), F32), dma((clips - 1,)), dma((clips - 1,)),
            edge, edge, edge, dma((2,)), dma((2,)),
            pltpu.VMEM((clips, chunk, 3 * part), BF16), pltpu.VMEM((clips - 1, chunk, 3 * part), BF16),
            pltpu.VMEM((clips, 2, 3 * part), F32), pltpu.VMEM((clips - 1, 2, 3 * part), F32),
            dma((clips - 1,)), dma((clips - 1,)), dma((clips - 1,)), dma((clips - 1,)),
            pltpu.VMEM((peers, 2, tokens, LANES), BF16), dma((peers - 1,)), dma((peers - 1,)),
            pltpu.VMEM((clips, peers, chunk, 3 * part), BF16), pltpu.VMEM((peers, 2, 3 * part), F32),
            dma((peers - 1,)), dma((peers - 1,)), dma((peers - 1,)), dma((peers - 1,)),
            dma((clips // 2,)), dma((clips // 2,)), dma((clips // 2,)), dma((clips // 2,)),
        ],
        compiler_params=pltpu.CompilerParams(collective_id=0, has_side_effects=True),
        name="front",
    )(flow_times, source, weight, embed_cut, gain, time_cut, features, enc, time_weight, noise, embed_weight)
    output, output_t = attend(x, x_own, weights, peers * part)
    return output[None], output_t[None]


def solution(mesh):
    placed = (
        P("clip", None, "seq", None, None),
        P(),
        P("clip", None, "seq", None, None),
        P("clip", None),
        P(),
        P(),
        P(),
        P("clip", None, "seq"),
    )
    return jax.shard_map(
        local,
        mesh=mesh,
        in_specs=placed,
        out_specs=(P("clip", "seq", None), P("clip", "seq", None)),
        check_vma=False,
    )
```

```python
import functools

import jax
import jax.numpy as jnp
import numpy as np
from jax import lax
from jax.experimental import pallas as pl
from jax.experimental.pallas import tpu as pltpu
from jax.sharding import PartitionSpec as P

HD = 128
TFEAT = 256
TGRID = 1000
EPSILON = 1e-06
LANES = 128
TAIL = 16
F32 = jnp.float32
BF16 = jnp.bfloat16


def split(value, parts):
    terms = []
    for _ in range(parts):
        term = value.astype(BF16)
        terms.append(term)
        value = value - term.astype(F32)
    return terms


def dot(a, b):
    return jnp.dot(a, b, preferred_element_type=F32)


def dot_nt(a, b):
    return lax.dot_general(a, b, (((1,), (1,)), ((), ())), preferred_element_type=F32)


def conv_part(features, weight, frames, width, chans):
    pixels = features.shape[1]
    taps = [dot_nt(weight[...], features[f]) for f in range(frames)]
    lane = lax.broadcasted_iota(jnp.int32, (chans, pixels), 1)
    column = lax.rem(lane, width)
    block = 9 * chans
    own, edge = [], []
    for f in range(frames):
        acc = taps[f][2 * block : 3 * block]
        if f >= 1:
            acc = acc + taps[f - 1][block : 2 * block]
        if f >= 2:
            acc = acc + taps[f - 2][:block]
        rows = []
        for b in range(3):
            part = [acc[(b * 3 + e) * chans : (b * 3 + e + 1) * chans] for e in range(3)]
            total = part[1]
            total = total + jnp.where(column > 0, pltpu.roll(part[0], 1, 1), 0.0)
            total = total + jnp.where(column < width - 1, pltpu.roll(part[2], pixels - 1, 1), 0.0)
            rows.append(total)
        down = pltpu.roll(rows[0], width, 1)
        up = pltpu.roll(rows[2], pixels - width, 1)
        here = rows[1] + jnp.where(lane >= width, down, 0.0)
        own.append(here + jnp.where(lane < pixels - width, up, 0.0))
        edge.append(jnp.where(lane < width, down, up))
    return jnp.concatenate(own, axis=1), jnp.concatenate(edge, axis=1)


def tokens_part(latent, noise, pick, flow_t, chans):
    tokens = pick.shape[1] // 4
    terms = split(latent, 3) + split(noise, 3)
    moved = dot(jnp.concatenate(terms, axis=0), pick)
    lat = moved[:chans] + moved[chans : 2 * chans] + moved[2 * chans : 3 * chans]
    noi = moved[3 * chans : 4 * chans] + moved[4 * chans : 5 * chans] + moved[5 * chans :]
    noisy = (1.0 - flow_t) * lat + flow_t * noi
    velocity = noi - lat
    stacked = jnp.concatenate(
        [noisy[:, k * tokens : (k + 1) * tokens] for k in range(4)]
        + [velocity[:, k * tokens : (k + 1) * tokens] for k in range(4)],
        axis=0,
    )
    flipped = stacked.T
    return flipped.astype(BF16)


def norm_part(raw, gram_pair, depth, patch):
    tokens = raw.shape[0]
    lane = lax.broadcasted_iota(jnp.int32, (tokens, LANES), 1)
    both = raw.astype(F32)
    noisy = jnp.where(lane < patch, both, 0.0)
    velocity = jnp.where(lane < patch, pltpu.roll(both, LANES - patch, 1), 0.0)
    ones = jnp.where((lane == patch) | (lane == patch + 1), 1.0, noisy)
    ones_t = jnp.where((lane == patch + 2) | (lane == patch + 3), 1.0, velocity)
    left = ones.astype(BF16)
    moved = dot(jnp.concatenate([left, left], axis=1), gram_pair)
    mean_sq = jnp.sum(moved * ones, axis=1, keepdims=True) / depth
    mean_cr = jnp.sum(moved * ones_t, axis=1, keepdims=True) / depth
    inv = lax.rsqrt(mean_sq + EPSILON)
    shift = -(inv * inv * inv) * mean_cr
    inv_hi, inv_lo = [v.astype(F32) for v in split(inv, 2)]
    sh_hi, sh_lo = [v.astype(F32) for v in split(shift, 2)]
    rows, rows_t = noisy * inv, velocity * inv + noisy * shift
    for index, column in enumerate([inv_hi, inv_lo, inv_hi]):
        rows = jnp.where(lane == patch + index, column, rows)
    for index, column in enumerate([sh_hi, sh_lo, sh_hi, inv_hi, inv_lo, inv_hi]):
        rows_t = jnp.where(lane == patch + index, column, rows_t)
    return rows.astype(BF16), rows_t.astype(BF16)


MESH = pl.DeviceIdType.MESH


def front_kernel(
    dims,
    flow_ref, source_ref, f_hbm, enc_hbm, ecut_hbm, gcut_hbm, w_hbm, tcut_hbm, noise_hbm, embed_hbm, time_hbm,
    x_out, x_own, m_out,
    f_ref, enc_ref, ecut_ref, gcut_ref, w_ref, tcut_ref, noise_ref, embed_ref, time_ref, load_sem, feats_ref,
    feats_buf, feats_send, feats_recv,
    edge_buf, before_buf, after_buf, edge_send, edge_recv,
    e_send, e_recv, tau_send, tau_recv, e_ss, e_rs, t_ss, t_rs,
    x_buf, x_ss, x_rs,
    g_buf, tau_buf, b_ss, b_rs, bt_ss, bt_rs, a_ss, a_rs, c_ss, c_rs,
):
    frames, width, chans, patch, peers, clips = dims
    seq, clip = lax.axis_index("seq"), lax.axis_index("clip")
    depth = embed_ref.shape[1]
    share = ecut_ref.shape[1]
    part = w_ref.shape[2]
    chunk = patch // clips
    on_seq = [{"seq": lax.rem(seq + k, peers)} for k in range(1, peers)]
    on_clip = [{"clip": lax.rem(clip + k, clips)} for k in range(1, clips)]
    mate = {"clip": clip + 1 - 2 * lax.rem(clip, 2)}

    barrier = pltpu.get_barrier_semaphore()
    for who in on_seq + on_clip:
        pl.semaphore_signal(barrier, inc=1, device_id=who, device_id_type=MESH)

    def cut(ref):
        if ref.shape[-1] == share:
            return ref
        return ref.at[:, pl.ds(pl.multiple_of(clip * share, share), share)]

    pairs = [(f_hbm, f_ref), (enc_hbm, enc_ref), (cut(ecut_hbm), ecut_ref), (cut(gcut_hbm), gcut_ref)]
    pairs += [(w_hbm.at[i], w_ref.at[i]) for i in range(3)]
    pairs += [
        (cut(tcut_hbm), tcut_ref), (noise_hbm, noise_ref), (embed_hbm, embed_ref.at[:patch]), (time_hbm, time_ref),
    ]
    loads = [pltpu.make_async_copy(src, dst, load_sem.at[k]) for k, (src, dst) in enumerate(pairs)]
    for load in loads:
        load.start()
    f_load, enc_load, ecut_load, gcut_load, w0, w1, w2, tcut_load, noise_load, embed_load, time_load = loads
    flow_r = flow_ref[0, 0].astype(F32) / TGRID
    flow_t = flow_ref[0, 1].astype(F32) / TGRID
    quarter = TFEAT // 4
    order = lax.broadcasted_iota(jnp.int32, (8, TFEAT), 1)
    line = lax.broadcasted_iota(jnp.int32, (8, TFEAT), 0)
    omega = 8.0 * jnp.exp(-np.float32(np.log(100.0)) * lax.rem(order, quarter).astype(F32) / quarter)
    angle = omega * jnp.where(order < 2 * quarter, flow_t, flow_t - flow_r)
    sine, cosine = jnp.sin(angle), jnp.cos(angle)
    first = lax.rem(order // quarter, 2) == 0
    feats_ref[...] = jnp.where(
        line == 0,
        jnp.where(first, sine, cosine),
        jnp.where(line == 1, jnp.where(first, omega * cosine, -omega * sine), 0.0),
    )
    sent = []

    def push(src, dst, ssem, rsem, who):
        copy = pltpu.make_async_remote_copy(
            src_ref=src, dst_ref=dst, send_sem=ssem, recv_sem=rsem, device_id=who, device_id_type=MESH
        )
        copy.start()
        sent.append(copy)
        return copy

    f_load.wait()
    enc_load.wait()
    own, edge = conv_part(f_ref, enc_ref, frames, width, chans)
    edge_buf[...] = edge

    @pl.when(seq == 0)
    def _():
        before_buf[...] = jnp.zeros_like(before_buf)

    @pl.when(seq == peers - 1)
    def _():
        after_buf[...] = jnp.zeros_like(after_buf)

    pl.semaphore_wait(barrier, len(on_seq) + len(on_clip))
    feats_in = [
        push(feats_ref, feats_buf.at[clip], feats_send.at[k], feats_recv.at[k], who) for k, who in enumerate(on_clip)
    ]
    feats_buf[clip] = feats_ref[...]

    def edge_copy(dst, k, step):
        return pltpu.make_async_remote_copy(
            src_ref=edge_buf, dst_ref=dst, send_sem=edge_send.at[k], recv_sem=edge_recv.at[k],
            device_id={"seq": lax.rem(seq + peers + step, peers)}, device_id_type=MESH,
        )

    to_next, to_last = edge_copy(before_buf, 0, 1), edge_copy(after_buf, 1, -1)

    @pl.when(seq < peers - 1)
    def _():
        to_next.start()

    @pl.when(seq > 0)
    def _():
        to_last.start()

    ecut_load.wait()
    gcut_load.wait()
    gain = gcut_ref[...]
    left = jnp.concatenate(split(ecut_ref[...].astype(F32) * gain, 2), axis=0)
    e_in = []
    for i, load in enumerate((w0, w1, w2)):
        load.wait()
        both = dot(left, w_ref[i])
        both = both[:patch] + both[patch:]
        for c in range(clips):
            e_send[i, c] = both[c * chunk : (c + 1) * chunk].astype(BF16)
        e_in.append([
            push(e_send.at[i, lax.rem(clip + k + 1, clips)], e_recv.at[i, k], e_ss.at[i, k], e_rs.at[i, k], who)
            for k, who in enumerate(on_clip)
        ])
    for copy in feats_in:
        copy.wait_recv()
    tcut_load.wait()
    feats = feats_buf[...].reshape(clips * 8, feats_buf.shape[2])
    both = dot(jnp.concatenate(split(feats, 2), axis=0), tcut_ref[...])
    left = jnp.concatenate(split((both[: clips * 8] + both[clips * 8 :]) * gain, 2), axis=0)
    for i in range(3):
        both = dot(left, w_ref[i])
        both = both[: clips * 8] + both[clips * 8 :]
        for c in range(clips):
            tau_send[c, :, i * part : (i + 1) * part] = both[c * 8 : c * 8 + 2]
    tau_in = [
        push(tau_send.at[lax.rem(clip + k + 1, clips)], tau_recv.at[k], t_ss.at[k], t_rs.at[k], who)
        for k, who in enumerate(on_clip)
    ]

    @pl.when(seq > 0)
    def _():
        to_next.wait_recv()

    @pl.when(seq < peers - 1)
    def _():
        to_last.wait_recv()

    pixels = f_ref.shape[1]
    lane = lax.rem(lax.broadcasted_iota(jnp.int32, own.shape, 1), pixels)
    latent = own + jnp.where(lane < width, before_buf[...], 0.0)
    latent = latent + jnp.where(lane >= pixels - width, after_buf[...], 0.0)
    noise_load.wait()
    noise = jnp.concatenate(
        [noise_ref[f, r] for f in range(frames) for r in range(noise_ref.shape[1])], axis=1
    )
    places = lax.broadcasted_iota(jnp.int32, (own.shape[1], source_ref.shape[1]), 0)
    pick = (places == source_ref[...]).astype(F32).astype(BF16)
    x_buf[seq] = tokens_part(latent, noise, pick, flow_t, chans)
    x_in = [push(x_buf.at[seq], x_buf.at[seq], x_ss.at[k], x_rs.at[k], who) for k, who in enumerate(on_seq)]

    for i in range(3):
        for copy in e_in[i]:
            copy.wait_recv()
        total = e_send[i, clip].astype(F32)
        for k in range(clips - 1):
            total = total + e_recv[i, k].astype(F32)
        g_buf[clip, seq, :, i * part : (i + 1) * part] = total.astype(BF16)

    b_in = [
        push(g_buf.at[clip, seq], g_buf.at[clip, seq], b_ss.at[k], b_rs.at[k], who) for k, who in enumerate(on_seq)
    ]

    def spread(k):
        block = g_buf.at[clip, lax.rem(seq + peers - k, peers)]
        a_in.append([
            push(block, block, a_ss.at[k, j], a_rs.at[k, j], on_clip[2 * j + 1]) for j in range(clips // 2 - 1)
        ])
        c_in.append(push(block, block, c_ss.at[k, 0], c_rs.at[k, 0], mate))

    a_in, c_in = [], []
    spread(0)
    for copy in tau_in:
        copy.wait_recv()
    total = tau_send[clip]
    for k in range(clips - 1):
        total = total + tau_recv[k]
    tau_buf[seq] = total
    bt_in = [
        push(tau_buf.at[seq], tau_buf.at[seq], bt_ss.at[k], bt_rs.at[k], who) for k, who in enumerate(on_seq)
    ]
    time_load.wait()
    mine = jnp.concatenate(split(feats_ref[...], 2), axis=0)
    times = dot(mine, time_ref[...])
    times = times[:8] + times[8:]
    time_hi, time_lo = split(times, 2)
    filler = jnp.zeros((LANES - patch - 4, depth), BF16)
    rest = jnp.concatenate([time_hi[:1], time_lo[:1], time_hi[1:2], time_lo[1:2], filler], axis=0)
    embed_ref[patch:] = rest
    embed_load.wait()
    table = embed_ref[...]
    gram_pair = jnp.concatenate(split(dot_nt(table, table), 2), axis=0)

    for k, copy in enumerate(b_in):
        copy.wait_recv()
        spread(k + 1)
    for copy in x_in:
        copy.wait_recv()
    tokens = x_buf.shape[1]
    for p in range(peers):
        rows, rows_t = norm_part(x_buf[p], gram_pair, depth, patch)
        x_out[p * tokens : (p + 1) * tokens, :LANES] = rows
        x_out[p * tokens : (p + 1) * tokens, LANES:] = rows_t
    x_own[:tokens] = x_out[pl.ds(pl.multiple_of(seq * tokens, tokens), tokens), :LANES]
    x_own[tokens:] = x_out[pl.ds(pl.multiple_of(seq * tokens, tokens), tokens), LANES:]
    for copy in bt_in:
        copy.wait_recv()
    far = []
    for k in range(peers + 1):
        if k < peers:
            p = lax.rem(seq + peers - k, peers)
            relays = []
            for j, copy in enumerate(a_in[k]):
                copy.wait_recv()
                block = g_buf.at[lax.rem(clip + clips - 2 * (j + 1), clips), p]
                relays.append(push(block, block, c_ss.at[k, j + 1], c_rs.at[k, j + 1], mate))
            far.append(relays)
        if k == 0:
            continue
        p = lax.rem(seq + peers - k + 1, peers)
        for copy in [c_in[k - 1]] + far[k - 1]:
            copy.wait_recv()
        for c in range(clips):
            m_out[p, c * chunk : (c + 1) * chunk] = g_buf[c, p]
        tau = tau_buf[p]
        hi = tau.astype(BF16).astype(F32)
        lo = tau - hi
        extra = [hi[0:1], hi[0:1], lo[0:1], hi[1:2], hi[1:2], lo[1:2]]
        row = lax.broadcasted_iota(jnp.int32, (TAIL, 3 * part), 0)
        tail = jnp.zeros((TAIL, 3 * part), F32)
        for index, value in enumerate(extra):
            tail = jnp.where(row == index, value, tail)
        m_out[p, patch:] = tail.astype(BF16)
    for copy in sent:
        copy.wait_send()

    @pl.when(seq < peers - 1)
    def _():
        to_next.wait_send()

    @pl.when(seq > 0)
    def _():
        to_last.wait_send()


def attend_kernel(x_ref, own_ref, m_ref, out_ref, out_t_ref):
    peers, part = m_ref.shape[0], m_ref.shape[2] // 3
    per = peers * part // HD
    tokens = own_ref.shape[0] // 2
    fold = HD ** (-0.5) * np.log2(np.e).astype(np.float32)
    ln2 = np.log(2.0).astype(np.float32)
    zero = jnp.zeros((tokens, LANES), BF16)
    cuts = [slice(h * HD, (h + 1) * HD) for h in range(per)]
    each = part // HD

    def piece(h, g):
        rows = m_ref[h // each, :, g * part + h % each * HD : g * part + (h % each + 1) * HD]
        return jnp.concatenate([rows, jnp.zeros((LANES - rows.shape[0], HD), BF16)], axis=0)

    inner = [(dot_nt(piece(h, 0), piece(h, 1)) * fold).astype(BF16) for h in range(per)]
    u = dot(own_ref[...], jnp.concatenate(inner, axis=1)).astype(BF16)
    def scores_of(at):
        left = jnp.concatenate(
            [jnp.concatenate([u[:tokens, at], zero], axis=1), jnp.concatenate([u[tokens:, at], u[:tokens, at]], axis=1)],
            axis=0,
        )
        return dot_nt(left, x_ref[...])

    ys = []
    for h, at in enumerate(cuts):
        ahead = scores_of(at)
        scores, score_t = ahead[:tokens], ahead[tokens:]
        expo = jnp.exp2(scores - jnp.max(scores, axis=1, keepdims=True))
        inv = 1.0 / jnp.sum(expo, axis=1, keepdims=True)
        mean = jnp.sum(expo * score_t, axis=1, keepdims=True) * inv
        left = jnp.concatenate([expo.astype(BF16), (expo * (score_t - mean)).astype(BF16)], axis=0)
        both = dot(left, x_ref[...])
        y = both[:tokens, :LANES] * inv
        yt = both[tokens:, :LANES] * (inv * ln2) + both[:tokens, LANES:] * inv
        ys.append(jnp.concatenate(split(jnp.concatenate([y, yt], axis=0), 2), axis=1))
    for h, at in enumerate(cuts):
        v = piece(h, 2)
        o = dot(ys[h], jnp.concatenate([v, v], axis=0))
        out_ref[:, at] = o[:tokens].astype(BF16)
        out_t_ref[:, at] = o[tokens:].astype(BF16)


VMEM = pl.BlockSpec(memory_space=pltpu.VMEM)


def attend(rows, own, weights, inner):
    tokens = own.shape[0] // 2
    shape = jax.ShapeDtypeStruct((tokens, inner), BF16)
    return pl.pallas_call(
        attend_kernel,
        out_shape=(shape, shape),
        in_specs=[VMEM] * 3,
        out_specs=(VMEM, VMEM),
        name="attend",
    )(rows, own, weights)


def local(clip_features, enc_weight, noise_field, flow_times, embed_weight, time_weight, norm_gain, qkv_weight):
    _, frames, rows, width, depth_c = clip_features.shape
    chans = enc_weight.shape[4]
    patch, depth = embed_weight.shape
    peers, clips = lax.axis_size("seq"), lax.axis_size("clip")
    share = qkv_weight.shape[0]
    part = qkv_weight.shape[2]
    pixels = rows * width
    tokens = frames * pixels // 4

    gain, embed_cut, time_cut = norm_gain[None, :], embed_weight, time_weight
    if share % LANES:
        me = lax.axis_index("clip")
        gain, embed_cut, time_cut = (
            lax.dynamic_slice_in_dim(m, me * share, share, 1) for m in (gain, embed_weight, time_weight)
        )
    weight = qkv_weight.transpose(1, 0, 2)
    features = clip_features.reshape(frames, pixels, depth_c)
    enc = enc_weight.transpose(0, 1, 2, 4, 3).reshape(27 * chans, depth_c)
    noise = noise_field[0].transpose(0, 1, 3, 2)
    i, f, j = np.meshgrid(np.arange(rows // 2), np.arange(frames), np.arange(width // 2), indexing="ij")
    source = np.stack(
        [((f * rows + 2 * i + p) * width + 2 * j + q).reshape(-1) for p in range(2) for q in range(2)]
    ).reshape(1, -1)
    source = jnp.asarray(source.astype(np.int32))
    chunk = patch // clips
    dma = pltpu.SemaphoreType.DMA
    anywhere = pl.BlockSpec(memory_space=pl.ANY)
    edge = pltpu.VMEM((chans, frames * pixels), F32)
    x, x_own, weights = pl.pallas_call(
        functools.partial(front_kernel, (frames, width, chans, patch, peers, clips)),
        out_shape=(
            jax.ShapeDtypeStruct((peers * tokens, 2 * LANES), BF16),
            jax.ShapeDtypeStruct((2 * tokens, LANES), BF16),
            jax.ShapeDtypeStruct((peers, patch + TAIL, 3 * part), BF16),
        ),
        in_specs=[pl.BlockSpec(memory_space=pltpu.SMEM), VMEM] + [anywhere] * 9,
        out_specs=(VMEM,) * 3,
        scratch_shapes=[
            pltpu.VMEM(features.shape, BF16), pltpu.VMEM(enc.shape, BF16), pltpu.VMEM((patch, share), BF16),
            pltpu.VMEM((1, share), F32), pltpu.VMEM(weight.shape, BF16), pltpu.VMEM((TFEAT, share), BF16),
            pltpu.VMEM(noise.shape, F32), pltpu.VMEM((LANES, depth), BF16), pltpu.VMEM(time_weight.shape, BF16),
            dma((11,)), pltpu.VMEM((8, TFEAT), F32),
            pltpu.VMEM((clips, 8, TFEAT), F32), dma((clips - 1,)), dma((clips - 1,)),
            edge, edge, edge, dma((2,)), dma((2,)),
            pltpu.VMEM((3, clips, chunk, part), BF16), pltpu.VMEM((3, clips - 1, chunk, part), BF16),
            pltpu.VMEM((clips, 2, 3 * part), F32), pltpu.VMEM((clips - 1, 2, 3 * part), F32),
            dma((3, clips - 1)), dma((3, clips - 1)), dma((clips - 1,)), dma((clips - 1,)),
            pltpu.VMEM((peers, tokens, LANES), BF16), dma((peers - 1,)), dma((peers - 1,)),
            pltpu.VMEM((clips, peers, chunk, 3 * part), BF16), pltpu.VMEM((peers, 2, 3 * part), F32),
            dma((peers - 1,)), dma((peers - 1,)), dma((peers - 1,)), dma((peers - 1,)),
            dma((peers, clips // 2)), dma((peers, clips // 2)), dma((peers, clips // 2)), dma((peers, clips // 2)),
        ],
        compiler_params=pltpu.CompilerParams(collective_id=0, has_side_effects=True),
        name="front",
    )(flow_times, source, features, enc, embed_cut, gain, weight, time_cut, noise, embed_weight, time_weight)
    output, output_t = attend(x, x_own, weights, peers * part)
    return output[None], output_t[None]


def solution(mesh):
    placed = (
        P("clip", None, "seq", None, None),
        P(),
        P("clip", None, "seq", None, None),
        P("clip", None),
        P(),
        P(),
        P(),
        P("clip", None, "seq"),
    )
    return jax.shard_map(
        local,
        mesh=mesh,
        in_specs=placed,
        out_specs=(P("clip", "seq", None), P("clip", "seq", None)),
        check_vma=False,
    )
```

```python
import functools

import jax
import jax.numpy as jnp
import numpy as np
from jax import lax
from jax.experimental import pallas as pl
from jax.experimental.pallas import tpu as pltpu
from jax.sharding import PartitionSpec as P

HD = 128
TFEAT = 256
TGRID = 1000
EPSILON = 1e-06
LANES = 128
TAIL = 16
NEAR = 1
F32 = jnp.float32
BF16 = jnp.bfloat16


def split(value, parts):
    terms = []
    for _ in range(parts):
        term = value.astype(BF16)
        terms.append(term)
        value = value - term.astype(F32)
    return terms


def dot(a, b):
    return jnp.dot(a, b, preferred_element_type=F32)


def dot_nt(a, b):
    return lax.dot_general(a, b, (((1,), (1,)), ((), ())), preferred_element_type=F32)


def conv_part(features, weight, frames, width, chans):
    pixels = features.shape[1]
    taps = [dot_nt(weight[...], features[f]) for f in range(frames)]
    lane = lax.broadcasted_iota(jnp.int32, (chans, pixels), 1)
    column = lax.rem(lane, width)
    block = 9 * chans
    own, edge = [], []
    for f in range(frames):
        acc = taps[f][2 * block : 3 * block]
        if f >= 1:
            acc = acc + taps[f - 1][block : 2 * block]
        if f >= 2:
            acc = acc + taps[f - 2][:block]
        rows = []
        for b in range(3):
            part = [acc[(b * 3 + e) * chans : (b * 3 + e + 1) * chans] for e in range(3)]
            total = part[1]
            total = total + jnp.where(column > 0, pltpu.roll(part[0], 1, 1), 0.0)
            total = total + jnp.where(column < width - 1, pltpu.roll(part[2], pixels - 1, 1), 0.0)
            rows.append(total)
        down = pltpu.roll(rows[0], width, 1)
        up = pltpu.roll(rows[2], pixels - width, 1)
        here = rows[1] + jnp.where(lane >= width, down, 0.0)
        own.append(here + jnp.where(lane < pixels - width, up, 0.0))
        edge.append(jnp.where(lane < width, down, up))
    return jnp.concatenate(own, axis=1), jnp.concatenate(edge, axis=1)


def tokens_part(latent, noise, pick, flow_t, chans):
    tokens = pick.shape[1] // 4
    terms = split(latent, 3) + split(noise, 3)
    moved = dot(jnp.concatenate(terms, axis=0), pick)
    lat = moved[:chans] + moved[chans : 2 * chans] + moved[2 * chans : 3 * chans]
    noi = moved[3 * chans : 4 * chans] + moved[4 * chans : 5 * chans] + moved[5 * chans :]
    noisy = (1.0 - flow_t) * lat + flow_t * noi
    velocity = noi - lat
    stacked = jnp.concatenate(
        [noisy[:, k * tokens : (k + 1) * tokens] for k in range(4)]
        + [velocity[:, k * tokens : (k + 1) * tokens] for k in range(4)],
        axis=0,
    )
    flipped = stacked.T
    return flipped.astype(BF16)


def norm_part(raw, gram_pair, depth, patch):
    tokens = raw.shape[0]
    lane = lax.broadcasted_iota(jnp.int32, (tokens, LANES), 1)
    both = raw.astype(F32)
    noisy = jnp.where(lane < patch, both, 0.0)
    velocity = jnp.where(lane < patch, pltpu.roll(both, LANES - patch, 1), 0.0)
    ones = jnp.where((lane == patch) | (lane == patch + 1), 1.0, noisy)
    ones_t = jnp.where((lane == patch + 2) | (lane == patch + 3), 1.0, velocity)
    left = ones.astype(BF16)
    moved = dot(jnp.concatenate([left, left], axis=1), gram_pair)
    mean_sq = jnp.sum(moved * ones, axis=1, keepdims=True) / depth
    mean_cr = jnp.sum(moved * ones_t, axis=1, keepdims=True) / depth
    inv = lax.rsqrt(mean_sq + EPSILON)
    shift = -(inv * inv * inv) * mean_cr
    inv_hi, inv_lo = [v.astype(F32) for v in split(inv, 2)]
    sh_hi, sh_lo = [v.astype(F32) for v in split(shift, 2)]
    rows, rows_t = noisy * inv, velocity * inv + noisy * shift
    for index, column in enumerate([inv_hi, inv_lo]):
        rows = jnp.where(lane == patch + index, column, rows)
    for index, column in enumerate([sh_hi, sh_lo, inv_hi, inv_lo]):
        rows_t = jnp.where(lane == patch + index, column, rows_t)
    return rows.astype(BF16), rows_t.astype(BF16)


MESH = pl.DeviceIdType.MESH


def attend_heads(x_ref, own_ref, pieces, store):
    tokens = own_ref.shape[0] // 2
    fold = HD ** (-0.5) * np.log2(np.e).astype(np.float32)
    ln2 = np.log(2.0).astype(np.float32)
    zero = jnp.zeros((tokens, LANES), BF16)

    def tall(rows):
        return jnp.concatenate([rows, jnp.zeros((LANES - rows.shape[0], HD), BF16)], axis=0)

    inner = [(dot_nt(tall(q), tall(k)) * fold).astype(BF16) for q, k, _ in pieces]
    u = dot(own_ref[...], jnp.concatenate(inner, axis=1)).astype(BF16)
    ys = []
    for h in range(len(pieces)):
        at = slice(h * HD, (h + 1) * HD)
        left = jnp.concatenate(
            [jnp.concatenate([u[:tokens, at], zero], axis=1), jnp.concatenate([u[tokens:, at], u[:tokens, at]], axis=1)],
            axis=0,
        )
        both = dot_nt(left, x_ref[...])
        scores, score_t = both[:tokens], both[tokens:]
        expo = jnp.exp2(scores - jnp.max(scores, axis=1, keepdims=True))
        inv = 1.0 / jnp.sum(expo, axis=1, keepdims=True)
        mean = jnp.sum(expo * score_t, axis=1, keepdims=True) * inv
        left = jnp.concatenate([expo.astype(BF16), (expo * (score_t - mean)).astype(BF16)], axis=0)
        both = dot(left, x_ref[...])
        y = both[:tokens, :LANES] * inv
        yt = both[tokens:, :LANES] * (inv * ln2) + both[:tokens, LANES:] * inv
        ys.append(jnp.concatenate(split(jnp.concatenate([y, yt], axis=0), 2), axis=1))
    for h, (_, _, v) in enumerate(pieces):
        both = dot(ys[h], jnp.concatenate([tall(v), tall(v)], axis=0))
        store(h, both[:tokens].astype(BF16), both[tokens:].astype(BF16))


def pieces_of(m_ref, k):
    part = m_ref.shape[2] // 3
    cols = [slice(h * HD, (h + 1) * HD) for h in range(3 * part // HD)]
    per = part // HD
    return [[m_ref[k, :, cols[g * per + h]] for g in range(3)] for h in range(per)]


def flip(index, bits):
    place = 1
    while place <= bits:
        if bits & place:
            index = index + place - 2 * place * lax.rem(index // place, 2)
        place *= 2
    return index


def front_kernel(
    dims,
    flow_ref, source_ref, f_hbm, enc_hbm, ecut_hbm, gcut_hbm, w_hbm, tcut_hbm, noise_hbm, embed_hbm, time_hbm,
    x_out, x_own, m_out, near_out,
    f_ref, enc_ref, ecut_ref, gcut_ref, w_ref, tcut_ref, noise_ref, embed_ref, time_ref, load_sem, feats_ref,
    feats_buf, feats_send, feats_recv,
    edge_buf, before_buf, after_buf, edge_send, edge_recv,
    e_send, e_recv, tau_send, tau_recv, e_ss, e_rs, t_ss, t_rs,
    x_buf, x_ss, x_rs,
    g_buf, tau_buf, b_ss, b_rs, bt_ss, bt_rs, a_ss, a_rs, c_ss, c_rs, m_ref,
):
    frames, width, chans, patch, peers, clips = dims
    seq, clip = lax.axis_index("seq"), lax.axis_index("clip")
    depth = embed_ref.shape[1]
    share = ecut_ref.shape[1]
    part = w_ref.shape[2]
    chunk = patch // clips
    on_seq = [{"seq": flip(seq, k)} for k in range(1, peers)]
    on_clip = [{"clip": flip(clip, k)} for k in range(1, clips)]
    mate = on_clip[0]

    barrier = pltpu.get_barrier_semaphore()
    for who in on_seq + on_clip:
        pl.semaphore_signal(barrier, inc=1, device_id=who, device_id_type=MESH)

    def cut(ref):
        if ref.shape[-1] == share:
            return ref
        return ref.at[:, pl.ds(pl.multiple_of(clip * share, share), share)]

    pairs = [(f_hbm, f_ref), (enc_hbm, enc_ref), (cut(ecut_hbm), ecut_ref), (cut(gcut_hbm), gcut_ref)]
    pairs += [(w_hbm.at[i], w_ref.at[i]) for i in range(3)]
    pairs += [
        (cut(tcut_hbm), tcut_ref), (noise_hbm, noise_ref), (embed_hbm, embed_ref.at[:patch]), (time_hbm, time_ref),
    ]
    loads = [pltpu.make_async_copy(src, dst, load_sem.at[k]) for k, (src, dst) in enumerate(pairs)]
    for load in loads:
        load.start()
    f_load, enc_load, ecut_load, gcut_load, w0, w1, w2, tcut_load, noise_load, embed_load, time_load = loads
    flow_r = flow_ref[0, 0].astype(F32) / TGRID
    flow_t = flow_ref[0, 1].astype(F32) / TGRID
    quarter = TFEAT // 4
    order = lax.broadcasted_iota(jnp.int32, (8, TFEAT), 1)
    line = lax.broadcasted_iota(jnp.int32, (8, TFEAT), 0)
    omega = 8.0 * jnp.exp(-np.float32(np.log(100.0)) * lax.rem(order, quarter).astype(F32) / quarter)
    angle = omega * jnp.where(order < 2 * quarter, flow_t, flow_t - flow_r)
    sine, cosine = jnp.sin(angle), jnp.cos(angle)
    first = lax.rem(order // quarter, 2) == 0
    feats_ref[...] = jnp.where(
        line == 0,
        jnp.where(first, sine, cosine),
        jnp.where(line == 1, jnp.where(first, omega * cosine, -omega * sine), 0.0),
    )
    sent = []

    def push(src, dst, ssem, rsem, who):
        copy = pltpu.make_async_remote_copy(
            src_ref=src, dst_ref=dst, send_sem=ssem, recv_sem=rsem, device_id=who, device_id_type=MESH
        )
        copy.start()
        sent.append(copy)
        return copy

    f_load.wait()
    enc_load.wait()
    own, edge = conv_part(f_ref, enc_ref, frames, width, chans)
    edge_buf[...] = edge

    @pl.when(seq == 0)
    def _():
        before_buf[...] = jnp.zeros_like(before_buf)

    @pl.when(seq == peers - 1)
    def _():
        after_buf[...] = jnp.zeros_like(after_buf)

    pl.semaphore_wait(barrier, len(on_seq) + len(on_clip))
    feats_in = [
        push(feats_ref, feats_buf.at[clip], feats_send.at[k], feats_recv.at[k], who) for k, who in enumerate(on_clip)
    ]
    feats_buf[clip] = feats_ref[...]

    def edge_copy(dst, k, step):
        return pltpu.make_async_remote_copy(
            src_ref=edge_buf, dst_ref=dst, send_sem=edge_send.at[k], recv_sem=edge_recv.at[k],
            device_id={"seq": lax.rem(seq + peers + step, peers)}, device_id_type=MESH,
        )

    to_next, to_last = edge_copy(before_buf, 0, 1), edge_copy(after_buf, 1, -1)

    @pl.when(seq < peers - 1)
    def _():
        to_next.start()

    @pl.when(seq > 0)
    def _():
        to_last.start()

    ecut_load.wait()
    gcut_load.wait()
    gain = gcut_ref[...]
    left = jnp.concatenate(split(ecut_ref[...].astype(F32) * gain, 2), axis=0)
    e_in = []
    for i, load in enumerate((w0, w1, w2)):
        load.wait()
        both = dot(left, w_ref[i])
        both = both[:patch] + both[patch:]
        for c in range(clips):
            e_send[i, c] = both[c * chunk : (c + 1) * chunk].astype(BF16)
        e_in.append([
            push(e_send.at[i, flip(clip, k + 1)], e_recv.at[i, k], e_ss.at[i, k], e_rs.at[i, k], who)
            for k, who in enumerate(on_clip)
        ])
    for copy in feats_in:
        copy.wait_recv()
    tcut_load.wait()
    feats = feats_buf[...].reshape(clips * 8, feats_buf.shape[2])
    both = dot(jnp.concatenate(split(feats, 2), axis=0), tcut_ref[...])
    left = jnp.concatenate(split((both[: clips * 8] + both[clips * 8 :]) * gain, 2), axis=0)
    for i in range(3):
        both = dot(left, w_ref[i])
        both = both[: clips * 8] + both[clips * 8 :]
        for c in range(clips):
            tau_send[c, :, i * part : (i + 1) * part] = both[c * 8 : c * 8 + 2]
    tau_in = [
        push(tau_send.at[flip(clip, k + 1)], tau_recv.at[k], t_ss.at[k], t_rs.at[k], who)
        for k, who in enumerate(on_clip)
    ]

    @pl.when(seq > 0)
    def _():
        to_next.wait_recv()

    @pl.when(seq < peers - 1)
    def _():
        to_last.wait_recv()

    pixels = f_ref.shape[1]
    lane = lax.rem(lax.broadcasted_iota(jnp.int32, own.shape, 1), pixels)
    latent = own + jnp.where(lane < width, before_buf[...], 0.0)
    latent = latent + jnp.where(lane >= pixels - width, after_buf[...], 0.0)
    noise_load.wait()
    noise = jnp.concatenate(
        [noise_ref[f, r] for f in range(frames) for r in range(noise_ref.shape[1])], axis=1
    )
    places = lax.broadcasted_iota(jnp.int32, (own.shape[1], source_ref.shape[1]), 0)
    pick = (places == source_ref[...]).astype(F32).astype(BF16)
    x_buf[seq] = tokens_part(latent, noise, pick, flow_t, chans)
    x_in = [push(x_buf.at[seq], x_buf.at[seq], x_ss.at[k], x_rs.at[k], who) for k, who in enumerate(on_seq)]

    for i in range(3):
        for copy in e_in[i]:
            copy.wait_recv()
        total = e_send[i, clip].astype(F32)
        for k in range(clips - 1):
            total = total + e_recv[i, k].astype(F32)
        g_buf[clip, seq, :, i * part : (i + 1) * part] = total.astype(BF16)

    b_in = [
        push(g_buf.at[clip, seq], g_buf.at[clip, seq], b_ss.at[k], b_rs.at[k], who) for k, who in enumerate(on_seq)
    ]

    def spread(k):
        block = g_buf.at[clip, flip(seq, k)]
        a_in.append([
            push(block, block, a_ss.at[k, j], a_rs.at[k, j], on_clip[2 * j + 1]) for j in range(clips // 2 - 1)
        ])
        c_in.append(push(block, block, c_ss.at[k, 0], c_rs.at[k, 0], mate))

    a_in, c_in = [], []
    spread(0)
    for copy in tau_in:
        copy.wait_recv()
    total = tau_send[clip]
    for k in range(clips - 1):
        total = total + tau_recv[k]
    tau_buf[seq] = total.astype(BF16)
    bt_in = [
        push(tau_buf.at[seq], tau_buf.at[seq], bt_ss.at[k], bt_rs.at[k], who) for k, who in enumerate(on_seq)
    ]
    time_load.wait()
    mine = jnp.concatenate(split(feats_ref[...], 2), axis=0)
    times = dot(mine, time_ref[...])
    times = times[:8] + times[8:]
    time_hi, time_lo = split(times, 2)
    filler = jnp.zeros((LANES - patch - 4, depth), BF16)
    rest = jnp.concatenate([time_hi[:1], time_lo[:1], time_hi[1:2], time_lo[1:2], filler], axis=0)
    embed_ref[patch:] = rest
    embed_load.wait()
    table = embed_ref[...]
    gram_pair = jnp.concatenate(split(dot_nt(table, table), 2), axis=0)

    for copy in x_in:
        copy.wait_recv()
    tokens = x_buf.shape[1]
    for p in range(peers):
        rows, rows_t = norm_part(x_buf[p], gram_pair, depth, patch)
        x_out[p * tokens : (p + 1) * tokens, :LANES] = rows
        x_out[p * tokens : (p + 1) * tokens, LANES:] = rows_t
    x_own[:tokens] = x_out[pl.ds(pl.multiple_of(seq * tokens, tokens), tokens), :LANES]
    x_own[tokens:] = x_out[pl.ds(pl.multiple_of(seq * tokens, tokens), tokens), LANES:]
    for k, copy in enumerate(b_in):
        copy.wait_recv()
        spread(k + 1)
    for copy in bt_in:
        copy.wait_recv()
    far = []

    def relay(k):
        p = flip(seq, k)
        relays = []
        for j, copy in enumerate(a_in[k]):
            copy.wait_recv()
            block = g_buf.at[flip(clip, 2 * j + 2), p]
            relays.append(push(block, block, c_ss.at[k, j + 1], c_rs.at[k, j + 1], mate))
        far.append(relays)

    def finish(k, whole, slot):
        p = flip(seq, k)
        for copy in [c_in[k]] + far[k]:
            copy.wait_recv()
        for c in range(clips):
            whole[slot, c * chunk : (c + 1) * chunk] = g_buf[c, p]
        tau = tau_buf[p].astype(F32)
        extra = [tau[0:1], tau[0:1], tau[1:2], tau[1:2]]
        row = lax.broadcasted_iota(jnp.int32, (TAIL, 3 * part), 0)
        tail = jnp.zeros((TAIL, 3 * part), F32)
        for index, value in enumerate(extra):
            tail = jnp.where(row == index, value, tail)
        whole[slot, patch:] = tail.astype(BF16)

    for k in range(NEAR):
        relay(k)
        finish(k, m_ref, k)

        def store(h, out, out_t):
            near_out[0, k, :, h * HD : (h + 1) * HD] = out
            near_out[1, k, :, h * HD : (h + 1) * HD] = out_t

        attend_heads(x_out, x_own, pieces_of(m_ref, k), store)
    for k in range(NEAR, peers):
        relay(k)
        if k > NEAR:
            finish(k - 1, m_out, k - 1 - NEAR)
    finish(peers - 1, m_out, peers - 1 - NEAR)
    for copy in sent:
        copy.wait_send()

    @pl.when(seq < peers - 1)
    def _():
        to_next.wait_send()

    @pl.when(seq > 0)
    def _():
        to_last.wait_send()


def attend_kernel(x_ref, own_ref, m_ref, near_ref, out_hbm, out_t_hbm, far_ref, near_sem, far_sem):
    seq = lax.axis_index("seq")
    part = m_ref.shape[2] // 3
    per = part // HD
    outs = (out_hbm, out_t_hbm)

    def place(k):
        return pl.ds(pl.multiple_of(flip(seq, k) * part, part), part)

    moves = [
        pltpu.make_async_copy(near_ref.at[i, k], outs[i].at[:, place(k)], near_sem.at[i, k])
        for k in range(NEAR) for i in range(2)
    ]
    for move in moves:
        move.start()
    pieces = [piece for k in range(m_ref.shape[0]) for piece in pieces_of(m_ref, k)]

    def store(h, out, out_t):
        k, at = h // per, slice(h % per * HD, (h % per + 1) * HD)
        far_ref[0, k, :, at] = out
        far_ref[1, k, :, at] = out_t
        if h % per == per - 1:
            for i in range(2):
                moves.append(pltpu.make_async_copy(far_ref.at[i, k], outs[i].at[:, place(NEAR + k)], far_sem.at[i, k]))
                moves[-1].start()

    attend_heads(x_ref, own_ref, pieces, store)
    for move in moves:
        move.wait()


VMEM = pl.BlockSpec(memory_space=pltpu.VMEM)


def attend(rows, own, weights, near, inner):
    tokens, far, part = own.shape[0] // 2, weights.shape[0], weights.shape[2] // 3
    shape = jax.ShapeDtypeStruct((tokens, inner), BF16)
    anywhere = pl.BlockSpec(memory_space=pl.ANY)
    return pl.pallas_call(
        attend_kernel,
        out_shape=(shape, shape),
        in_specs=[VMEM, VMEM, VMEM, VMEM],
        out_specs=(anywhere, anywhere),
        scratch_shapes=[
            pltpu.VMEM((2, far, tokens, part), BF16),
            pltpu.SemaphoreType.DMA((2, NEAR)), pltpu.SemaphoreType.DMA((2, far)),
        ],
        name="attend",
    )(rows, own, weights, near)


def local(clip_features, enc_weight, noise_field, flow_times, embed_weight, time_weight, norm_gain, qkv_weight):
    _, frames, rows, width, depth_c = clip_features.shape
    chans = enc_weight.shape[4]
    patch, depth = embed_weight.shape
    peers, clips = lax.axis_size("seq"), lax.axis_size("clip")
    share = qkv_weight.shape[0]
    part = qkv_weight.shape[2]
    pixels = rows * width
    tokens = frames * pixels // 4

    gain, embed_cut, time_cut = norm_gain[None, :], embed_weight, time_weight
    if share % LANES:
        me = lax.axis_index("clip")
        gain, embed_cut, time_cut = (
            lax.dynamic_slice_in_dim(m, me * share, share, 1) for m in (gain, embed_weight, time_weight)
        )
    weight = qkv_weight.transpose(1, 0, 2)
    features = clip_features.reshape(frames, pixels, depth_c)
    enc = enc_weight.transpose(0, 1, 2, 4, 3).reshape(27 * chans, depth_c)
    noise = noise_field[0].transpose(0, 1, 3, 2)
    i, f, j = np.meshgrid(np.arange(rows // 2), np.arange(frames), np.arange(width // 2), indexing="ij")
    source = np.stack(
        [((f * rows + 2 * i + p) * width + 2 * j + q).reshape(-1) for p in range(2) for q in range(2)]
    ).reshape(1, -1)
    source = jnp.asarray(source.astype(np.int32))
    chunk = patch // clips
    dma = pltpu.SemaphoreType.DMA
    anywhere = pl.BlockSpec(memory_space=pl.ANY)
    edge = pltpu.VMEM((chans, frames * pixels), F32)
    x, x_own, weights, near = pl.pallas_call(
        functools.partial(front_kernel, (frames, width, chans, patch, peers, clips)),
        out_shape=(
            jax.ShapeDtypeStruct((peers * tokens, 2 * LANES), BF16),
            jax.ShapeDtypeStruct((2 * tokens, LANES), BF16),
            jax.ShapeDtypeStruct((peers - NEAR, patch + TAIL, 3 * part), BF16),
            jax.ShapeDtypeStruct((2, NEAR, tokens, part), BF16),
        ),
        in_specs=[pl.BlockSpec(memory_space=pltpu.SMEM), VMEM] + [anywhere] * 9,
        out_specs=(VMEM,) * 4,
        scratch_shapes=[
            pltpu.VMEM(features.shape, BF16), pltpu.VMEM(enc.shape, BF16), pltpu.VMEM((patch, share), BF16),
            pltpu.VMEM((1, share), F32), pltpu.VMEM(weight.shape, BF16), pltpu.VMEM((TFEAT, share), BF16),
            pltpu.VMEM(noise.shape, F32), pltpu.VMEM((LANES, depth), BF16), pltpu.VMEM(time_weight.shape, BF16),
            dma((11,)), pltpu.VMEM((8, TFEAT), F32),
            pltpu.VMEM((clips, 8, TFEAT), F32), dma((clips - 1,)), dma((clips - 1,)),
            edge, edge, edge, dma((2,)), dma((2,)),
            pltpu.VMEM((3, clips, chunk, part), BF16), pltpu.VMEM((3, clips - 1, chunk, part), BF16),
            pltpu.VMEM((clips, 2, 3 * part), F32), pltpu.VMEM((clips - 1, 2, 3 * part), F32),
            dma((3, clips - 1)), dma((3, clips - 1)), dma((clips - 1,)), dma((clips - 1,)),
            pltpu.VMEM((peers, tokens, LANES), BF16), dma((peers - 1,)), dma((peers - 1,)),
            pltpu.VMEM((clips, peers, chunk, 3 * part), BF16), pltpu.VMEM((peers, 2, 3 * part), BF16),
            dma((peers - 1,)), dma((peers - 1,)), dma((peers - 1,)), dma((peers - 1,)),
            dma((peers, clips // 2)), dma((peers, clips // 2)), dma((peers, clips // 2)), dma((peers, clips // 2)),
            pltpu.VMEM((NEAR, patch + TAIL, 3 * part), BF16),
        ],
        compiler_params=pltpu.CompilerParams(collective_id=0, has_side_effects=True),
        name="front",
    )(flow_times, source, features, enc, embed_cut, gain, weight, time_cut, noise, embed_weight, time_weight)
    output, output_t = attend(x, x_own, weights, near, peers * part)
    return output[None], output_t[None]


def solution(mesh):
    placed = (
        P("clip", None, "seq", None, None),
        P(),
        P("clip", None, "seq", None, None),
        P("clip", None),
        P(),
        P(),
        P(),
        P("clip", None, "seq"),
    )
    return jax.shard_map(
        local,
        mesh=mesh,
        in_specs=placed,
        out_specs=(P("clip", "seq", None), P("clip", "seq", None)),
        check_vma=False,
    )
```

```python
import functools

import jax
import jax.numpy as jnp
import numpy as np
from jax import lax
from jax.experimental import pallas as pl
from jax.experimental.pallas import tpu as pltpu
from jax.sharding import PartitionSpec as P

HD = 128
TFEAT = 256
TGRID = 1000
EPSILON = 1e-06
LANES = 128
TAIL = 16
NEAR = 1
F32 = jnp.float32
BF16 = jnp.bfloat16


def split(value, parts):
    terms = []
    for _ in range(parts):
        term = value.astype(BF16)
        terms.append(term)
        value = value - term.astype(F32)
    return terms


def dot(a, b):
    return jnp.dot(a, b, preferred_element_type=F32)


def dot_nt(a, b):
    return lax.dot_general(a, b, (((1,), (1,)), ((), ())), preferred_element_type=F32)


def conv_part(features, weight, frames, width, chans):
    pixels = features.shape[1]
    taps = [dot_nt(weight[...], features[f]) for f in range(frames)]
    lane = lax.broadcasted_iota(jnp.int32, (chans, pixels), 1)
    column = lax.rem(lane, width)
    block = 9 * chans
    own, edge = [], []
    for f in range(frames):
        acc = taps[f][2 * block : 3 * block]
        if f >= 1:
            acc = acc + taps[f - 1][block : 2 * block]
        if f >= 2:
            acc = acc + taps[f - 2][:block]
        rows = []
        for b in range(3):
            part = [acc[(b * 3 + e) * chans : (b * 3 + e + 1) * chans] for e in range(3)]
            total = part[1]
            total = total + jnp.where(column > 0, pltpu.roll(part[0], 1, 1), 0.0)
            total = total + jnp.where(column < width - 1, pltpu.roll(part[2], pixels - 1, 1), 0.0)
            rows.append(total)
        down = pltpu.roll(rows[0], width, 1)
        up = pltpu.roll(rows[2], pixels - width, 1)
        here = rows[1] + jnp.where(lane >= width, down, 0.0)
        own.append(here + jnp.where(lane < pixels - width, up, 0.0))
        edge.append(jnp.where(lane < width, down, up))
    return jnp.concatenate(own, axis=1), jnp.concatenate(edge, axis=1)


def tokens_part(latent, noise, pick, flow_t, chans):
    tokens = pick.shape[1] // 4
    terms = split(latent, 3) + split(noise, 3)
    moved = dot(jnp.concatenate(terms, axis=0), pick)
    lat = moved[:chans] + moved[chans : 2 * chans] + moved[2 * chans : 3 * chans]
    noi = moved[3 * chans : 4 * chans] + moved[4 * chans : 5 * chans] + moved[5 * chans :]
    noisy = (1.0 - flow_t) * lat + flow_t * noi
    velocity = noi - lat
    stacked = jnp.concatenate(
        [noisy[:, k * tokens : (k + 1) * tokens] for k in range(4)]
        + [velocity[:, k * tokens : (k + 1) * tokens] for k in range(4)],
        axis=0,
    )
    flipped = stacked.T
    return flipped.astype(BF16)


def norm_part(raw, gram_pair, depth, patch):
    tokens = raw.shape[0]
    lane = lax.broadcasted_iota(jnp.int32, (tokens, LANES), 1)
    both = raw.astype(F32)
    noisy = jnp.where(lane < patch, both, 0.0)
    velocity = jnp.where(lane < patch, pltpu.roll(both, LANES - patch, 1), 0.0)
    ones = jnp.where((lane == patch) | (lane == patch + 1), 1.0, noisy)
    ones_t = jnp.where((lane == patch + 2) | (lane == patch + 3), 1.0, velocity)
    left = ones.astype(BF16)
    moved = dot(jnp.concatenate([left, left], axis=1), gram_pair)
    mean_sq = jnp.sum(moved * ones, axis=1, keepdims=True) / depth
    mean_cr = jnp.sum(moved * ones_t, axis=1, keepdims=True) / depth
    inv = lax.rsqrt(mean_sq + EPSILON)
    shift = -(inv * inv * inv) * mean_cr
    inv_hi, inv_lo = [v.astype(F32) for v in split(inv, 2)]
    sh_hi, sh_lo = [v.astype(F32) for v in split(shift, 2)]
    rows, rows_t = noisy * inv, velocity * inv + noisy * shift
    for index, column in enumerate([inv_hi, inv_lo, inv_hi]):
        rows = jnp.where(lane == patch + index, column, rows)
    for index, column in enumerate([sh_hi, sh_lo, sh_hi, inv_hi, inv_lo, inv_hi]):
        rows_t = jnp.where(lane == patch + index, column, rows_t)
    return rows.astype(BF16), rows_t.astype(BF16)


MESH = pl.DeviceIdType.MESH


def attend_heads(x_ref, own_ref, pieces, store):
    tokens = own_ref.shape[0] // 2
    fold = HD ** (-0.5) * np.log2(np.e).astype(np.float32)
    ln2 = np.log(2.0).astype(np.float32)
    zero = jnp.zeros((tokens, LANES), BF16)

    def tall(rows):
        return jnp.concatenate([rows, jnp.zeros((LANES - rows.shape[0], HD), BF16)], axis=0)

    inner = [(dot_nt(tall(q), tall(k)) * fold).astype(BF16) for q, k, _ in pieces]
    u = dot(own_ref[...], jnp.concatenate(inner, axis=1)).astype(BF16)
    ys = []
    for h in range(len(pieces)):
        at = slice(h * HD, (h + 1) * HD)
        left = jnp.concatenate(
            [jnp.concatenate([u[:tokens, at], zero], axis=1), jnp.concatenate([u[tokens:, at], u[:tokens, at]], axis=1)],
            axis=0,
        )
        both = dot_nt(left, x_ref[...])
        scores, score_t = both[:tokens], both[tokens:]
        expo = jnp.exp2(scores - jnp.max(scores, axis=1, keepdims=True))
        inv = 1.0 / jnp.sum(expo, axis=1, keepdims=True)
        mean = jnp.sum(expo * score_t, axis=1, keepdims=True) * inv
        left = jnp.concatenate([expo.astype(BF16), (expo * (score_t - mean)).astype(BF16)], axis=0)
        both = dot(left, x_ref[...])
        y = both[:tokens, :LANES] * inv
        yt = both[tokens:, :LANES] * (inv * ln2) + both[:tokens, LANES:] * inv
        ys.append(jnp.concatenate(split(jnp.concatenate([y, yt], axis=0), 2), axis=1))
    for h, (_, _, v) in enumerate(pieces):
        both = dot(ys[h], jnp.concatenate([tall(v), tall(v)], axis=0))
        store(h, both[:tokens].astype(BF16), both[tokens:].astype(BF16))


def pieces_of(m_ref, k):
    part = m_ref.shape[2] // 3
    cols = [slice(h * HD, (h + 1) * HD) for h in range(3 * part // HD)]
    per = part // HD
    return [[m_ref[k, :, cols[g * per + h]] for g in range(3)] for h in range(per)]


def flip(index, bits):
    place = 1
    while place <= bits:
        if bits & place:
            index = index + place - 2 * place * lax.rem(index // place, 2)
        place *= 2
    return index


def front_kernel(
    dims,
    flow_ref, source_ref, f_hbm, enc_hbm, ecut_hbm, gcut_hbm, w_hbm, tcut_hbm, noise_hbm, embed_hbm, time_hbm,
    x_out, x_own, m_out, near_out,
    f_ref, enc_ref, ecut_ref, gcut_ref, w_ref, tcut_ref, noise_ref, embed_ref, time_ref, load_sem, feats_ref,
    feats_buf, feats_send, feats_recv,
    edge_buf, before_buf, after_buf, edge_send, edge_recv,
    e_send, e_recv, tau_send, tau_recv, e_ss, e_rs, t_ss, t_rs,
    x_buf, x_ss, x_rs,
    g_buf, tau_buf, b_ss, b_rs, bt_ss, bt_rs, a_ss, a_rs, c_ss, c_rs, m_ref,
):
    frames, width, chans, patch, peers, clips = dims
    seq, clip = lax.axis_index("seq"), lax.axis_index("clip")
    depth = embed_ref.shape[1]
    share = ecut_ref.shape[1]
    part = w_ref.shape[2]
    chunk = patch // clips
    on_seq = [{"seq": flip(seq, k)} for k in range(1, peers)]
    on_clip = [{"clip": flip(clip, k)} for k in range(1, clips)]
    mate = on_clip[0]
    core, chip = lax.rem(clip, 2), clip // 2

    barrier = pltpu.get_barrier_semaphore()
    for who in on_seq + on_clip:
        pl.semaphore_signal(barrier, inc=1, device_id=who, device_id_type=MESH)

    def cut(ref):
        if ref.shape[-1] == share:
            return ref
        return ref.at[:, pl.ds(pl.multiple_of(clip * share, share), share)]

    pairs = [(f_hbm, f_ref), (enc_hbm, enc_ref), (cut(ecut_hbm), ecut_ref), (cut(gcut_hbm), gcut_ref)]
    pairs += [(w_hbm.at[i], w_ref.at[i]) for i in range(3)]
    pairs += [
        (cut(tcut_hbm), tcut_ref), (noise_hbm, noise_ref), (embed_hbm, embed_ref.at[:patch]), (time_hbm, time_ref),
    ]
    loads = [pltpu.make_async_copy(src, dst, load_sem.at[k]) for k, (src, dst) in enumerate(pairs)]
    for load in loads:
        load.start()
    f_load, enc_load, ecut_load, gcut_load, w0, w1, w2, tcut_load, noise_load, embed_load, time_load = loads
    flow_r = flow_ref[0, 0].astype(F32) / TGRID
    flow_t = flow_ref[0, 1].astype(F32) / TGRID
    quarter = TFEAT // 4
    order = lax.broadcasted_iota(jnp.int32, (8, TFEAT), 1)
    line = lax.broadcasted_iota(jnp.int32, (8, TFEAT), 0)
    omega = 8.0 * jnp.exp(-np.float32(np.log(100.0)) * lax.rem(order, quarter).astype(F32) / quarter)
    angle = omega * jnp.where(order < 2 * quarter, flow_t, flow_t - flow_r)
    sine, cosine = jnp.sin(angle), jnp.cos(angle)
    first = lax.rem(order // quarter, 2) == 0
    feats_ref[...] = jnp.where(
        line == 0,
        jnp.where(first, sine, cosine),
        jnp.where(line == 1, jnp.where(first, omega * cosine, -omega * sine), 0.0),
    )
    sent = []

    def push(src, dst, ssem, rsem, who):
        copy = pltpu.make_async_remote_copy(
            src_ref=src, dst_ref=dst, send_sem=ssem, recv_sem=rsem, device_id=who, device_id_type=MESH
        )
        copy.start()
        sent.append(copy)
        return copy

    f_load.wait()
    enc_load.wait()
    own, edge = conv_part(f_ref, enc_ref, frames, width, chans)
    edge_buf[...] = edge

    @pl.when(seq == 0)
    def _():
        before_buf[...] = jnp.zeros_like(before_buf)

    @pl.when(seq == peers - 1)
    def _():
        after_buf[...] = jnp.zeros_like(after_buf)

    pl.semaphore_wait(barrier, len(on_seq) + len(on_clip))
    feats_in = [
        push(feats_ref, feats_buf.at[clip], feats_send.at[k], feats_recv.at[k], who) for k, who in enumerate(on_clip)
    ]
    feats_buf[clip] = feats_ref[...]

    def edge_copy(dst, k, step):
        return pltpu.make_async_remote_copy(
            src_ref=edge_buf, dst_ref=dst, send_sem=edge_send.at[k], recv_sem=edge_recv.at[k],
            device_id={"seq": lax.rem(seq + peers + step, peers)}, device_id_type=MESH,
        )

    to_next, to_last = edge_copy(before_buf, 0, 1), edge_copy(after_buf, 1, -1)

    @pl.when(seq < peers - 1)
    def _():
        to_next.start()

    @pl.when(seq > 0)
    def _():
        to_last.start()

    ecut_load.wait()
    gcut_load.wait()
    gain = gcut_ref[...]
    left = jnp.concatenate(split(ecut_ref[...].astype(F32) * gain, 2), axis=0)
    e_in = []
    for i, load in enumerate((w0, w1, w2)):
        load.wait()
        both = dot(left, w_ref[i])
        both = both[:patch] + both[patch:]
        for c in range(clips):
            e_send[i, c] = both[c * chunk : (c + 1) * chunk].astype(BF16)
        e_in.append([
            push(e_send.at[i, flip(clip, k + 1)], e_recv.at[i, k], e_ss.at[i, k], e_rs.at[i, k], who)
            for k, who in enumerate(on_clip)
        ])
    for copy in feats_in:
        copy.wait_recv()
    tcut_load.wait()
    feats = feats_buf[...].reshape(clips * 8, feats_buf.shape[2])
    both = dot(jnp.concatenate(split(feats, 2), axis=0), tcut_ref[...])
    left = jnp.concatenate(split((both[: clips * 8] + both[clips * 8 :]) * gain, 2), axis=0)
    for i in range(3):
        both = dot(left, w_ref[i])
        both = both[: clips * 8] + both[clips * 8 :]
        for c in range(clips):
            tau_send[c, :, i * part : (i + 1) * part] = both[c * 8 : c * 8 + 2]
    tau_in = [
        push(tau_send.at[flip(clip, k + 1)], tau_recv.at[k], t_ss.at[k], t_rs.at[k], who)
        for k, who in enumerate(on_clip)
    ]

    @pl.when(seq > 0)
    def _():
        to_next.wait_recv()

    @pl.when(seq < peers - 1)
    def _():
        to_last.wait_recv()

    pixels = f_ref.shape[1]
    lane = lax.rem(lax.broadcasted_iota(jnp.int32, own.shape, 1), pixels)
    latent = own + jnp.where(lane < width, before_buf[...], 0.0)
    latent = latent + jnp.where(lane >= pixels - width, after_buf[...], 0.0)
    noise_load.wait()
    noise = jnp.concatenate(
        [noise_ref[f, r] for f in range(frames) for r in range(noise_ref.shape[1])], axis=1
    )
    places = lax.broadcasted_iota(jnp.int32, (own.shape[1], source_ref.shape[1]), 0)
    pick = (places == source_ref[...]).astype(F32).astype(BF16)
    x_buf[seq] = tokens_part(latent, noise, pick, flow_t, chans)
    x_in = [push(x_buf.at[seq], x_buf.at[seq], x_ss.at[k], x_rs.at[k], who) for k, who in enumerate(on_seq)]

    for i in range(3):
        for copy in e_in[i]:
            copy.wait_recv()
        total = e_send[i, clip].astype(F32)
        for k in range(clips - 1):
            total = total + e_recv[i, k].astype(F32)
        g_buf[core, chip, 0, :, i * part : (i + 1) * part] = total.astype(BF16)

    b_in = [
        push(g_buf.at[core, chip, 0], g_buf.at[core, chip, k + 1], b_ss.at[k], b_rs.at[k], who)
        for k, who in enumerate(on_seq)
    ]

    runs = [slice(k, k + 1) for k in range(peers)]
    a_in, c_in = [], []

    def spread(n):
        block = g_buf.at[core, chip, runs[n]]
        a_in.append([
            push(block, block, a_ss.at[n, j], a_rs.at[n, j], on_clip[2 * j + 1]) for j in range(clips // 2 - 1)
        ])

    spread(0)
    time_load.wait()
    mine = jnp.concatenate(split(feats_ref[...], 2), axis=0)
    times = dot(mine, time_ref[...])
    times = times[:8] + times[8:]
    time_hi, time_lo = split(times, 2)
    filler = jnp.zeros((LANES - patch - 4, depth), BF16)
    rest = jnp.concatenate([time_hi[:1], time_lo[:1], time_hi[1:2], time_lo[1:2], filler], axis=0)
    embed_ref[patch:] = rest
    embed_load.wait()
    table = embed_ref[...]
    gram_pair = jnp.concatenate(split(dot_nt(table, table), 2), axis=0)

    for copy in tau_in:
        copy.wait_recv()
    total = tau_send[clip]
    for k in range(clips - 1):
        total = total + tau_recv[k]
    tau_buf[0] = total
    bt_in = [
        push(tau_buf.at[0], tau_buf.at[k + 1], bt_ss.at[k], bt_rs.at[k], who) for k, who in enumerate(on_seq)
    ]
    def relay(n):
        for copy in a_in[n]:
            copy.wait_recv()
        block = g_buf.at[core, :, runs[n]]
        c_in.append(push(block, block, c_ss.at[n], c_rs.at[n], mate))

    def finish(k, whole, slot):
        if k:
            bt_in[k - 1].wait_recv()
        for c in range(clips):
            whole[slot, c * chunk : (c + 1) * chunk] = g_buf[c % 2, c // 2, k]
        hi = tau_buf[k].astype(BF16).astype(F32)
        lo = tau_buf[k] - hi
        extra = [hi[0:1], hi[0:1], lo[0:1], hi[1:2], hi[1:2], lo[1:2]]
        row = lax.broadcasted_iota(jnp.int32, (TAIL, 3 * part), 0)
        tail = jnp.zeros((TAIL, 3 * part), F32)
        for index, value in enumerate(extra):
            tail = jnp.where(row == index, value, tail)
        whole[slot, patch:] = tail.astype(BF16)

    relay(0)
    for n, run in list(enumerate(runs))[1:]:
        for copy in b_in[run.start - 1 : run.stop - 1]:
            copy.wait_recv()
        spread(n)
    for copy in x_in:
        copy.wait_recv()
    tokens = x_buf.shape[1]
    for p in range(peers):
        rows, rows_t = norm_part(x_buf[p], gram_pair, depth, patch)
        x_out[p * tokens : (p + 1) * tokens, :LANES] = rows
        x_out[p * tokens : (p + 1) * tokens, LANES:] = rows_t
    x_own[:tokens] = x_out[pl.ds(pl.multiple_of(seq * tokens, tokens), tokens), :LANES]
    x_own[tokens:] = x_out[pl.ds(pl.multiple_of(seq * tokens, tokens), tokens), LANES:]
    c_in[0].wait_recv()
    for k in range(NEAR):
        finish(k, m_ref, k)

        def store(h, out, out_t):
            near_out[0, k, :, h * HD : (h + 1) * HD] = out
            near_out[1, k, :, h * HD : (h + 1) * HD] = out_t

        attend_heads(x_out, x_own, pieces_of(m_ref, k), store)
    for n in range(1, len(runs)):
        relay(n)
    for n, run in list(enumerate(runs))[1:]:
        c_in[n].wait_recv()
        for k in range(run.start, run.stop):
            finish(k, m_out, k - NEAR)
    for copy in sent:
        copy.wait_send()

    @pl.when(seq < peers - 1)
    def _():
        to_next.wait_send()

    @pl.when(seq > 0)
    def _():
        to_last.wait_send()


def attend_kernel(x_ref, own_ref, m_ref, near_ref, out_hbm, out_t_hbm, far_ref, near_sem, far_sem):
    seq = lax.axis_index("seq")
    part = m_ref.shape[2] // 3
    per = part // HD
    outs = (out_hbm, out_t_hbm)

    def place(k):
        return pl.ds(pl.multiple_of(flip(seq, k) * part, part), part)

    moves = [
        pltpu.make_async_copy(near_ref.at[i, k], outs[i].at[:, place(k)], near_sem.at[i, k])
        for k in range(NEAR) for i in range(2)
    ]
    for move in moves:
        move.start()
    pieces = [piece for k in range(m_ref.shape[0]) for piece in pieces_of(m_ref, k)]

    def store(h, out, out_t):
        k, at = h // per, slice(h % per * HD, (h % per + 1) * HD)
        far_ref[0, k, :, at] = out
        far_ref[1, k, :, at] = out_t
        if h % per == per - 1:
            for i in range(2):
                moves.append(pltpu.make_async_copy(far_ref.at[i, k], outs[i].at[:, place(NEAR + k)], far_sem.at[i, k]))
                moves[-1].start()

    attend_heads(x_ref, own_ref, pieces, store)
    for move in moves:
        move.wait()


VMEM = pl.BlockSpec(memory_space=pltpu.VMEM)


def attend(rows, own, weights, near, inner):
    tokens, far, part = own.shape[0] // 2, weights.shape[0], weights.shape[2] // 3
    shape = jax.ShapeDtypeStruct((tokens, inner), BF16)
    anywhere = pl.BlockSpec(memory_space=pl.ANY)
    return pl.pallas_call(
        attend_kernel,
        out_shape=(shape, shape),
        in_specs=[VMEM, VMEM, VMEM, VMEM],
        out_specs=(anywhere, anywhere),
        scratch_shapes=[
            pltpu.VMEM((2, far, tokens, part), BF16),
            pltpu.SemaphoreType.DMA((2, NEAR)), pltpu.SemaphoreType.DMA((2, far)),
        ],
        name="attend",
    )(rows, own, weights, near)


def local(clip_features, enc_weight, noise_field, flow_times, embed_weight, time_weight, norm_gain, qkv_weight):
    _, frames, rows, width, depth_c = clip_features.shape
    chans = enc_weight.shape[4]
    patch, depth = embed_weight.shape
    peers, clips = lax.axis_size("seq"), lax.axis_size("clip")
    share = qkv_weight.shape[0]
    part = qkv_weight.shape[2]
    pixels = rows * width
    tokens = frames * pixels // 4

    gain, embed_cut, time_cut = norm_gain[None, :], embed_weight, time_weight
    if share % LANES:
        me = lax.axis_index("clip")
        gain, embed_cut, time_cut = (
            lax.dynamic_slice_in_dim(m, me * share, share, 1) for m in (gain, embed_weight, time_weight)
        )
    weight = qkv_weight.transpose(1, 0, 2)
    features = clip_features.reshape(frames, pixels, depth_c)
    enc = enc_weight.transpose(0, 1, 2, 4, 3).reshape(27 * chans, depth_c)
    noise = noise_field[0].transpose(0, 1, 3, 2)
    i, f, j = np.meshgrid(np.arange(rows // 2), np.arange(frames), np.arange(width // 2), indexing="ij")
    source = np.stack(
        [((f * rows + 2 * i + p) * width + 2 * j + q).reshape(-1) for p in range(2) for q in range(2)]
    ).reshape(1, -1)
    source = jnp.asarray(source.astype(np.int32))
    chunk = patch // clips
    dma = pltpu.SemaphoreType.DMA
    anywhere = pl.BlockSpec(memory_space=pl.ANY)
    edge = pltpu.VMEM((chans, frames * pixels), F32)
    x, x_own, weights, near = pl.pallas_call(
        functools.partial(front_kernel, (frames, width, chans, patch, peers, clips)),
        out_shape=(
            jax.ShapeDtypeStruct((peers * tokens, 2 * LANES), BF16),
            jax.ShapeDtypeStruct((2 * tokens, LANES), BF16),
            jax.ShapeDtypeStruct((peers - NEAR, patch + TAIL, 3 * part), BF16),
            jax.ShapeDtypeStruct((2, NEAR, tokens, part), BF16),
        ),
        in_specs=[pl.BlockSpec(memory_space=pltpu.SMEM), VMEM] + [anywhere] * 9,
        out_specs=(VMEM,) * 4,
        scratch_shapes=[
            pltpu.VMEM(features.shape, BF16), pltpu.VMEM(enc.shape, BF16), pltpu.VMEM((patch, share), BF16),
            pltpu.VMEM((1, share), F32), pltpu.VMEM(weight.shape, BF16), pltpu.VMEM((TFEAT, share), BF16),
            pltpu.VMEM(noise.shape, F32), pltpu.VMEM((LANES, depth), BF16), pltpu.VMEM(time_weight.shape, BF16),
            dma((11,)), pltpu.VMEM((8, TFEAT), F32),
            pltpu.VMEM((clips, 8, TFEAT), F32), dma((clips - 1,)), dma((clips - 1,)),
            edge, edge, edge, dma((2,)), dma((2,)),
            pltpu.VMEM((3, clips, chunk, part), BF16), pltpu.VMEM((3, clips - 1, chunk, part), BF16),
            pltpu.VMEM((clips, 2, 3 * part), F32), pltpu.VMEM((clips - 1, 2, 3 * part), F32),
            dma((3, clips - 1)), dma((3, clips - 1)), dma((clips - 1,)), dma((clips - 1,)),
            pltpu.VMEM((peers, tokens, LANES), BF16), dma((peers - 1,)), dma((peers - 1,)),
            pltpu.VMEM((2, clips // 2, peers, chunk, 3 * part), BF16), pltpu.VMEM((peers, 2, 3 * part), F32),
            dma((peers - 1,)), dma((peers - 1,)), dma((peers - 1,)), dma((peers - 1,)),
            dma((peers, clips // 2)), dma((peers, clips // 2)), dma((peers,)), dma((peers,)),
            pltpu.VMEM((NEAR, patch + TAIL, 3 * part), BF16),
        ],
        compiler_params=pltpu.CompilerParams(collective_id=0, has_side_effects=True),
        name="front",
    )(flow_times, source, features, enc, embed_cut, gain, weight, time_cut, noise, embed_weight, time_weight)
    output, output_t = attend(x, x_own, weights, near, peers * part)
    return output[None], output_t[None]


def solution(mesh):
    placed = (
        P("clip", None, "seq", None, None),
        P(),
        P("clip", None, "seq", None, None),
        P("clip", None),
        P(),
        P(),
        P(),
        P("clip", None, "seq"),
    )
    return jax.shard_map(
        local,
        mesh=mesh,
        in_specs=placed,
        out_specs=(P("clip", "seq", None), P("clip", "seq", None)),
        check_vma=False,
    )
```

```python
import functools

import jax
import jax.numpy as jnp
import numpy as np
from jax import lax
from jax.experimental import pallas as pl
from jax.experimental.pallas import tpu as pltpu
from jax.sharding import PartitionSpec as P

HD = 128
TFEAT = 256
TGRID = 1000
EPSILON = 1e-06
LANES = 128
TAIL = 16
NEAR = 1
LATE = (1,)
F32 = jnp.float32
BF16 = jnp.bfloat16


def split(value, parts):
    terms = []
    for _ in range(parts):
        term = value.astype(BF16)
        terms.append(term)
        value = value - term.astype(F32)
    return terms


def dot(a, b):
    return jnp.dot(a, b, preferred_element_type=F32)


def dot_nt(a, b):
    return lax.dot_general(a, b, (((1,), (1,)), ((), ())), preferred_element_type=F32)


def conv_part(features, weight, frames, width, chans):
    pixels = features.shape[1]
    taps = [dot_nt(weight[...], features[f]) for f in range(frames)]
    lane = lax.broadcasted_iota(jnp.int32, (chans, pixels), 1)
    column = lax.rem(lane, width)
    block = 9 * chans
    own, edge = [], []
    for f in range(frames):
        acc = taps[f][2 * block : 3 * block]
        if f >= 1:
            acc = acc + taps[f - 1][block : 2 * block]
        if f >= 2:
            acc = acc + taps[f - 2][:block]
        rows = []
        for b in range(3):
            part = [acc[(b * 3 + e) * chans : (b * 3 + e + 1) * chans] for e in range(3)]
            total = part[1]
            total = total + jnp.where(column > 0, pltpu.roll(part[0], 1, 1), 0.0)
            total = total + jnp.where(column < width - 1, pltpu.roll(part[2], pixels - 1, 1), 0.0)
            rows.append(total)
        down = pltpu.roll(rows[0], width, 1)
        up = pltpu.roll(rows[2], pixels - width, 1)
        here = rows[1] + jnp.where(lane >= width, down, 0.0)
        own.append(here + jnp.where(lane < pixels - width, up, 0.0))
        edge.append(jnp.where(lane < width, down, up))
    return jnp.concatenate(own, axis=1), jnp.concatenate(edge, axis=1)


def tokens_part(latent, noise, pick, flow_t, chans):
    tokens = pick.shape[1] // 4
    terms = split(latent, 3) + split(noise, 3)
    moved = dot(jnp.concatenate(terms, axis=0), pick)
    lat = moved[:chans] + moved[chans : 2 * chans] + moved[2 * chans : 3 * chans]
    noi = moved[3 * chans : 4 * chans] + moved[4 * chans : 5 * chans] + moved[5 * chans :]
    noisy = (1.0 - flow_t) * lat + flow_t * noi
    velocity = noi - lat
    stacked = jnp.concatenate(
        [noisy[:, k * tokens : (k + 1) * tokens] for k in range(4)]
        + [velocity[:, k * tokens : (k + 1) * tokens] for k in range(4)],
        axis=0,
    )
    flipped = stacked.T
    return flipped.astype(BF16)


def norm_part(raw, gram_pair, depth, patch):
    tokens = raw.shape[0]
    lane = lax.broadcasted_iota(jnp.int32, (tokens, LANES), 1)
    both = raw.astype(F32)
    noisy = jnp.where(lane < patch, both, 0.0)
    velocity = jnp.where(lane < patch, pltpu.roll(both, LANES - patch, 1), 0.0)
    ones = jnp.where((lane == patch) | (lane == patch + 1), 1.0, noisy)
    ones_t = jnp.where((lane == patch + 2) | (lane == patch + 3), 1.0, velocity)
    left = ones.astype(BF16)
    moved = dot(jnp.concatenate([left, left], axis=1), gram_pair)
    mean_sq = jnp.sum(moved * ones, axis=1, keepdims=True) / depth
    mean_cr = jnp.sum(moved * ones_t, axis=1, keepdims=True) / depth
    inv = lax.rsqrt(mean_sq + EPSILON)
    shift = -(inv * inv * inv) * mean_cr
    inv_hi, inv_lo = [v.astype(F32) for v in split(inv, 2)]
    sh_hi, sh_lo = [v.astype(F32) for v in split(shift, 2)]
    rows, rows_t = noisy * inv, velocity * inv + noisy * shift
    for index, column in enumerate([inv_hi, inv_lo, inv_hi]):
        rows = jnp.where(lane == patch + index, column, rows)
    for index, column in enumerate([sh_hi, sh_lo, sh_hi, inv_hi, inv_lo, inv_hi]):
        rows_t = jnp.where(lane == patch + index, column, rows_t)
    return rows.astype(BF16), rows_t.astype(BF16)


MESH = pl.DeviceIdType.MESH


def attend_heads(x_ref, own_ref, pieces, store):
    tokens = own_ref.shape[0] // 2
    fold = HD ** (-0.5) * np.log2(np.e).astype(np.float32)
    ln2 = np.log(2.0).astype(np.float32)
    zero = jnp.zeros((tokens, LANES), BF16)

    def tall(rows):
        return jnp.concatenate([rows, jnp.zeros((LANES - rows.shape[0], HD), BF16)], axis=0)

    inner = [(dot_nt(tall(q), tall(k)) * fold).astype(BF16) for q, k, _ in pieces]
    u = dot(own_ref[...], jnp.concatenate(inner, axis=1)).astype(BF16)
    ys = []
    for h in range(len(pieces)):
        at = slice(h * HD, (h + 1) * HD)
        left = jnp.concatenate(
            [jnp.concatenate([u[:tokens, at], zero], axis=1), jnp.concatenate([u[tokens:, at], u[:tokens, at]], axis=1)],
            axis=0,
        )
        both = dot_nt(left, x_ref[...])
        scores, score_t = both[:tokens], both[tokens:]
        expo = jnp.exp2(scores - jnp.max(scores, axis=1, keepdims=True))
        inv = 1.0 / jnp.sum(expo, axis=1, keepdims=True)
        mean = jnp.sum(expo * score_t, axis=1, keepdims=True) * inv
        left = jnp.concatenate([expo.astype(BF16), (expo * (score_t - mean)).astype(BF16)], axis=0)
        both = dot(left, x_ref[...])
        y = both[:tokens, :LANES] * inv
        yt = both[tokens:, :LANES] * (inv * ln2) + both[:tokens, LANES:] * inv
        ys.append(jnp.concatenate(split(jnp.concatenate([y, yt], axis=0), 2), axis=1))
    for h, (_, _, v) in enumerate(pieces):
        both = dot(ys[h], jnp.concatenate([tall(v), tall(v)], axis=0))
        store(h, both[:tokens].astype(BF16), both[tokens:].astype(BF16))


def pieces_of(m_ref, k):
    part = m_ref.shape[2] // 3
    cols = [slice(h * HD, (h + 1) * HD) for h in range(3 * part // HD)]
    per = part // HD
    return [[m_ref[k, :, cols[g * per + h]] for g in range(3)] for h in range(per)]


def flip(index, bits):
    place = 1
    while place <= bits:
        if bits & place:
            index = index + place - 2 * place * lax.rem(index // place, 2)
        place *= 2
    return index


def front_kernel(
    dims,
    flow_ref, source_ref, f_hbm, enc_hbm, ecut_hbm, gcut_hbm, w_hbm, tcut_hbm, noise_hbm, embed_hbm, time_hbm,
    x_hbm, own_hbm, m_hbm, near_hbm,
    f_ref, enc_ref, ecut_ref, gcut_ref, w_ref, tcut_ref, noise_ref, embed_ref, time_ref, load_sem, feats_ref,
    feats_buf, feats_send, feats_recv,
    edge_buf, before_buf, after_buf, edge_send, edge_recv,
    e_send, e_recv, tau_send, tau_recv, e_ss, e_rs, t_ss, t_rs,
    x_buf, x_ss, x_rs,
    g_buf, tau_buf, b_ss, b_rs, bt_ss, bt_rs, a_ss, a_rs, c_ss, c_rs, m_ref, x_out, x_own, m_out, near_out, out_sem,
    d_ss, d_rs,
):
    frames, width, chans, patch, peers, clips = dims
    seq, clip = lax.axis_index("seq"), lax.axis_index("clip")
    depth = embed_ref.shape[1]
    share = ecut_ref.shape[1]
    part = w_ref.shape[2]
    chunk = patch // clips
    on_seq = [{"seq": flip(seq, k)} for k in range(1, peers)]
    on_clip = [{"clip": flip(clip, k)} for k in range(1, clips)]
    mate = on_clip[0]
    core, chip = lax.rem(clip, 2), clip // 2

    barrier = pltpu.get_barrier_semaphore()
    for who in on_seq + on_clip:
        pl.semaphore_signal(barrier, inc=1, device_id=who, device_id_type=MESH)

    def cut(ref):
        if ref.shape[-1] == share:
            return ref
        return ref.at[:, pl.ds(pl.multiple_of(clip * share, share), share)]

    pairs = [(f_hbm, f_ref), (enc_hbm, enc_ref), (cut(ecut_hbm), ecut_ref), (cut(gcut_hbm), gcut_ref)]
    pairs += [(w_hbm.at[i], w_ref.at[i]) for i in range(3)]
    pairs += [
        (cut(tcut_hbm), tcut_ref), (noise_hbm, noise_ref), (embed_hbm, embed_ref.at[:patch]), (time_hbm, time_ref),
    ]
    loads = [pltpu.make_async_copy(src, dst, load_sem.at[k]) for k, (src, dst) in enumerate(pairs)]
    for load in loads:
        load.start()
    f_load, enc_load, ecut_load, gcut_load, w0, w1, w2, tcut_load, noise_load, embed_load, time_load = loads
    flow_r = flow_ref[0, 0].astype(F32) / TGRID
    flow_t = flow_ref[0, 1].astype(F32) / TGRID
    quarter = TFEAT // 4
    order = lax.broadcasted_iota(jnp.int32, (8, TFEAT), 1)
    line = lax.broadcasted_iota(jnp.int32, (8, TFEAT), 0)
    omega = 8.0 * jnp.exp(-np.float32(np.log(100.0)) * lax.rem(order, quarter).astype(F32) / quarter)
    angle = omega * jnp.where(order < 2 * quarter, flow_t, flow_t - flow_r)
    sine, cosine = jnp.sin(angle), jnp.cos(angle)
    first = lax.rem(order // quarter, 2) == 0
    feats_ref[...] = jnp.where(
        line == 0,
        jnp.where(first, sine, cosine),
        jnp.where(line == 1, jnp.where(first, omega * cosine, -omega * sine), 0.0),
    )
    sent = []

    def push(src, dst, ssem, rsem, who):
        copy = pltpu.make_async_remote_copy(
            src_ref=src, dst_ref=dst, send_sem=ssem, recv_sem=rsem, device_id=who, device_id_type=MESH
        )
        copy.start()
        sent.append(copy)
        return copy

    f_load.wait()
    enc_load.wait()
    own, edge = conv_part(f_ref, enc_ref, frames, width, chans)
    edge_buf[...] = edge

    @pl.when(seq == 0)
    def _():
        before_buf[...] = jnp.zeros_like(before_buf)

    @pl.when(seq == peers - 1)
    def _():
        after_buf[...] = jnp.zeros_like(after_buf)

    places = lax.broadcasted_iota(jnp.int32, (own.shape[1], source_ref.shape[1]), 0)
    pick = (places == source_ref[...]).astype(F32).astype(BF16)
    pl.semaphore_wait(barrier, len(on_seq) + len(on_clip))
    feats_in = [
        push(feats_ref, feats_buf.at[clip], feats_send.at[k], feats_recv.at[k], who) for k, who in enumerate(on_clip)
    ]
    feats_buf[clip] = feats_ref[...]

    def edge_copy(dst, k, step):
        return pltpu.make_async_remote_copy(
            src_ref=edge_buf, dst_ref=dst, send_sem=edge_send.at[k], recv_sem=edge_recv.at[k],
            device_id={"seq": lax.rem(seq + peers + step, peers)}, device_id_type=MESH,
        )

    to_next, to_last = edge_copy(before_buf, 0, 1), edge_copy(after_buf, 1, -1)

    @pl.when(seq < peers - 1)
    def _():
        to_next.start()

    @pl.when(seq > 0)
    def _():
        to_last.start()

    ecut_load.wait()
    gcut_load.wait()
    gain = gcut_ref[...]
    left = jnp.concatenate(split(ecut_ref[...].astype(F32) * gain, 2), axis=0)
    e_in = []
    for i, load in enumerate((w0, w1, w2)):
        load.wait()
        both = dot(left, w_ref[i])
        both = both[:patch] + both[patch:]
        for c in range(clips):
            e_send[i, c] = both[c * chunk : (c + 1) * chunk].astype(BF16)
        e_in.append([
            push(e_send.at[i, flip(clip, k + 1)], e_recv.at[i, k], e_ss.at[i, k], e_rs.at[i, k], who)
            for k, who in enumerate(on_clip)
        ])
    for copy in feats_in:
        copy.wait_recv()
    tcut_load.wait()
    feats = jnp.concatenate([feats_buf[c, :2] for c in range(clips)], axis=0)
    both = dot(jnp.concatenate(split(feats, 2), axis=0), tcut_ref[...])
    left = jnp.concatenate(split((both[: clips * 2] + both[clips * 2 :]) * gain, 2), axis=0)
    for i in range(3):
        both = dot(left, w_ref[i])
        both = both[: clips * 2] + both[clips * 2 :]
        for c in range(clips):
            tau_send[c, :, i * part : (i + 1) * part] = both[c * 2 : c * 2 + 2]
    tau_in = [
        push(tau_send.at[flip(clip, k + 1)], tau_recv.at[k], t_ss.at[k], t_rs.at[k], who)
        for k, who in enumerate(on_clip)
    ]

    @pl.when(seq > 0)
    def _():
        to_next.wait_recv()

    @pl.when(seq < peers - 1)
    def _():
        to_last.wait_recv()

    pixels = f_ref.shape[1]
    lane = lax.rem(lax.broadcasted_iota(jnp.int32, own.shape, 1), pixels)
    latent = own + jnp.where(lane < width, before_buf[...], 0.0)
    latent = latent + jnp.where(lane >= pixels - width, after_buf[...], 0.0)
    noise_load.wait()
    noise = jnp.concatenate(
        [noise_ref[f, r] for f in range(frames) for r in range(noise_ref.shape[1])], axis=1
    )
    x_buf[seq] = tokens_part(latent, noise, pick, flow_t, chans)
    x_in = [push(x_buf.at[seq], x_buf.at[seq], x_ss.at[k], x_rs.at[k], who) for k, who in enumerate(on_seq)]

    for i in range(3):
        for copy in e_in[i]:
            copy.wait_recv()
        total = e_send[i, clip].astype(F32)
        for k in range(clips - 1):
            total = total + e_recv[i, k].astype(F32)
        g_buf[core, chip, 0, :, i * part : (i + 1) * part] = total.astype(BF16)

    b_in = [
        push(g_buf.at[core, chip, 0], g_buf.at[core, chip, k + 1], b_ss.at[k], b_rs.at[k], who)
        for k, who in enumerate(on_seq)
    ]

    runs = [slice(k, k + 1) for k in range(peers)]
    a_in, c_in = [], []

    def spread(n):
        block = g_buf.at[core, chip, runs[n]]
        a_in.append([
            push(block, block, a_ss.at[n, j], a_rs.at[n, j], on_clip[2 * j + 1])
            for j in range(clips // 2 - 1 - (n in LATE))
        ])

    spread(0)
    time_load.wait()
    mine = jnp.concatenate(split(feats_ref[...], 2), axis=0)
    times = dot(mine, time_ref[...])
    times = times[:8] + times[8:]
    time_hi, time_lo = split(times, 2)
    filler = jnp.zeros((LANES - patch - 4, depth), BF16)
    rest = jnp.concatenate([time_hi[:1], time_lo[:1], time_hi[1:2], time_lo[1:2], filler], axis=0)
    embed_ref[patch:] = rest
    embed_load.wait()
    table = embed_ref[...]
    gram_pair = jnp.concatenate(split(dot_nt(table, table), 2), axis=0)

    for copy in tau_in:
        copy.wait_recv()
    total = tau_send[clip]
    for k in range(clips - 1):
        total = total + tau_recv[k]
    tau_buf[0] = total
    bt_in = [
        push(tau_buf.at[0], tau_buf.at[k + 1], bt_ss.at[k], bt_rs.at[k], who) for k, who in enumerate(on_seq)
    ]
    far = flip(chip, clips // 2 - 1)
    d_in = {}

    def relay(n):
        for copy in a_in[n]:
            copy.wait_recv()
        if n == 0:
            for k in LATE:
                d_in[k] = push(
                    g_buf.at[core, far, 0], g_buf.at[core, far, k], d_ss.at[k - 1], d_rs.at[k - 1], on_seq[k - 1]
                )
        if n in d_in:
            d_in[n].wait_recv()
        block = g_buf.at[core, :, runs[n]]
        c_in.append(push(block, block, c_ss.at[n], c_rs.at[n], mate))

    def finish(k, whole, slot):
        if k:
            bt_in[k - 1].wait_recv()
        for c in range(clips):
            whole[slot, c * chunk : (c + 1) * chunk] = g_buf[c % 2, c // 2, k]
        hi = tau_buf[k].astype(BF16).astype(F32)
        lo = tau_buf[k] - hi
        extra = [hi[0:1], hi[0:1], lo[0:1], hi[1:2], hi[1:2], lo[1:2]]
        row = lax.broadcasted_iota(jnp.int32, (TAIL, 3 * part), 0)
        tail = jnp.zeros((TAIL, 3 * part), F32)
        for index, value in enumerate(extra):
            tail = jnp.where(row == index, value, tail)
        whole[slot, patch:] = tail.astype(BF16)

    relay(0)
    for n, run in list(enumerate(runs))[1:]:
        for copy in b_in[run.start - 1 : run.stop - 1]:
            copy.wait_recv()
        spread(n)
    for copy in x_in:
        copy.wait_recv()
    tokens = x_buf.shape[1]
    for p in range(peers):
        rows, rows_t = norm_part(x_buf[p], gram_pair, depth, patch)
        x_out[p * tokens : (p + 1) * tokens, :LANES] = rows
        x_out[p * tokens : (p + 1) * tokens, LANES:] = rows_t
    x_own[:tokens] = x_out[pl.ds(pl.multiple_of(seq * tokens, tokens), tokens), :LANES]
    x_own[tokens:] = x_out[pl.ds(pl.multiple_of(seq * tokens, tokens), tokens), LANES:]
    stores = []

    def save(src, dst):
        stores.append(pltpu.make_async_copy(src, dst, out_sem.at[len(stores)]))
        stores[-1].start()

    save(x_out, x_hbm)
    save(x_own, own_hbm)
    c_in[0].wait_recv()
    for k in range(NEAR):
        finish(k, m_ref, k)

        def store(h, out, out_t):
            near_out[0, k, :, h * HD : (h + 1) * HD] = out
            near_out[1, k, :, h * HD : (h + 1) * HD] = out_t

        attend_heads(x_out, x_own, pieces_of(m_ref, k), store)
    for n in range(1, len(runs)):
        relay(n)
        if n == 1:
            save(near_out, near_hbm)
    for n, run in list(enumerate(runs))[1:]:
        c_in[n].wait_recv()
        for k in range(run.start, run.stop):
            finish(k, m_out, k - NEAR)
            save(m_out.at[k - NEAR], m_hbm.at[k - NEAR])
    for move in stores:
        move.wait()
    for copy in sent:
        copy.wait_send()

    @pl.when(seq < peers - 1)
    def _():
        to_next.wait_send()

    @pl.when(seq > 0)
    def _():
        to_last.wait_send()


def attend_kernel(x_ref, own_ref, m_ref, near_ref, out_hbm, out_t_hbm, far_ref, near_sem, far_sem):
    seq = lax.axis_index("seq")
    part = m_ref.shape[2] // 3
    per = part // HD
    outs = (out_hbm, out_t_hbm)

    def place(k):
        return pl.ds(pl.multiple_of(flip(seq, k) * part, part), part)

    moves = [
        pltpu.make_async_copy(near_ref.at[i, k], outs[i].at[:, place(k)], near_sem.at[i, k])
        for k in range(NEAR) for i in range(2)
    ]
    for move in moves:
        move.start()
    pieces = [piece for k in range(m_ref.shape[0]) for piece in pieces_of(m_ref, k)]

    def store(h, out, out_t):
        k, at = h // per, slice(h % per * HD, (h % per + 1) * HD)
        far_ref[0, k, :, at] = out
        far_ref[1, k, :, at] = out_t
        if h % per == per - 1:
            for i in range(2):
                moves.append(pltpu.make_async_copy(far_ref.at[i, k], outs[i].at[:, place(NEAR + k)], far_sem.at[i, k]))
                moves[-1].start()

    attend_heads(x_ref, own_ref, pieces, store)
    for move in moves:
        move.wait()


VMEM = pl.BlockSpec(memory_space=pltpu.VMEM)


def attend(rows, own, weights, near, inner):
    tokens, far, part = own.shape[0] // 2, weights.shape[0], weights.shape[2] // 3
    shape = jax.ShapeDtypeStruct((tokens, inner), BF16)
    anywhere = pl.BlockSpec(memory_space=pl.ANY)
    return pl.pallas_call(
        attend_kernel,
        out_shape=(shape, shape),
        in_specs=[VMEM, VMEM, VMEM, VMEM],
        out_specs=(anywhere, anywhere),
        scratch_shapes=[
            pltpu.VMEM((2, far, tokens, part), BF16),
            pltpu.SemaphoreType.DMA((2, NEAR)), pltpu.SemaphoreType.DMA((2, far)),
        ],
        name="attend",
    )(rows, own, weights, near)


def local(clip_features, enc_weight, noise_field, flow_times, embed_weight, time_weight, norm_gain, qkv_weight):
    _, frames, rows, width, depth_c = clip_features.shape
    chans = enc_weight.shape[4]
    patch, depth = embed_weight.shape
    peers, clips = lax.axis_size("seq"), lax.axis_size("clip")
    share = qkv_weight.shape[0]
    part = qkv_weight.shape[2]
    pixels = rows * width
    tokens = frames * pixels // 4

    gain, embed_cut, time_cut = norm_gain[None, :], embed_weight, time_weight
    if share % LANES:
        me = lax.axis_index("clip")
        gain, embed_cut, time_cut = (
            lax.dynamic_slice_in_dim(m, me * share, share, 1) for m in (gain, embed_weight, time_weight)
        )
    weight = qkv_weight.transpose(1, 0, 2)
    features = clip_features.reshape(frames, pixels, depth_c)
    enc = enc_weight.transpose(0, 1, 2, 4, 3).reshape(27 * chans, depth_c)
    noise = noise_field[0].transpose(0, 1, 3, 2)
    i, f, j = np.meshgrid(np.arange(rows // 2), np.arange(frames), np.arange(width // 2), indexing="ij")
    source = np.stack(
        [((f * rows + 2 * i + p) * width + 2 * j + q).reshape(-1) for p in range(2) for q in range(2)]
    ).reshape(1, -1)
    source = jnp.asarray(source.astype(np.int32))
    chunk = patch // clips
    dma = pltpu.SemaphoreType.DMA
    anywhere = pl.BlockSpec(memory_space=pl.ANY)
    edge = pltpu.VMEM((chans, frames * pixels), F32)
    x, x_own, weights, near = pl.pallas_call(
        functools.partial(front_kernel, (frames, width, chans, patch, peers, clips)),
        out_shape=(
            jax.ShapeDtypeStruct((peers * tokens, 2 * LANES), BF16),
            jax.ShapeDtypeStruct((2 * tokens, LANES), BF16),
            jax.ShapeDtypeStruct((peers - NEAR, patch + TAIL, 3 * part), BF16),
            jax.ShapeDtypeStruct((2, NEAR, tokens, part), BF16),
        ),
        in_specs=[pl.BlockSpec(memory_space=pltpu.SMEM), VMEM] + [anywhere] * 9,
        out_specs=(anywhere,) * 4,
        scratch_shapes=[
            pltpu.VMEM(features.shape, BF16), pltpu.VMEM(enc.shape, BF16), pltpu.VMEM((patch, share), BF16),
            pltpu.VMEM((1, share), F32), pltpu.VMEM(weight.shape, BF16), pltpu.VMEM((TFEAT, share), BF16),
            pltpu.VMEM(noise.shape, F32), pltpu.VMEM((LANES, depth), BF16), pltpu.VMEM(time_weight.shape, BF16),
            dma((11,)), pltpu.VMEM((8, TFEAT), F32),
            pltpu.VMEM((clips, 8, TFEAT), F32), dma((clips - 1,)), dma((clips - 1,)),
            edge, edge, edge, dma((2,)), dma((2,)),
            pltpu.VMEM((3, clips, chunk, part), BF16), pltpu.VMEM((3, clips - 1, chunk, part), BF16),
            pltpu.VMEM((clips, 2, 3 * part), F32), pltpu.VMEM((clips - 1, 2, 3 * part), F32),
            dma((3, clips - 1)), dma((3, clips - 1)), dma((clips - 1,)), dma((clips - 1,)),
            pltpu.VMEM((peers, tokens, LANES), BF16), dma((peers - 1,)), dma((peers - 1,)),
            pltpu.VMEM((2, clips // 2, peers, chunk, 3 * part), BF16), pltpu.VMEM((peers, 2, 3 * part), F32),
            dma((peers - 1,)), dma((peers - 1,)), dma((peers - 1,)), dma((peers - 1,)),
            dma((peers, clips // 2)), dma((peers, clips // 2)), dma((peers,)), dma((peers,)),
            pltpu.VMEM((NEAR, patch + TAIL, 3 * part), BF16), pltpu.VMEM((peers * tokens, 2 * LANES), BF16),
            pltpu.VMEM((2 * tokens, LANES), BF16), pltpu.VMEM((peers - NEAR, patch + TAIL, 3 * part), BF16),
            pltpu.VMEM((2, NEAR, tokens, part), BF16), dma((3 + peers - NEAR,)),
            dma((peers - 1,)), dma((peers - 1,)),
        ],
        compiler_params=pltpu.CompilerParams(collective_id=0, has_side_effects=True),
        name="front",
    )(flow_times, source, features, enc, embed_cut, gain, weight, time_cut, noise, embed_weight, time_weight)
    output, output_t = attend(x, x_own, weights, near, peers * part)
    return output[None], output_t[None]


def solution(mesh):
    placed = (
        P("clip", None, "seq", None, None),
        P(),
        P("clip", None, "seq", None, None),
        P("clip", None),
        P(),
        P(),
        P(),
        P("clip", None, "seq"),
    )
    return jax.shard_map(
        local,
        mesh=mesh,
        in_specs=placed,
        out_specs=(P("clip", "seq", None), P("clip", "seq", None)),
        check_vma=False,
    )
```

```python
import functools

import jax
import jax.numpy as jnp
import numpy as np
from jax import lax
from jax.experimental import pallas as pl
from jax.experimental.pallas import tpu as pltpu
from jax.sharding import PartitionSpec as P

HD = 128
TFEAT = 256
TGRID = 1000
EPSILON = 1e-06
LANES = 128
TAIL = 16
NEAR = 1
LATE = (1,)
F32 = jnp.float32
BF16 = jnp.bfloat16


def split(value, parts):
    terms = []
    for _ in range(parts):
        term = value.astype(BF16)
        terms.append(term)
        value = value - term.astype(F32)
    return terms


def dot(a, b):
    return jnp.dot(a, b, preferred_element_type=F32)


def dot_nt(a, b):
    return lax.dot_general(a, b, (((1,), (1,)), ((), ())), preferred_element_type=F32)


def conv_part(features, weight, frames, width, chans):
    pixels = features.shape[1]
    taps = [dot_nt(weight[...], features[f]) for f in range(frames)]
    lane = lax.broadcasted_iota(jnp.int32, (chans, pixels), 1)
    column = lax.rem(lane, width)
    block = 9 * chans
    own, edge = [], []
    for f in range(frames):
        acc = taps[f][2 * block : 3 * block]
        if f >= 1:
            acc = acc + taps[f - 1][block : 2 * block]
        if f >= 2:
            acc = acc + taps[f - 2][:block]
        rows = []
        for b in range(3):
            part = [acc[(b * 3 + e) * chans : (b * 3 + e + 1) * chans] for e in range(3)]
            total = part[1]
            total = total + jnp.where(column > 0, pltpu.roll(part[0], 1, 1), 0.0)
            total = total + jnp.where(column < width - 1, pltpu.roll(part[2], pixels - 1, 1), 0.0)
            rows.append(total)
        down = pltpu.roll(rows[0], width, 1)
        up = pltpu.roll(rows[2], pixels - width, 1)
        here = rows[1] + jnp.where(lane >= width, down, 0.0)
        own.append(here + jnp.where(lane < pixels - width, up, 0.0))
        edge.append(jnp.where(lane < width, down, up))
    return jnp.concatenate(own, axis=1), jnp.concatenate(edge, axis=1)


def tokens_part(latent, noise, pick, flow_t, chans):
    tokens = pick.shape[1] // 4
    terms = split(latent, 3) + split(noise, 3)
    moved = dot(jnp.concatenate(terms, axis=0), pick)
    lat = moved[:chans] + moved[chans : 2 * chans] + moved[2 * chans : 3 * chans]
    noi = moved[3 * chans : 4 * chans] + moved[4 * chans : 5 * chans] + moved[5 * chans :]
    noisy = (1.0 - flow_t) * lat + flow_t * noi
    velocity = noi - lat
    stacked = jnp.concatenate(
        [noisy[:, k * tokens : (k + 1) * tokens] for k in range(4)]
        + [velocity[:, k * tokens : (k + 1) * tokens] for k in range(4)],
        axis=0,
    )
    flipped = stacked.T
    return flipped.astype(BF16)


def norm_part(raw, gram_pair, depth, patch):
    tokens = raw.shape[0]
    lane = lax.broadcasted_iota(jnp.int32, (tokens, LANES), 1)
    both = raw.astype(F32)
    noisy = jnp.where(lane < patch, both, 0.0)
    velocity = jnp.where(lane < patch, pltpu.roll(both, LANES - patch, 1), 0.0)
    ones = jnp.where((lane == patch) | (lane == patch + 1), 1.0, noisy)
    ones_t = jnp.where((lane == patch + 2) | (lane == patch + 3), 1.0, velocity)
    left = ones.astype(BF16)
    moved = dot(jnp.concatenate([left, left], axis=1), gram_pair)
    mean_sq = jnp.sum(moved * ones, axis=1, keepdims=True) / depth
    mean_cr = jnp.sum(moved * ones_t, axis=1, keepdims=True) / depth
    inv = lax.rsqrt(mean_sq + EPSILON)
    shift = -(inv * inv * inv) * mean_cr
    inv_hi, inv_lo = [v.astype(F32) for v in split(inv, 2)]
    sh_hi, sh_lo = [v.astype(F32) for v in split(shift, 2)]
    rows, rows_t = noisy * inv, velocity * inv + noisy * shift
    for index, column in enumerate([inv_hi, inv_lo, inv_hi]):
        rows = jnp.where(lane == patch + index, column, rows)
    for index, column in enumerate([sh_hi, sh_lo, sh_hi, inv_hi, inv_lo, inv_hi]):
        rows_t = jnp.where(lane == patch + index, column, rows_t)
    return rows.astype(BF16), rows_t.astype(BF16)


MESH = pl.DeviceIdType.MESH


def attend_heads(x_ref, own_ref, pieces, store):
    tokens = own_ref.shape[0] // 2
    fold = HD ** (-0.5) * np.log2(np.e).astype(np.float32)
    ln2 = np.log(2.0).astype(np.float32)
    zero = jnp.zeros((tokens, LANES), BF16)

    def tall(rows):
        return jnp.concatenate([rows, jnp.zeros((LANES - rows.shape[0], HD), BF16)], axis=0)

    inner = [(dot_nt(tall(q), tall(k)) * fold).astype(BF16) for q, k, _ in pieces]
    u = dot(own_ref[...], jnp.concatenate(inner, axis=1)).astype(BF16)
    ys = []
    for start in range(0, len(pieces), 2):
        group = range(start, min(start + 2, len(pieces)))
        left = []
        for h in group:
            at = slice(h * HD, (h + 1) * HD)
            left.append(jnp.concatenate([u[:tokens, at], zero], axis=1))
            left.append(jnp.concatenate([u[tokens:, at], u[:tokens, at]], axis=1))
        both = dot_nt(jnp.concatenate(left, axis=0), x_ref[...])
        left, invs = [], []
        for g in range(len(group)):
            scores, score_t = both[2 * g * tokens : (2 * g + 1) * tokens], both[(2 * g + 1) * tokens : (2 * g + 2) * tokens]
            expo = jnp.exp2(scores - jnp.max(scores, axis=1, keepdims=True))
            inv = 1.0 / jnp.sum(expo, axis=1, keepdims=True)
            mean = jnp.sum(expo * score_t, axis=1, keepdims=True) * inv
            left += [expo.astype(BF16), (expo * (score_t - mean)).astype(BF16)]
            invs.append(inv)
        both = dot(jnp.concatenate(left, axis=0), x_ref[...])
        for g, inv in enumerate(invs):
            p, pt = both[2 * g * tokens : (2 * g + 1) * tokens], both[(2 * g + 1) * tokens : (2 * g + 2) * tokens]
            y = p[:, :LANES] * inv
            yt = pt[:, :LANES] * (inv * ln2) + p[:, LANES:] * inv
            ys.append(jnp.concatenate(split(jnp.concatenate([y, yt], axis=0), 2), axis=1))
    for h, (_, _, v) in enumerate(pieces):
        both = dot(ys[h], jnp.concatenate([tall(v), tall(v)], axis=0))
        store(h, both[:tokens].astype(BF16), both[tokens:].astype(BF16))


def pieces_of(m_ref, k):
    part = m_ref.shape[2] // 3
    cols = [slice(h * HD, (h + 1) * HD) for h in range(3 * part // HD)]
    per = part // HD
    return [[m_ref[k, :, cols[g * per + h]] for g in range(3)] for h in range(per)]


def flip(index, bits):
    place = 1
    while place <= bits:
        if bits & place:
            index = index + place - 2 * place * lax.rem(index // place, 2)
        place *= 2
    return index


def front_kernel(
    dims,
    flow_ref, source_ref, f_hbm, enc_hbm, ecut_hbm, gcut_hbm, w_hbm, tcut_hbm, noise_hbm, embed_hbm, time_hbm,
    x_hbm, own_hbm, m_hbm, near_hbm,
    f_ref, enc_ref, ecut_ref, gcut_ref, w_ref, tcut_ref, noise_ref, embed_ref, time_ref, load_sem, feats_ref,
    feats_buf, feats_send, feats_recv,
    edge_buf, before_buf, after_buf, edge_send, edge_recv,
    e_send, e_recv, tau_send, tau_recv, e_ss, e_rs, t_ss, t_rs,
    x_buf, x_ss, x_rs,
    g_buf, tau_buf, b_ss, b_rs, bt_ss, bt_rs, a_ss, a_rs, c_ss, c_rs, m_ref, x_out, x_own, m_out, near_out, out_sem,
    d_ss, d_rs,
):
    frames, width, chans, patch, peers, clips = dims
    seq, clip = lax.axis_index("seq"), lax.axis_index("clip")
    depth = embed_ref.shape[1]
    share = ecut_ref.shape[1]
    part = w_ref.shape[2]
    chunk = patch // clips
    on_seq = [{"seq": flip(seq, k)} for k in range(1, peers)]
    on_clip = [{"clip": flip(clip, k)} for k in range(1, clips)]
    mate = on_clip[0]
    core, chip = lax.rem(clip, 2), clip // 2

    barrier = pltpu.get_barrier_semaphore()
    for who in on_seq + on_clip:
        pl.semaphore_signal(barrier, inc=1, device_id=who, device_id_type=MESH)

    def cut(ref):
        if ref.shape[-1] == share:
            return ref
        return ref.at[:, pl.ds(pl.multiple_of(clip * share, share), share)]

    pairs = [(f_hbm, f_ref), (enc_hbm, enc_ref), (cut(ecut_hbm), ecut_ref), (cut(gcut_hbm), gcut_ref)]
    pairs += [(w_hbm.at[i], w_ref.at[i]) for i in range(3)]
    pairs += [
        (cut(tcut_hbm), tcut_ref), (noise_hbm, noise_ref), (embed_hbm, embed_ref.at[:patch]), (time_hbm, time_ref),
    ]
    loads = [pltpu.make_async_copy(src, dst, load_sem.at[k]) for k, (src, dst) in enumerate(pairs)]
    for load in loads:
        load.start()
    f_load, enc_load, ecut_load, gcut_load, w0, w1, w2, tcut_load, noise_load, embed_load, time_load = loads
    flow_r = flow_ref[0, 0].astype(F32) / TGRID
    flow_t = flow_ref[0, 1].astype(F32) / TGRID
    quarter = TFEAT // 4
    order = lax.broadcasted_iota(jnp.int32, (8, TFEAT), 1)
    line = lax.broadcasted_iota(jnp.int32, (8, TFEAT), 0)
    omega = 8.0 * jnp.exp(-np.float32(np.log(100.0)) * lax.rem(order, quarter).astype(F32) / quarter)
    angle = omega * jnp.where(order < 2 * quarter, flow_t, flow_t - flow_r)
    sine, cosine = jnp.sin(angle), jnp.cos(angle)
    first = lax.rem(order // quarter, 2) == 0
    feats_ref[...] = jnp.where(
        line == 0,
        jnp.where(first, sine, cosine),
        jnp.where(line == 1, jnp.where(first, omega * cosine, -omega * sine), 0.0),
    )
    sent = []

    def push(src, dst, ssem, rsem, who):
        copy = pltpu.make_async_remote_copy(
            src_ref=src, dst_ref=dst, send_sem=ssem, recv_sem=rsem, device_id=who, device_id_type=MESH
        )
        copy.start()
        sent.append(copy)
        return copy

    f_load.wait()
    enc_load.wait()
    own, edge = conv_part(f_ref, enc_ref, frames, width, chans)
    edge_buf[...] = edge

    @pl.when(seq == 0)
    def _():
        before_buf[...] = jnp.zeros_like(before_buf)

    @pl.when(seq == peers - 1)
    def _():
        after_buf[...] = jnp.zeros_like(after_buf)

    places = lax.broadcasted_iota(jnp.int32, (own.shape[1], source_ref.shape[1]), 0)
    pick = (places == source_ref[...]).astype(F32).astype(BF16)
    pl.semaphore_wait(barrier, len(on_seq) + len(on_clip))
    feats_in = [
        push(feats_ref, feats_buf.at[clip], feats_send.at[k], feats_recv.at[k], who) for k, who in enumerate(on_clip)
    ]
    feats_buf[clip] = feats_ref[...]

    def edge_copy(dst, k, step):
        return pltpu.make_async_remote_copy(
            src_ref=edge_buf, dst_ref=dst, send_sem=edge_send.at[k], recv_sem=edge_recv.at[k],
            device_id={"seq": lax.rem(seq + peers + step, peers)}, device_id_type=MESH,
        )

    to_next, to_last = edge_copy(before_buf, 0, 1), edge_copy(after_buf, 1, -1)

    @pl.when(seq < peers - 1)
    def _():
        to_next.start()

    @pl.when(seq > 0)
    def _():
        to_last.start()

    ecut_load.wait()
    gcut_load.wait()
    gain = gcut_ref[...]
    left = jnp.concatenate(split(ecut_ref[...].astype(F32) * gain, 2), axis=0)
    e_in = []
    for i, load in enumerate((w0, w1, w2)):
        load.wait()
        both = dot(left, w_ref[i])
        both = both[:patch] + both[patch:]
        for c in range(clips):
            e_send[i, c] = both[c * chunk : (c + 1) * chunk].astype(BF16)
        e_in.append([
            push(e_send.at[i, flip(clip, k + 1)], e_recv.at[i, k], e_ss.at[i, k], e_rs.at[i, k], who)
            for k, who in enumerate(on_clip)
        ])
    for copy in feats_in:
        copy.wait_recv()
    tcut_load.wait()
    feats = jnp.concatenate([feats_buf[c, :2] for c in range(clips)], axis=0)
    both = dot(jnp.concatenate(split(feats, 2), axis=0), tcut_ref[...])
    left = jnp.concatenate(split((both[: clips * 2] + both[clips * 2 :]) * gain, 2), axis=0)
    for i in range(3):
        both = dot(left, w_ref[i])
        both = both[: clips * 2] + both[clips * 2 :]
        for c in range(clips):
            tau_send[c, :, i * part : (i + 1) * part] = both[c * 2 : c * 2 + 2]
    tau_in = [
        push(tau_send.at[flip(clip, k + 1)], tau_recv.at[k], t_ss.at[k], t_rs.at[k], who)
        for k, who in enumerate(on_clip)
    ]

    @pl.when(seq > 0)
    def _():
        to_next.wait_recv()

    @pl.when(seq < peers - 1)
    def _():
        to_last.wait_recv()

    pixels = f_ref.shape[1]
    lane = lax.rem(lax.broadcasted_iota(jnp.int32, own.shape, 1), pixels)
    latent = own + jnp.where(lane < width, before_buf[...], 0.0)
    latent = latent + jnp.where(lane >= pixels - width, after_buf[...], 0.0)
    noise_load.wait()
    noise = jnp.concatenate(
        [noise_ref[f, r] for f in range(frames) for r in range(noise_ref.shape[1])], axis=1
    )
    x_buf[seq] = tokens_part(latent, noise, pick, flow_t, chans)
    x_in = [push(x_buf.at[seq], x_buf.at[seq], x_ss.at[k], x_rs.at[k], who) for k, who in enumerate(on_seq)]

    for i in range(3):
        for copy in e_in[i]:
            copy.wait_recv()
        total = e_send[i, clip].astype(F32)
        for k in range(clips - 1):
            total = total + e_recv[i, k].astype(F32)
        g_buf[core, chip, 0, :, i * part : (i + 1) * part] = total.astype(BF16)

    b_in = [
        push(g_buf.at[core, chip, 0], g_buf.at[core, chip, k + 1], b_ss.at[k], b_rs.at[k], who)
        for k, who in enumerate(on_seq)
    ]

    runs = [slice(k, k + 1) for k in range(peers)]
    a_in, c_in = [], []

    def spread(n):
        block = g_buf.at[core, chip, runs[n]]
        a_in.append([
            push(block, block, a_ss.at[n, j], a_rs.at[n, j], on_clip[2 * j + 1])
            for j in range(clips // 2 - 1 - (n in LATE))
        ])

    spread(0)
    time_load.wait()
    mine = jnp.concatenate(split(feats_ref[...], 2), axis=0)
    times = dot(mine, time_ref[...])
    times = times[:8] + times[8:]
    time_hi, time_lo = split(times, 2)
    filler = jnp.zeros((LANES - patch - 4, depth), BF16)
    rest = jnp.concatenate([time_hi[:1], time_lo[:1], time_hi[1:2], time_lo[1:2], filler], axis=0)
    embed_ref[patch:] = rest
    embed_load.wait()
    table = embed_ref[...]
    gram_pair = jnp.concatenate(split(dot_nt(table, table), 2), axis=0)

    for copy in tau_in:
        copy.wait_recv()
    total = tau_send[clip]
    for k in range(clips - 1):
        total = total + tau_recv[k]
    tau_buf[0] = total
    bt_in = [
        push(tau_buf.at[0], tau_buf.at[k + 1], bt_ss.at[k], bt_rs.at[k], who) for k, who in enumerate(on_seq)
    ]
    far = flip(chip, clips // 2 - 1)
    d_in = {}

    def relay(n):
        for copy in a_in[n]:
            copy.wait_recv()
        if n == 0:
            for k in LATE:
                d_in[k] = push(
                    g_buf.at[core, far, 0], g_buf.at[core, far, k], d_ss.at[k - 1], d_rs.at[k - 1], on_seq[k - 1]
                )
        if n in d_in:
            d_in[n].wait_recv()
        block = g_buf.at[core, :, runs[n]]
        c_in.append(push(block, block, c_ss.at[n], c_rs.at[n], mate))

    def finish(k, whole, slot):
        if k:
            bt_in[k - 1].wait_recv()
        for c in range(clips):
            whole[slot, c * chunk : (c + 1) * chunk] = g_buf[c % 2, c // 2, k]
        hi = tau_buf[k].astype(BF16).astype(F32)
        lo = tau_buf[k] - hi
        extra = [hi[0:1], hi[0:1], lo[0:1], hi[1:2], hi[1:2], lo[1:2]]
        row = lax.broadcasted_iota(jnp.int32, (TAIL, 3 * part), 0)
        tail = jnp.zeros((TAIL, 3 * part), F32)
        for index, value in enumerate(extra):
            tail = jnp.where(row == index, value, tail)
        whole[slot, patch:] = tail.astype(BF16)

    relay(0)
    for n, run in list(enumerate(runs))[1:]:
        for copy in b_in[run.start - 1 : run.stop - 1]:
            copy.wait_recv()
        spread(n)
    for copy in x_in:
        copy.wait_recv()
    tokens = x_buf.shape[1]
    for p in range(peers):
        rows, rows_t = norm_part(x_buf[p], gram_pair, depth, patch)
        x_out[p * tokens : (p + 1) * tokens, :LANES] = rows
        x_out[p * tokens : (p + 1) * tokens, LANES:] = rows_t
    x_own[:tokens] = x_out[pl.ds(pl.multiple_of(seq * tokens, tokens), tokens), :LANES]
    x_own[tokens:] = x_out[pl.ds(pl.multiple_of(seq * tokens, tokens), tokens), LANES:]
    stores = []

    def save(src, dst):
        stores.append(pltpu.make_async_copy(src, dst, out_sem.at[len(stores)]))
        stores[-1].start()

    save(x_out, x_hbm)
    save(x_own, own_hbm)
    def near_part(k):
        c_in[k].wait_recv()
        finish(k, m_ref, k)

        def store(h, out, out_t):
            near_out[0, k, :, h * HD : (h + 1) * HD] = out
            near_out[1, k, :, h * HD : (h + 1) * HD] = out_t

        attend_heads(x_out, x_own, pieces_of(m_ref, k), store)
        save(near_out.at[:, k], near_hbm.at[:, k])

    def far_part(k):
        c_in[k].wait_recv()
        finish(k, m_out, k - NEAR)
        save(m_out.at[k - NEAR], m_hbm.at[k - NEAR])

    near_part(0)
    for k in range(1, peers):
        relay(k)
    for k in range(1, peers):
        far_part(k)
    for move in stores:
        move.wait()
    for copy in sent:
        copy.wait_send()

    @pl.when(seq < peers - 1)
    def _():
        to_next.wait_send()

    @pl.when(seq > 0)
    def _():
        to_last.wait_send()


def attend_kernel(x_ref, own_ref, m_ref, near_ref, out_hbm, out_t_hbm, far_ref, near_sem, far_sem):
    seq = lax.axis_index("seq")
    part = m_ref.shape[2] // 3
    per = part // HD
    outs = (out_hbm, out_t_hbm)

    def place(k):
        return pl.ds(pl.multiple_of(flip(seq, k) * part, part), part)

    moves = [
        pltpu.make_async_copy(near_ref.at[i, k], outs[i].at[:, place(k)], near_sem.at[i, k])
        for k in range(NEAR) for i in range(2)
    ]
    for move in moves:
        move.start()
    pieces = [piece for k in range(m_ref.shape[0]) for piece in pieces_of(m_ref, k)]

    def store(h, out, out_t):
        k, at = h // per, slice(h % per * HD, (h % per + 1) * HD)
        far_ref[0, k, :, at] = out
        far_ref[1, k, :, at] = out_t
        if h % per == per - 1:
            for i in range(2):
                moves.append(pltpu.make_async_copy(far_ref.at[i, k], outs[i].at[:, place(NEAR + k)], far_sem.at[i, k]))
                moves[-1].start()

    attend_heads(x_ref, own_ref, pieces, store)
    for move in moves:
        move.wait()


VMEM = pl.BlockSpec(memory_space=pltpu.VMEM)


def attend(rows, own, weights, near, inner):
    tokens, far, part = own.shape[0] // 2, weights.shape[0], weights.shape[2] // 3
    shape = jax.ShapeDtypeStruct((tokens, inner), BF16)
    anywhere = pl.BlockSpec(memory_space=pl.ANY)
    return pl.pallas_call(
        attend_kernel,
        out_shape=(shape, shape),
        in_specs=[VMEM, VMEM, VMEM, VMEM],
        out_specs=(anywhere, anywhere),
        scratch_shapes=[
            pltpu.VMEM((2, far, tokens, part), BF16),
            pltpu.SemaphoreType.DMA((2, NEAR)), pltpu.SemaphoreType.DMA((2, far)),
        ],
        name="attend",
    )(rows, own, weights, near)


def local(clip_features, enc_weight, noise_field, flow_times, embed_weight, time_weight, norm_gain, qkv_weight):
    _, frames, rows, width, depth_c = clip_features.shape
    chans = enc_weight.shape[4]
    patch, depth = embed_weight.shape
    peers, clips = lax.axis_size("seq"), lax.axis_size("clip")
    share = qkv_weight.shape[0]
    part = qkv_weight.shape[2]
    pixels = rows * width
    tokens = frames * pixels // 4

    gain, embed_cut, time_cut = norm_gain[None, :], embed_weight, time_weight
    if share % LANES:
        me = lax.axis_index("clip")
        gain, embed_cut, time_cut = (
            lax.dynamic_slice_in_dim(m, me * share, share, 1) for m in (gain, embed_weight, time_weight)
        )
    weight = qkv_weight.transpose(1, 0, 2)
    features = clip_features.reshape(frames, pixels, depth_c)
    enc = enc_weight.transpose(0, 1, 2, 4, 3).reshape(27 * chans, depth_c)
    noise = noise_field[0].transpose(0, 1, 3, 2)
    i, f, j = np.meshgrid(np.arange(rows // 2), np.arange(frames), np.arange(width // 2), indexing="ij")
    source = np.stack(
        [((f * rows + 2 * i + p) * width + 2 * j + q).reshape(-1) for p in range(2) for q in range(2)]
    ).reshape(1, -1)
    source = jnp.asarray(source.astype(np.int32))
    chunk = patch // clips
    dma = pltpu.SemaphoreType.DMA
    anywhere = pl.BlockSpec(memory_space=pl.ANY)
    edge = pltpu.VMEM((chans, frames * pixels), F32)
    x, x_own, weights, near = pl.pallas_call(
        functools.partial(front_kernel, (frames, width, chans, patch, peers, clips)),
        out_shape=(
            jax.ShapeDtypeStruct((peers * tokens, 2 * LANES), BF16),
            jax.ShapeDtypeStruct((2 * tokens, LANES), BF16),
            jax.ShapeDtypeStruct((peers - NEAR, patch + TAIL, 3 * part), BF16),
            jax.ShapeDtypeStruct((2, NEAR, tokens, part), BF16),
        ),
        in_specs=[pl.BlockSpec(memory_space=pltpu.SMEM), VMEM] + [anywhere] * 9,
        out_specs=(anywhere,) * 4,
        scratch_shapes=[
            pltpu.VMEM(features.shape, BF16), pltpu.VMEM(enc.shape, BF16), pltpu.VMEM((patch, share), BF16),
            pltpu.VMEM((1, share), F32), pltpu.VMEM(weight.shape, BF16), pltpu.VMEM((TFEAT, share), BF16),
            pltpu.VMEM(noise.shape, F32), pltpu.VMEM((LANES, depth), BF16), pltpu.VMEM(time_weight.shape, BF16),
            dma((11,)), pltpu.VMEM((8, TFEAT), F32),
            pltpu.VMEM((clips, 8, TFEAT), F32), dma((clips - 1,)), dma((clips - 1,)),
            edge, edge, edge, dma((2,)), dma((2,)),
            pltpu.VMEM((3, clips, chunk, part), BF16), pltpu.VMEM((3, clips - 1, chunk, part), BF16),
            pltpu.VMEM((clips, 2, 3 * part), F32), pltpu.VMEM((clips - 1, 2, 3 * part), F32),
            dma((3, clips - 1)), dma((3, clips - 1)), dma((clips - 1,)), dma((clips - 1,)),
            pltpu.VMEM((peers, tokens, LANES), BF16), dma((peers - 1,)), dma((peers - 1,)),
            pltpu.VMEM((2, clips // 2, peers, chunk, 3 * part), BF16), pltpu.VMEM((peers, 2, 3 * part), F32),
            dma((peers - 1,)), dma((peers - 1,)), dma((peers - 1,)), dma((peers - 1,)),
            dma((peers, clips // 2)), dma((peers, clips // 2)), dma((peers,)), dma((peers,)),
            pltpu.VMEM((NEAR, patch + TAIL, 3 * part), BF16), pltpu.VMEM((peers * tokens, 2 * LANES), BF16),
            pltpu.VMEM((2 * tokens, LANES), BF16), pltpu.VMEM((peers - NEAR, patch + TAIL, 3 * part), BF16),
            pltpu.VMEM((2, NEAR, tokens, part), BF16), dma((2 + peers,)),
            dma((peers - 1,)), dma((peers - 1,)),
        ],
        compiler_params=pltpu.CompilerParams(collective_id=0, has_side_effects=True),
        name="front",
    )(flow_times, source, features, enc, embed_cut, gain, weight, time_cut, noise, embed_weight, time_weight)
    output, output_t = attend(x, x_own, weights, near, peers * part)
    return output[None], output_t[None]


def solution(mesh):
    placed = (
        P("clip", None, "seq", None, None),
        P(),
        P("clip", None, "seq", None, None),
        P("clip", None),
        P(),
        P(),
        P(),
        P("clip", None, "seq"),
    )
    return jax.shard_map(
        local,
        mesh=mesh,
        in_specs=placed,
        out_specs=(P("clip", "seq", None), P("clip", "seq", None)),
        check_vma=False,
    )
```

```python
import functools

import jax
import jax.numpy as jnp
import numpy as np
from jax import lax
from jax.experimental import pallas as pl
from jax.experimental.pallas import tpu as pltpu
from jax.sharding import PartitionSpec as P

HD = 128
TFEAT = 256
TGRID = 1000
EPSILON = 1e-06
LANES = 128
TAIL = 16
NEAR = 1
LATE = (1,)
F32 = jnp.float32
BF16 = jnp.bfloat16


def split(value, parts):
    terms = []
    for _ in range(parts):
        term = value.astype(BF16)
        terms.append(term)
        value = value - term.astype(F32)
    return terms


def dot(a, b):
    return jnp.dot(a, b, preferred_element_type=F32)


def dot_nt(a, b):
    return lax.dot_general(a, b, (((1,), (1,)), ((), ())), preferred_element_type=F32)


def conv_part(features, weight, frames, width, chans):
    pixels = features.shape[1]
    taps = [dot_nt(weight[...], features[f]) for f in range(frames)]
    lane = lax.broadcasted_iota(jnp.int32, (chans, pixels), 1)
    column = lax.rem(lane, width)
    block = 9 * chans
    own, edge = [], []
    for f in range(frames):
        acc = taps[f][2 * block : 3 * block]
        if f >= 1:
            acc = acc + taps[f - 1][block : 2 * block]
        if f >= 2:
            acc = acc + taps[f - 2][:block]
        rows = []
        for b in range(3):
            part = [acc[(b * 3 + e) * chans : (b * 3 + e + 1) * chans] for e in range(3)]
            total = part[1]
            total = total + jnp.where(column > 0, pltpu.roll(part[0], 1, 1), 0.0)
            total = total + jnp.where(column < width - 1, pltpu.roll(part[2], pixels - 1, 1), 0.0)
            rows.append(total)
        down = pltpu.roll(rows[0], width, 1)
        up = pltpu.roll(rows[2], pixels - width, 1)
        here = rows[1] + jnp.where(lane >= width, down, 0.0)
        own.append(here + jnp.where(lane < pixels - width, up, 0.0))
        edge.append(jnp.where(lane < width, down, up))
    return jnp.concatenate(own, axis=1), jnp.concatenate(edge, axis=1)


def tokens_part(latent, edge, noise, pick, flow_t, chans):
    tokens = pick.shape[1] // 4
    terms = split(latent, 3) + split(noise, 3) + split(edge, 2)
    moved = dot(jnp.concatenate(terms, axis=0), pick)
    part = [moved[k * chans : (k + 1) * chans] for k in range(8)]
    lat, noi, rim = part[0] + part[1] + part[2], part[3] + part[4] + part[5], part[6] + part[7]
    noisy = (1.0 - flow_t) * lat + flow_t * noi
    velocity = noi - lat

    def flipped(*values):
        return jnp.concatenate([v[:, k * tokens : (k + 1) * tokens] for v in values for k in range(4)], axis=0).T

    rim = flipped(rim, jnp.zeros_like(rim))
    rim = rim[: tokens // 2] + pltpu.roll(rim[tokens // 2 :], 4 * chans, 1)
    return jnp.concatenate([flipped(noisy, velocity), rim], axis=0).astype(BF16)


def rim_of(block, tokens):
    rim = block[tokens:].astype(F32)
    return jnp.concatenate([rim, pltpu.roll(rim, LANES // 2, 1)], axis=0)


def joined(x_buf, p, flow_t, patch):
    tokens = x_buf.shape[1] * 2 // 3
    lane = lax.broadcasted_iota(jnp.int32, (tokens, LANES), 1)
    extra = jnp.zeros((tokens, LANES), F32)
    if p > 0:
        extra = jnp.where(lane < patch // 2, rim_of(x_buf[p - 1], tokens), extra)
    if p + 1 < x_buf.shape[0]:
        extra = jnp.where((lane >= patch // 2) & (lane < patch), rim_of(x_buf[p + 1], tokens), extra)
    return x_buf[p, :tokens].astype(F32) + (1.0 - flow_t) * extra - pltpu.roll(extra, patch, 1)


def norm_part(raw, gram_pair, depth, patch):
    tokens = raw.shape[0]
    lane = lax.broadcasted_iota(jnp.int32, (tokens, LANES), 1)
    noisy = jnp.where(lane < patch, raw, 0.0)
    velocity = jnp.where(lane < patch, pltpu.roll(raw, LANES - patch, 1), 0.0)
    ones = jnp.where((lane == patch) | (lane == patch + 1), 1.0, noisy)
    ones_t = jnp.where((lane == patch + 2) | (lane == patch + 3), 1.0, velocity)
    left = ones.astype(BF16)
    moved = dot(jnp.concatenate([left, left], axis=1), gram_pair)
    mean_sq = jnp.sum(moved * ones, axis=1, keepdims=True) / depth
    mean_cr = jnp.sum(moved * ones_t, axis=1, keepdims=True) / depth
    inv = lax.rsqrt(mean_sq + EPSILON)
    shift = -(inv * inv * inv) * mean_cr
    inv_hi, inv_lo = [v.astype(F32) for v in split(inv, 2)]
    sh_hi, sh_lo = [v.astype(F32) for v in split(shift, 2)]
    rows, rows_t = noisy * inv, velocity * inv + noisy * shift
    for index, column in enumerate([inv_hi, inv_lo, inv_hi]):
        rows = jnp.where(lane == patch + index, column, rows)
    for index, column in enumerate([sh_hi, sh_lo, sh_hi, inv_hi, inv_lo, inv_hi]):
        rows_t = jnp.where(lane == patch + index, column, rows_t)
    return rows.astype(BF16), rows_t.astype(BF16)


MESH = pl.DeviceIdType.MESH


def attend_heads(x_ref, own_ref, pieces, store):
    tokens = own_ref.shape[0] // 2
    fold = HD ** (-0.5) * np.log2(np.e).astype(np.float32)
    ln2 = np.log(2.0).astype(np.float32)
    zero = jnp.zeros((tokens, LANES), BF16)

    def tall(rows):
        return jnp.concatenate([rows, jnp.zeros((LANES - rows.shape[0], HD), BF16)], axis=0)

    inner = [(dot_nt(tall(q), tall(k)) * fold).astype(BF16) for q, k, _ in pieces]
    u = dot(own_ref[...], jnp.concatenate(inner, axis=1)).astype(BF16)
    ys = []
    for start in range(0, len(pieces), 2):
        group = range(start, min(start + 2, len(pieces)))
        left = []
        for h in group:
            at = slice(h * HD, (h + 1) * HD)
            left.append(jnp.concatenate([u[:tokens, at], zero], axis=1))
            left.append(jnp.concatenate([u[tokens:, at], u[:tokens, at]], axis=1))
        both = dot_nt(jnp.concatenate(left, axis=0), x_ref[...])
        left, invs = [], []
        for g in range(len(group)):
            scores, score_t = both[2 * g * tokens : (2 * g + 1) * tokens], both[(2 * g + 1) * tokens : (2 * g + 2) * tokens]
            expo = jnp.exp2(scores - jnp.max(scores, axis=1, keepdims=True))
            inv = 1.0 / jnp.sum(expo, axis=1, keepdims=True)
            mean = jnp.sum(expo * score_t, axis=1, keepdims=True) * inv
            left += [expo.astype(BF16), (expo * (score_t - mean)).astype(BF16)]
            invs.append(inv)
        both = dot(jnp.concatenate(left, axis=0), x_ref[...])
        for g, inv in enumerate(invs):
            p, pt = both[2 * g * tokens : (2 * g + 1) * tokens], both[(2 * g + 1) * tokens : (2 * g + 2) * tokens]
            y = p[:, :LANES] * inv
            yt = pt[:, :LANES] * (inv * ln2) + p[:, LANES:] * inv
            ys.append(jnp.concatenate(split(jnp.concatenate([y, yt], axis=0), 2), axis=1))
    for h, (_, _, v) in enumerate(pieces):
        both = dot(ys[h], jnp.concatenate([tall(v), tall(v)], axis=0))
        store(h, both[:tokens].astype(BF16), both[tokens:].astype(BF16))


def pieces_of(m_ref, k):
    part = m_ref.shape[2] // 3
    cols = [slice(h * HD, (h + 1) * HD) for h in range(3 * part // HD)]
    per = part // HD
    return [[m_ref[k, :, cols[g * per + h]] for g in range(3)] for h in range(per)]


def flip(index, bits):
    place = 1
    while place <= bits:
        if bits & place:
            index = index + place - 2 * place * lax.rem(index // place, 2)
        place *= 2
    return index


def front_kernel(
    dims,
    flow_ref, source_ref, f_hbm, enc_hbm, ecut_hbm, gcut_hbm, w_hbm, tcut_hbm, noise_hbm, embed_hbm, time_hbm,
    x_hbm, own_hbm, m_hbm, near_hbm,
    f_ref, enc_ref, ecut_ref, gcut_ref, w_ref, tcut_ref, noise_ref, embed_ref, time_ref, load_sem, feats_ref,
    feats_buf, feats_send, feats_recv,
    e_send, e_recv, tau_send, tau_recv, e_ss, e_rs, t_ss, t_rs,
    x_buf, x_ss, x_rs,
    g_buf, tau_buf, b_ss, b_rs, bt_ss, bt_rs, a_ss, a_rs, c_ss, c_rs, m_ref, x_out, x_own, m_out, near_out, out_sem,
    d_ss, d_rs,
):
    frames, width, chans, patch, peers, clips = dims
    seq, clip = lax.axis_index("seq"), lax.axis_index("clip")
    depth = embed_ref.shape[1]
    share = ecut_ref.shape[1]
    part = w_ref.shape[2]
    chunk = patch // clips
    on_seq = [{"seq": flip(seq, k)} for k in range(1, peers)]
    on_clip = [{"clip": flip(clip, k)} for k in range(1, clips)]
    mate = on_clip[0]
    core, chip = lax.rem(clip, 2), clip // 2

    barrier = pltpu.get_barrier_semaphore()
    for who in on_seq + on_clip:
        pl.semaphore_signal(barrier, inc=1, device_id=who, device_id_type=MESH)

    def cut(ref):
        if ref.shape[-1] == share:
            return ref
        return ref.at[:, pl.ds(pl.multiple_of(clip * share, share), share)]

    pairs = [(f_hbm, f_ref), (enc_hbm, enc_ref), (cut(ecut_hbm), ecut_ref), (cut(gcut_hbm), gcut_ref)]
    pairs += [(w_hbm.at[i], w_ref.at[i]) for i in range(3)]
    pairs += [
        (cut(tcut_hbm), tcut_ref), (noise_hbm, noise_ref), (embed_hbm, embed_ref.at[:patch]), (time_hbm, time_ref),
    ]
    loads = [pltpu.make_async_copy(src, dst, load_sem.at[k]) for k, (src, dst) in enumerate(pairs)]
    for load in loads:
        load.start()
    f_load, enc_load, ecut_load, gcut_load, w0, w1, w2, tcut_load, noise_load, embed_load, time_load = loads
    flow_r = flow_ref[0, 0].astype(F32) / TGRID
    flow_t = flow_ref[0, 1].astype(F32) / TGRID
    quarter = TFEAT // 4
    order = lax.broadcasted_iota(jnp.int32, (8, TFEAT), 1)
    line = lax.broadcasted_iota(jnp.int32, (8, TFEAT), 0)
    omega = 8.0 * jnp.exp(-np.float32(np.log(100.0)) * lax.rem(order, quarter).astype(F32) / quarter)
    angle = omega * jnp.where(order < 2 * quarter, flow_t, flow_t - flow_r)
    sine, cosine = jnp.sin(angle), jnp.cos(angle)
    first = lax.rem(order // quarter, 2) == 0
    feats_ref[...] = jnp.where(
        line == 0,
        jnp.where(first, sine, cosine),
        jnp.where(line == 1, jnp.where(first, omega * cosine, -omega * sine), 0.0),
    )
    sent = []

    def push(src, dst, ssem, rsem, who):
        copy = pltpu.make_async_remote_copy(
            src_ref=src, dst_ref=dst, send_sem=ssem, recv_sem=rsem, device_id=who, device_id_type=MESH
        )
        copy.start()
        sent.append(copy)
        return copy

    f_load.wait()
    enc_load.wait()
    own, edge = conv_part(f_ref, enc_ref, frames, width, chans)

    places = lax.broadcasted_iota(jnp.int32, (own.shape[1], source_ref.shape[1]), 0)
    pick = (places == source_ref[...]).astype(F32).astype(BF16)
    pl.semaphore_wait(barrier, len(on_seq) + len(on_clip))
    feats_in = [
        push(feats_ref, feats_buf.at[clip], feats_send.at[k], feats_recv.at[k], who) for k, who in enumerate(on_clip)
    ]
    feats_buf[clip] = feats_ref[...]

    ecut_load.wait()
    gcut_load.wait()
    gain = gcut_ref[...]
    left = jnp.concatenate(split(ecut_ref[...].astype(F32) * gain, 2), axis=0)
    e_in = []
    for i, load in enumerate((w0, w1, w2)):
        load.wait()
        both = dot(left, w_ref[i])
        both = both[:patch] + both[patch:]
        for c in range(clips):
            e_send[i, c] = both[c * chunk : (c + 1) * chunk].astype(BF16)
        e_in.append([
            push(e_send.at[i, flip(clip, k + 1)], e_recv.at[i, k], e_ss.at[i, k], e_rs.at[i, k], who)
            for k, who in enumerate(on_clip)
        ])
    noise_load.wait()
    noise = jnp.concatenate(
        [noise_ref[f, r] for f in range(frames) for r in range(noise_ref.shape[1])], axis=1
    )
    x_buf[seq] = tokens_part(own, edge, noise, pick, flow_t, chans)
    x_in = [push(x_buf.at[seq], x_buf.at[seq], x_ss.at[k], x_rs.at[k], who) for k, who in enumerate(on_seq)]


    for copy in feats_in:
        copy.wait_recv()
    tcut_load.wait()
    feats = jnp.concatenate([feats_buf[c, :2] for c in range(clips)], axis=0)
    both = dot(jnp.concatenate(split(feats, 2), axis=0), tcut_ref[...])
    left = jnp.concatenate(split((both[: clips * 2] + both[clips * 2 :]) * gain, 2), axis=0)
    for i in range(3):
        both = dot(left, w_ref[i])
        both = both[: clips * 2] + both[clips * 2 :]
        for c in range(clips):
            tau_send[c, :, i * part : (i + 1) * part] = both[c * 2 : c * 2 + 2]
    tau_in = [
        push(tau_send.at[flip(clip, k + 1)], tau_recv.at[k], t_ss.at[k], t_rs.at[k], who)
        for k, who in enumerate(on_clip)
    ]

    for i in range(3):
        for copy in e_in[i]:
            copy.wait_recv()
        total = e_send[i, clip].astype(F32)
        for k in range(clips - 1):
            total = total + e_recv[i, k].astype(F32)
        g_buf[core, chip, 0, :, i * part : (i + 1) * part] = total.astype(BF16)

    b_in = [
        push(g_buf.at[core, chip, 0], g_buf.at[core, chip, k + 1], b_ss.at[k], b_rs.at[k], who)
        for k, who in enumerate(on_seq)
    ]

    runs = [slice(k, k + 1) for k in range(peers)]
    a_in, c_in = [], []

    def spread(n):
        block = g_buf.at[core, chip, runs[n]]
        a_in.append([
            push(block, block, a_ss.at[n, j], a_rs.at[n, j], on_clip[2 * j + 1])
            for j in range(clips // 2 - 1 - (n in LATE))
        ])

    spread(0)
    time_load.wait()
    mine = jnp.concatenate(split(feats_ref[...], 2), axis=0)
    times = dot(mine, time_ref[...])
    times = times[:8] + times[8:]
    time_hi, time_lo = split(times, 2)
    filler = jnp.zeros((LANES - patch - 4, depth), BF16)
    rest = jnp.concatenate([time_hi[:1], time_lo[:1], time_hi[1:2], time_lo[1:2], filler], axis=0)
    embed_ref[patch:] = rest
    embed_load.wait()
    table = embed_ref[...]
    gram_pair = jnp.concatenate(split(dot_nt(table, table), 2), axis=0)

    for copy in tau_in:
        copy.wait_recv()
    total = tau_send[clip]
    for k in range(clips - 1):
        total = total + tau_recv[k]
    tau_buf[0] = total
    bt_in = [
        push(tau_buf.at[0], tau_buf.at[k + 1], bt_ss.at[k], bt_rs.at[k], who) for k, who in enumerate(on_seq)
    ]
    far = flip(chip, clips // 2 - 1)
    d_in = {}

    def relay(n):
        for copy in a_in[n]:
            copy.wait_recv()
        if n == 0:
            for k in LATE:
                d_in[k] = push(
                    g_buf.at[core, far, 0], g_buf.at[core, far, k], d_ss.at[k - 1], d_rs.at[k - 1], on_seq[k - 1]
                )
        if n in d_in:
            d_in[n].wait_recv()
        block = g_buf.at[core, :, runs[n]]
        c_in.append(push(block, block, c_ss.at[n], c_rs.at[n], mate))

    def finish(k, whole, slot):
        if k:
            bt_in[k - 1].wait_recv()
        for c in range(clips):
            whole[slot, c * chunk : (c + 1) * chunk] = g_buf[c % 2, c // 2, k]
        hi = tau_buf[k].astype(BF16).astype(F32)
        lo = tau_buf[k] - hi
        extra = [hi[0:1], hi[0:1], lo[0:1], hi[1:2], hi[1:2], lo[1:2]]
        row = lax.broadcasted_iota(jnp.int32, (TAIL, 3 * part), 0)
        tail = jnp.zeros((TAIL, 3 * part), F32)
        for index, value in enumerate(extra):
            tail = jnp.where(row == index, value, tail)
        whole[slot, patch:] = tail.astype(BF16)

    relay(0)
    for n, run in list(enumerate(runs))[1:]:
        for copy in b_in[run.start - 1 : run.stop - 1]:
            copy.wait_recv()
        spread(n)
    for copy in x_in:
        copy.wait_recv()
    tokens = x_buf.shape[1] * 2 // 3
    for p in range(peers):
        rows, rows_t = norm_part(joined(x_buf, p, flow_t, patch), gram_pair, depth, patch)
        x_out[p * tokens : (p + 1) * tokens, :LANES] = rows
        x_out[p * tokens : (p + 1) * tokens, LANES:] = rows_t
    x_own[:tokens] = x_out[pl.ds(pl.multiple_of(seq * tokens, tokens), tokens), :LANES]
    x_own[tokens:] = x_out[pl.ds(pl.multiple_of(seq * tokens, tokens), tokens), LANES:]
    stores = []

    def save(src, dst):
        stores.append(pltpu.make_async_copy(src, dst, out_sem.at[len(stores)]))
        stores[-1].start()

    save(x_out, x_hbm)
    save(x_own, own_hbm)
    def near_part(k):
        c_in[k].wait_recv()
        finish(k, m_ref, k)

        def store(h, out, out_t):
            near_out[0, k, :, h * HD : (h + 1) * HD] = out
            near_out[1, k, :, h * HD : (h + 1) * HD] = out_t

        attend_heads(x_out, x_own, pieces_of(m_ref, k), store)
        save(near_out.at[:, k], near_hbm.at[:, k])

    def far_part(k):
        c_in[k].wait_recv()
        finish(k, m_out, k - NEAR)
        save(m_out.at[k - NEAR], m_hbm.at[k - NEAR])

    near_part(0)
    for k in range(1, peers):
        relay(k)
    for k in range(1, peers):
        far_part(k)
    for move in stores:
        move.wait()
    for copy in sent:
        copy.wait_send()


def attend_kernel(x_ref, own_ref, m_ref, near_ref, out_hbm, out_t_hbm, far_ref, near_sem, far_sem):
    seq = lax.axis_index("seq")
    part = m_ref.shape[2] // 3
    per = part // HD
    outs = (out_hbm, out_t_hbm)

    def place(k):
        return pl.ds(pl.multiple_of(flip(seq, k) * part, part), part)

    moves = [
        pltpu.make_async_copy(near_ref.at[i, k], outs[i].at[:, place(k)], near_sem.at[i, k])
        for k in range(NEAR) for i in range(2)
    ]
    for move in moves:
        move.start()
    pieces = [piece for k in range(m_ref.shape[0]) for piece in pieces_of(m_ref, k)]

    def store(h, out, out_t):
        k, at = h // per, slice(h % per * HD, (h % per + 1) * HD)
        far_ref[0, k, :, at] = out
        far_ref[1, k, :, at] = out_t
        if h % per == per - 1:
            for i in range(2):
                moves.append(pltpu.make_async_copy(far_ref.at[i, k], outs[i].at[:, place(NEAR + k)], far_sem.at[i, k]))
                moves[-1].start()

    attend_heads(x_ref, own_ref, pieces, store)
    for move in moves:
        move.wait()


VMEM = pl.BlockSpec(memory_space=pltpu.VMEM)


def attend(rows, own, weights, near, inner):
    tokens, far, part = own.shape[0] // 2, weights.shape[0], weights.shape[2] // 3
    shape = jax.ShapeDtypeStruct((tokens, inner), BF16)
    anywhere = pl.BlockSpec(memory_space=pl.ANY)
    return pl.pallas_call(
        attend_kernel,
        out_shape=(shape, shape),
        in_specs=[VMEM, VMEM, VMEM, VMEM],
        out_specs=(anywhere, anywhere),
        scratch_shapes=[
            pltpu.VMEM((2, far, tokens, part), BF16),
            pltpu.SemaphoreType.DMA((2, NEAR)), pltpu.SemaphoreType.DMA((2, far)),
        ],
        name="attend",
    )(rows, own, weights, near)


def local(clip_features, enc_weight, noise_field, flow_times, embed_weight, time_weight, norm_gain, qkv_weight):
    _, frames, rows, width, depth_c = clip_features.shape
    chans = enc_weight.shape[4]
    patch, depth = embed_weight.shape
    peers, clips = lax.axis_size("seq"), lax.axis_size("clip")
    share = qkv_weight.shape[0]
    part = qkv_weight.shape[2]
    pixels = rows * width
    tokens = frames * pixels // 4

    gain, embed_cut, time_cut = norm_gain[None, :], embed_weight, time_weight
    if share % LANES:
        me = lax.axis_index("clip")
        gain, embed_cut, time_cut = (
            lax.dynamic_slice_in_dim(m, me * share, share, 1) for m in (gain, embed_weight, time_weight)
        )
    weight = qkv_weight.transpose(1, 0, 2)
    features = clip_features.reshape(frames, pixels, depth_c)
    enc = enc_weight.transpose(0, 1, 2, 4, 3).reshape(27 * chans, depth_c)
    noise = noise_field[0].transpose(0, 1, 3, 2)
    i, f, j = np.meshgrid(np.arange(rows // 2), np.arange(frames), np.arange(width // 2), indexing="ij")
    source = np.stack(
        [((f * rows + 2 * i + p) * width + 2 * j + q).reshape(-1) for p in range(2) for q in range(2)]
    ).reshape(1, -1)
    source = jnp.asarray(source.astype(np.int32))
    chunk = patch // clips
    dma = pltpu.SemaphoreType.DMA
    anywhere = pl.BlockSpec(memory_space=pl.ANY)
    x, x_own, weights, near = pl.pallas_call(
        functools.partial(front_kernel, (frames, width, chans, patch, peers, clips)),
        out_shape=(
            jax.ShapeDtypeStruct((peers * tokens, 2 * LANES), BF16),
            jax.ShapeDtypeStruct((2 * tokens, LANES), BF16),
            jax.ShapeDtypeStruct((peers - NEAR, patch + TAIL, 3 * part), BF16),
            jax.ShapeDtypeStruct((2, NEAR, tokens, part), BF16),
        ),
        in_specs=[pl.BlockSpec(memory_space=pltpu.SMEM), VMEM] + [anywhere] * 9,
        out_specs=(anywhere,) * 4,
        scratch_shapes=[
            pltpu.VMEM(features.shape, BF16), pltpu.VMEM(enc.shape, BF16), pltpu.VMEM((patch, share), BF16),
            pltpu.VMEM((1, share), F32), pltpu.VMEM(weight.shape, BF16), pltpu.VMEM((TFEAT, share), BF16),
            pltpu.VMEM(noise.shape, F32), pltpu.VMEM((LANES, depth), BF16), pltpu.VMEM(time_weight.shape, BF16),
            dma((11,)), pltpu.VMEM((8, TFEAT), F32),
            pltpu.VMEM((clips, 8, TFEAT), F32), dma((clips - 1,)), dma((clips - 1,)),
            pltpu.VMEM((3, clips, chunk, part), BF16), pltpu.VMEM((3, clips - 1, chunk, part), BF16),
            pltpu.VMEM((clips, 2, 3 * part), F32), pltpu.VMEM((clips - 1, 2, 3 * part), F32),
            dma((3, clips - 1)), dma((3, clips - 1)), dma((clips - 1,)), dma((clips - 1,)),
            pltpu.VMEM((peers, tokens + tokens // 2, LANES), BF16), dma((peers - 1,)), dma((peers - 1,)),
            pltpu.VMEM((2, clips // 2, peers, chunk, 3 * part), BF16), pltpu.VMEM((peers, 2, 3 * part), F32),
            dma((peers - 1,)), dma((peers - 1,)), dma((peers - 1,)), dma((peers - 1,)),
            dma((peers, clips // 2)), dma((peers, clips // 2)), dma((peers,)), dma((peers,)),
            pltpu.VMEM((NEAR, patch + TAIL, 3 * part), BF16), pltpu.VMEM((peers * tokens, 2 * LANES), BF16),
            pltpu.VMEM((2 * tokens, LANES), BF16), pltpu.VMEM((peers - NEAR, patch + TAIL, 3 * part), BF16),
            pltpu.VMEM((2, NEAR, tokens, part), BF16), dma((2 + peers,)),
            dma((peers - 1,)), dma((peers - 1,)),
        ],
        compiler_params=pltpu.CompilerParams(collective_id=0, has_side_effects=True),
        name="front",
    )(flow_times, source, features, enc, embed_cut, gain, weight, time_cut, noise, embed_weight, time_weight)
    output, output_t = attend(x, x_own, weights, near, peers * part)
    return output[None], output_t[None]


def solution(mesh):
    placed = (
        P("clip", None, "seq", None, None),
        P(),
        P("clip", None, "seq", None, None),
        P("clip", None),
        P(),
        P(),
        P(),
        P("clip", None, "seq"),
    )
    return jax.shard_map(
        local,
        mesh=mesh,
        in_specs=placed,
        out_specs=(P("clip", "seq", None), P("clip", "seq", None)),
        check_vma=False,
    )
```

```python
import functools

import jax
import jax.numpy as jnp
import numpy as np
from jax import lax
from jax.experimental import pallas as pl
from jax.experimental.pallas import tpu as pltpu
from jax.sharding import PartitionSpec as P

HD = 128
TFEAT = 256
TGRID = 1000
EPSILON = 1e-06
LANES = 128
TAIL = 16
NEAR = 1
LATE = (1, 2)
F32 = jnp.float32
BF16 = jnp.bfloat16


def split(value, parts):
    terms = []
    for _ in range(parts):
        term = value.astype(BF16)
        terms.append(term)
        value = value - term.astype(F32)
    return terms


def dot(a, b):
    return jnp.dot(a, b, preferred_element_type=F32)


def dot_nt(a, b):
    return lax.dot_general(a, b, (((1,), (1,)), ((), ())), preferred_element_type=F32)


def conv_part(features, weight, frames, width, chans):
    pixels = features.shape[1]
    taps = [dot_nt(weight[...], features[f]) for f in range(frames)]
    lane = lax.broadcasted_iota(jnp.int32, (chans, pixels), 1)
    column = lax.rem(lane, width)
    block = 9 * chans
    own, edge = [], []
    for f in range(frames):
        acc = taps[f][2 * block : 3 * block]
        if f >= 1:
            acc = acc + taps[f - 1][block : 2 * block]
        if f >= 2:
            acc = acc + taps[f - 2][:block]
        rows = []
        for b in range(3):
            part = [acc[(b * 3 + e) * chans : (b * 3 + e + 1) * chans] for e in range(3)]
            total = part[1]
            total = total + jnp.where(column > 0, pltpu.roll(part[0], 1, 1), 0.0)
            total = total + jnp.where(column < width - 1, pltpu.roll(part[2], pixels - 1, 1), 0.0)
            rows.append(total)
        down = pltpu.roll(rows[0], width, 1)
        up = pltpu.roll(rows[2], pixels - width, 1)
        here = rows[1] + jnp.where(lane >= width, down, 0.0)
        own.append(here + jnp.where(lane < pixels - width, up, 0.0))
        edge.append(jnp.where(lane < width, down, up))
    return jnp.concatenate(own, axis=1), jnp.concatenate(edge, axis=1)


def tokens_part(latent, edge, noise, pick, flow_t, chans):
    tokens = pick.shape[1] // 4
    terms = split(latent, 3) + split(noise, 3) + split(edge, 2)
    moved = dot(jnp.concatenate(terms, axis=0), pick)
    part = [moved[k * chans : (k + 1) * chans] for k in range(8)]
    lat, noi, rim = part[0] + part[1] + part[2], part[3] + part[4] + part[5], part[6] + part[7]
    noisy = (1.0 - flow_t) * lat + flow_t * noi
    velocity = noi - lat

    def flipped(*values):
        return jnp.concatenate([v[:, k * tokens : (k + 1) * tokens] for v in values for k in range(4)], axis=0).T

    rim = flipped(rim, jnp.zeros_like(rim))
    rim = rim[: tokens // 2] + pltpu.roll(rim[tokens // 2 :], 4 * chans, 1)
    return jnp.concatenate([flipped(noisy, velocity), rim], axis=0).astype(BF16)


def rim_of(block, tokens):
    rim = block[tokens:].astype(F32)
    return jnp.concatenate([rim, pltpu.roll(rim, LANES // 2, 1)], axis=0)


def joined(x_buf, p, flow_t, patch):
    tokens = x_buf.shape[1] * 2 // 3
    lane = lax.broadcasted_iota(jnp.int32, (tokens, LANES), 1)
    extra = jnp.zeros((tokens, LANES), F32)
    if p > 0:
        extra = jnp.where(lane < patch // 2, rim_of(x_buf[p - 1], tokens), extra)
    if p + 1 < x_buf.shape[0]:
        extra = jnp.where((lane >= patch // 2) & (lane < patch), rim_of(x_buf[p + 1], tokens), extra)
    return x_buf[p, :tokens].astype(F32) + (1.0 - flow_t) * extra - pltpu.roll(extra, patch, 1)


def norm_part(raw, gram_pair, depth, patch):
    tokens = raw.shape[0]
    lane = lax.broadcasted_iota(jnp.int32, (tokens, LANES), 1)
    noisy = jnp.where(lane < patch, raw, 0.0)
    velocity = jnp.where(lane < patch, pltpu.roll(raw, LANES - patch, 1), 0.0)
    ones = jnp.where((lane == patch) | (lane == patch + 1), 1.0, noisy)
    ones_t = jnp.where((lane == patch + 2) | (lane == patch + 3), 1.0, velocity)
    left = ones.astype(BF16)
    moved = dot(jnp.concatenate([left, left], axis=1), gram_pair)
    mean_sq = jnp.sum(moved * ones, axis=1, keepdims=True) / depth
    mean_cr = jnp.sum(moved * ones_t, axis=1, keepdims=True) / depth
    inv = lax.rsqrt(mean_sq + EPSILON)
    shift = -(inv * inv * inv) * mean_cr
    inv_hi, inv_lo = [v.astype(F32) for v in split(inv, 2)]
    sh_hi, sh_lo = [v.astype(F32) for v in split(shift, 2)]
    rows, rows_t = noisy * inv, velocity * inv + noisy * shift
    for index, column in enumerate([inv_hi, inv_lo, inv_hi]):
        rows = jnp.where(lane == patch + index, column, rows)
    for index, column in enumerate([sh_hi, sh_lo, sh_hi, inv_hi, inv_lo, inv_hi]):
        rows_t = jnp.where(lane == patch + index, column, rows_t)
    return rows.astype(BF16), rows_t.astype(BF16)


MESH = pl.DeviceIdType.MESH


def attend_heads(x_ref, own_ref, pieces, store):
    tokens = own_ref.shape[0] // 2
    fold = HD ** (-0.5) * np.log2(np.e).astype(np.float32)
    ln2 = np.log(2.0).astype(np.float32)
    zero = jnp.zeros((tokens, LANES), BF16)

    def tall(rows):
        return jnp.concatenate([rows, jnp.zeros((LANES - rows.shape[0], HD), BF16)], axis=0)

    inner = [(dot_nt(tall(q), tall(k)) * fold).astype(BF16) for q, k, _ in pieces]
    u = dot(own_ref[...], jnp.concatenate(inner, axis=1)).astype(BF16)
    ys = []
    for start in range(0, len(pieces), 2):
        group = range(start, min(start + 2, len(pieces)))
        left = []
        for h in group:
            at = slice(h * HD, (h + 1) * HD)
            left.append(jnp.concatenate([u[:tokens, at], zero], axis=1))
            left.append(jnp.concatenate([u[tokens:, at], u[:tokens, at]], axis=1))
        both = dot_nt(jnp.concatenate(left, axis=0), x_ref[...])
        left, invs = [], []
        for g in range(len(group)):
            scores, score_t = both[2 * g * tokens : (2 * g + 1) * tokens], both[(2 * g + 1) * tokens : (2 * g + 2) * tokens]
            expo = jnp.exp2(scores - jnp.max(scores, axis=1, keepdims=True))
            inv = 1.0 / jnp.sum(expo, axis=1, keepdims=True)
            mean = jnp.sum(expo * score_t, axis=1, keepdims=True) * inv
            left += [expo.astype(BF16), (expo * (score_t - mean)).astype(BF16)]
            invs.append(inv)
        both = dot(jnp.concatenate(left, axis=0), x_ref[...])
        for g, inv in enumerate(invs):
            p, pt = both[2 * g * tokens : (2 * g + 1) * tokens], both[(2 * g + 1) * tokens : (2 * g + 2) * tokens]
            y = p[:, :LANES] * inv
            yt = pt[:, :LANES] * (inv * ln2) + p[:, LANES:] * inv
            ys.append(jnp.concatenate(split(jnp.concatenate([y, yt], axis=0), 2), axis=1))
    for h, (_, _, v) in enumerate(pieces):
        both = dot(ys[h], jnp.concatenate([tall(v), tall(v)], axis=0))
        store(h, both[:tokens].astype(BF16), both[tokens:].astype(BF16))


def pieces_of(m_ref, k):
    part = m_ref.shape[2] // 3
    cols = [slice(h * HD, (h + 1) * HD) for h in range(3 * part // HD)]
    per = part // HD
    return [[m_ref[k, :, cols[g * per + h]] for g in range(3)] for h in range(per)]


def flip(index, bits):
    place = 1
    while place <= bits:
        if bits & place:
            index = index + place - 2 * place * lax.rem(index // place, 2)
        place *= 2
    return index


def front_kernel(
    dims,
    flow_ref, source_ref, f_hbm, enc_hbm, ecut_hbm, gcut_hbm, w_hbm, tcut_hbm, noise_hbm, embed_hbm, time_hbm,
    x_hbm, own_hbm, m_hbm, near_hbm,
    f_ref, enc_ref, ecut_ref, gcut_ref, w_ref, tcut_ref, noise_ref, embed_ref, time_ref, load_sem, feats_ref,
    feats_buf, feats_send, feats_recv,
    e_send, e_recv, tau_send, tau_recv, e_ss, e_rs, t_ss, t_rs,
    x_buf, x_ss, x_rs,
    g_buf, tau_buf, b_ss, b_rs, bt_ss, bt_rs, a_ss, a_rs, c_ss, c_rs, m_ref, x_out, x_own, m_out, near_out, out_sem,
    d_ss, d_rs,
):
    frames, width, chans, patch, peers, clips = dims
    seq, clip = lax.axis_index("seq"), lax.axis_index("clip")
    depth = embed_ref.shape[1]
    share = ecut_ref.shape[1]
    part = w_ref.shape[2]
    chunk = patch // clips
    on_seq = [{"seq": flip(seq, k)} for k in range(1, peers)]
    on_clip = [{"clip": flip(clip, k)} for k in range(1, clips)]
    mate = on_clip[0]
    core, chip = lax.rem(clip, 2), clip // 2

    barrier = pltpu.get_barrier_semaphore()
    for who in on_seq + on_clip:
        pl.semaphore_signal(barrier, inc=1, device_id=who, device_id_type=MESH)

    def cut(ref):
        if ref.shape[-1] == share:
            return ref
        return ref.at[:, pl.ds(pl.multiple_of(clip * share, share), share)]

    pairs = [(f_hbm, f_ref), (enc_hbm, enc_ref), (cut(ecut_hbm), ecut_ref), (cut(gcut_hbm), gcut_ref)]
    pairs += [(w_hbm.at[i], w_ref.at[i]) for i in range(3)]
    pairs += [
        (cut(tcut_hbm), tcut_ref), (noise_hbm, noise_ref), (embed_hbm, embed_ref.at[:patch]), (time_hbm, time_ref),
    ]
    loads = [pltpu.make_async_copy(src, dst, load_sem.at[k]) for k, (src, dst) in enumerate(pairs)]
    for load in loads:
        load.start()
    f_load, enc_load, ecut_load, gcut_load, w0, w1, w2, tcut_load, noise_load, embed_load, time_load = loads
    flow_r = flow_ref[0, 0].astype(F32) / TGRID
    flow_t = flow_ref[0, 1].astype(F32) / TGRID
    quarter = TFEAT // 4
    order = lax.broadcasted_iota(jnp.int32, (8, TFEAT), 1)
    line = lax.broadcasted_iota(jnp.int32, (8, TFEAT), 0)
    omega = 8.0 * jnp.exp(-np.float32(np.log(100.0)) * lax.rem(order, quarter).astype(F32) / quarter)
    angle = omega * jnp.where(order < 2 * quarter, flow_t, flow_t - flow_r)
    sine, cosine = jnp.sin(angle), jnp.cos(angle)
    first = lax.rem(order // quarter, 2) == 0
    feats_ref[...] = jnp.where(
        line == 0,
        jnp.where(first, sine, cosine),
        jnp.where(line == 1, jnp.where(first, omega * cosine, -omega * sine), 0.0),
    )
    sent = []

    def push(src, dst, ssem, rsem, who):
        copy = pltpu.make_async_remote_copy(
            src_ref=src, dst_ref=dst, send_sem=ssem, recv_sem=rsem, device_id=who, device_id_type=MESH
        )
        copy.start()
        sent.append(copy)
        return copy

    f_load.wait()
    enc_load.wait()
    own, edge = conv_part(f_ref, enc_ref, frames, width, chans)

    places = lax.broadcasted_iota(jnp.int32, (own.shape[1], source_ref.shape[1]), 0)
    pick = (places == source_ref[...]).astype(F32).astype(BF16)
    pl.semaphore_wait(barrier, len(on_seq) + len(on_clip))
    feats_in = [
        push(feats_ref, feats_buf.at[clip], feats_send.at[k], feats_recv.at[k], who) for k, who in enumerate(on_clip)
    ]
    feats_buf[clip] = feats_ref[...]

    ecut_load.wait()
    gcut_load.wait()
    gain = gcut_ref[...]
    left = jnp.concatenate(split(ecut_ref[...].astype(F32) * gain, 2), axis=0)
    e_in = []
    for i, load in enumerate((w0, w1, w2)):
        load.wait()
        both = dot(left, w_ref[i])
        both = both[:patch] + both[patch:]
        for c in range(clips):
            e_send[i, c] = both[c * chunk : (c + 1) * chunk].astype(BF16)
        e_in.append([
            push(e_send.at[i, flip(clip, k + 1)], e_recv.at[i, k], e_ss.at[i, k], e_rs.at[i, k], who)
            for k, who in enumerate(on_clip)
        ])
    noise_load.wait()
    noise = jnp.concatenate(
        [noise_ref[f, r] for f in range(frames) for r in range(noise_ref.shape[1])], axis=1
    )
    x_buf[seq] = tokens_part(own, edge, noise, pick, flow_t, chans)
    x_in = [push(x_buf.at[seq], x_buf.at[seq], x_ss.at[k], x_rs.at[k], who) for k, who in enumerate(on_seq)]


    for copy in feats_in:
        copy.wait_recv()
    tcut_load.wait()
    feats = jnp.concatenate([feats_buf[c, :2] for c in range(clips)], axis=0)
    both = dot(jnp.concatenate(split(feats, 2), axis=0), tcut_ref[...])
    left = jnp.concatenate(split((both[: clips * 2] + both[clips * 2 :]) * gain, 2), axis=0)
    for i in range(3):
        both = dot(left, w_ref[i])
        both = both[: clips * 2] + both[clips * 2 :]
        for c in range(clips):
            tau_send[c, :, i * part : (i + 1) * part] = both[c * 2 : c * 2 + 2]
    tau_in = [
        push(tau_send.at[flip(clip, k + 1)], tau_recv.at[k], t_ss.at[k], t_rs.at[k], who)
        for k, who in enumerate(on_clip)
    ]

    for i in range(3):
        for copy in e_in[i]:
            copy.wait_recv()
        total = e_send[i, clip].astype(F32)
        for k in range(clips - 1):
            total = total + e_recv[i, k].astype(F32)
        g_buf[core, chip, 0, :, i * part : (i + 1) * part] = total.astype(BF16)

    b_in = [
        push(g_buf.at[core, chip, 0], g_buf.at[core, chip, k + 1], b_ss.at[k], b_rs.at[k], who)
        for k, who in enumerate(on_seq)
    ]

    runs = [slice(k, k + 1) for k in range(peers)]
    a_in, c_in = [], []

    def spread(n):
        block = g_buf.at[core, chip, runs[n]]
        a_in.append([
            push(block, block, a_ss.at[n, j], a_rs.at[n, j], on_clip[2 * j + 1])
            for j in range(clips // 2 - 1 - (n in LATE))
        ])

    spread(0)
    time_load.wait()
    mine = jnp.concatenate(split(feats_ref[...], 2), axis=0)
    times = dot(mine, time_ref[...])
    times = times[:8] + times[8:]
    time_hi, time_lo = split(times, 2)
    filler = jnp.zeros((LANES - patch - 4, depth), BF16)
    rest = jnp.concatenate([time_hi[:1], time_lo[:1], time_hi[1:2], time_lo[1:2], filler], axis=0)
    embed_ref[patch:] = rest
    embed_load.wait()
    table = embed_ref[...]
    gram_pair = jnp.concatenate(split(dot_nt(table, table), 2), axis=0)

    far = flip(chip, clips // 2 - 1)
    d_in = {}

    def relay(n):
        for copy in a_in[n]:
            copy.wait_recv()
        if n == 0:
            for k in LATE:
                d_in[k] = push(
                    g_buf.at[core, far, 0], g_buf.at[core, far, k], d_ss.at[k - 1], d_rs.at[k - 1], on_seq[k - 1]
                )
        if n in d_in:
            d_in[n].wait_recv()
        block = g_buf.at[core, :, runs[n]]
        c_in.append(push(block, block, c_ss.at[n], c_rs.at[n], mate))

    def finish(k, whole, slot):
        if k:
            bt_in[k - 1].wait_recv()
        for c in range(clips):
            whole[slot, c * chunk : (c + 1) * chunk] = g_buf[c % 2, c // 2, k]
        hi = tau_buf[k].astype(BF16).astype(F32)
        lo = tau_buf[k] - hi
        extra = [hi[0:1], hi[0:1], lo[0:1], hi[1:2], hi[1:2], lo[1:2]]
        row = lax.broadcasted_iota(jnp.int32, (TAIL, 3 * part), 0)
        tail = jnp.zeros((TAIL, 3 * part), F32)
        for index, value in enumerate(extra):
            tail = jnp.where(row == index, value, tail)
        whole[slot, patch:] = tail.astype(BF16)

    relay(0)
    for n, run in list(enumerate(runs))[1:]:
        for copy in b_in[run.start - 1 : run.stop - 1]:
            copy.wait_recv()
        spread(n)
    for copy in tau_in:
        copy.wait_recv()
    total = tau_send[clip]
    for k in range(clips - 1):
        total = total + tau_recv[k]
    tau_buf[0] = total
    bt_in = [
        push(tau_buf.at[0], tau_buf.at[k + 1], bt_ss.at[k], bt_rs.at[k], who) for k, who in enumerate(on_seq)
    ]
    for copy in x_in:
        copy.wait_recv()
    tokens = x_buf.shape[1] * 2 // 3
    for p in range(peers):
        rows, rows_t = norm_part(joined(x_buf, p, flow_t, patch), gram_pair, depth, patch)
        x_out[p * tokens : (p + 1) * tokens, :LANES] = rows
        x_out[p * tokens : (p + 1) * tokens, LANES:] = rows_t
    x_own[:tokens] = x_out[pl.ds(pl.multiple_of(seq * tokens, tokens), tokens), :LANES]
    x_own[tokens:] = x_out[pl.ds(pl.multiple_of(seq * tokens, tokens), tokens), LANES:]
    stores = []

    def save(src, dst):
        stores.append(pltpu.make_async_copy(src, dst, out_sem.at[len(stores)]))
        stores[-1].start()

    save(x_out, x_hbm)
    save(x_own, own_hbm)
    def near_part(k):
        c_in[k].wait_recv()
        finish(k, m_ref, k)

        def store(h, out, out_t):
            near_out[0, k, :, h * HD : (h + 1) * HD] = out
            near_out[1, k, :, h * HD : (h + 1) * HD] = out_t

        attend_heads(x_out, x_own, pieces_of(m_ref, k), store)
        save(near_out.at[:, k], near_hbm.at[:, k])

    def far_part(k):
        c_in[k].wait_recv()
        finish(k, m_out, k - NEAR)
        save(m_out.at[k - NEAR], m_hbm.at[k - NEAR])

    near_part(0)
    for k in range(1, peers):
        relay(k)
    for k in range(1, peers):
        far_part(k)
    for move in stores:
        move.wait()
    for copy in sent:
        copy.wait_send()


def attend_kernel(x_ref, own_ref, m_ref, near_ref, out_hbm, out_t_hbm, far_ref, near_sem, far_sem):
    seq = lax.axis_index("seq")
    part = m_ref.shape[2] // 3
    per = part // HD
    outs = (out_hbm, out_t_hbm)

    def place(k):
        return pl.ds(pl.multiple_of(flip(seq, k) * part, part), part)

    moves = [
        pltpu.make_async_copy(near_ref.at[i, k], outs[i].at[:, place(k)], near_sem.at[i, k])
        for k in range(NEAR) for i in range(2)
    ]
    for move in moves:
        move.start()
    pieces = [piece for k in range(m_ref.shape[0]) for piece in pieces_of(m_ref, k)]

    def store(h, out, out_t):
        k, at = h // per, slice(h % per * HD, (h % per + 1) * HD)
        far_ref[0, k, :, at] = out
        far_ref[1, k, :, at] = out_t
        if h % per == per - 1:
            for i in range(2):
                moves.append(pltpu.make_async_copy(far_ref.at[i, k], outs[i].at[:, place(NEAR + k)], far_sem.at[i, k]))
                moves[-1].start()

    attend_heads(x_ref, own_ref, pieces, store)
    for move in moves:
        move.wait()


VMEM = pl.BlockSpec(memory_space=pltpu.VMEM)


def attend(rows, own, weights, near, inner):
    tokens, far, part = own.shape[0] // 2, weights.shape[0], weights.shape[2] // 3
    shape = jax.ShapeDtypeStruct((tokens, inner), BF16)
    anywhere = pl.BlockSpec(memory_space=pl.ANY)
    return pl.pallas_call(
        attend_kernel,
        out_shape=(shape, shape),
        in_specs=[VMEM, VMEM, VMEM, VMEM],
        out_specs=(anywhere, anywhere),
        scratch_shapes=[
            pltpu.VMEM((2, far, tokens, part), BF16),
            pltpu.SemaphoreType.DMA((2, NEAR)), pltpu.SemaphoreType.DMA((2, far)),
        ],
        name="attend",
    )(rows, own, weights, near)


def local(clip_features, enc_weight, noise_field, flow_times, embed_weight, time_weight, norm_gain, qkv_weight):
    _, frames, rows, width, depth_c = clip_features.shape
    chans = enc_weight.shape[4]
    patch, depth = embed_weight.shape
    peers, clips = lax.axis_size("seq"), lax.axis_size("clip")
    share = qkv_weight.shape[0]
    part = qkv_weight.shape[2]
    pixels = rows * width
    tokens = frames * pixels // 4

    gain, embed_cut, time_cut = norm_gain[None, :], embed_weight, time_weight
    if share % LANES:
        me = lax.axis_index("clip")
        gain, embed_cut, time_cut = (
            lax.dynamic_slice_in_dim(m, me * share, share, 1) for m in (gain, embed_weight, time_weight)
        )
    weight = qkv_weight.transpose(1, 0, 2)
    features = clip_features.reshape(frames, pixels, depth_c)
    enc = enc_weight.transpose(0, 1, 2, 4, 3).reshape(27 * chans, depth_c)
    noise = noise_field[0].transpose(0, 1, 3, 2)
    i, f, j = np.meshgrid(np.arange(rows // 2), np.arange(frames), np.arange(width // 2), indexing="ij")
    source = np.stack(
        [((f * rows + 2 * i + p) * width + 2 * j + q).reshape(-1) for p in range(2) for q in range(2)]
    ).reshape(1, -1)
    source = jnp.asarray(source.astype(np.int32))
    chunk = patch // clips
    dma = pltpu.SemaphoreType.DMA
    anywhere = pl.BlockSpec(memory_space=pl.ANY)
    x, x_own, weights, near = pl.pallas_call(
        functools.partial(front_kernel, (frames, width, chans, patch, peers, clips)),
        out_shape=(
            jax.ShapeDtypeStruct((peers * tokens, 2 * LANES), BF16),
            jax.ShapeDtypeStruct((2 * tokens, LANES), BF16),
            jax.ShapeDtypeStruct((peers - NEAR, patch + TAIL, 3 * part), BF16),
            jax.ShapeDtypeStruct((2, NEAR, tokens, part), BF16),
        ),
        in_specs=[pl.BlockSpec(memory_space=pltpu.SMEM), VMEM] + [anywhere] * 9,
        out_specs=(anywhere,) * 4,
        scratch_shapes=[
            pltpu.VMEM(features.shape, BF16), pltpu.VMEM(enc.shape, BF16), pltpu.VMEM((patch, share), BF16),
            pltpu.VMEM((1, share), F32), pltpu.VMEM(weight.shape, BF16), pltpu.VMEM((TFEAT, share), BF16),
            pltpu.VMEM(noise.shape, F32), pltpu.VMEM((LANES, depth), BF16), pltpu.VMEM(time_weight.shape, BF16),
            dma((11,)), pltpu.VMEM((8, TFEAT), F32),
            pltpu.VMEM((clips, 8, TFEAT), F32), dma((clips - 1,)), dma((clips - 1,)),
            pltpu.VMEM((3, clips, chunk, part), BF16), pltpu.VMEM((3, clips - 1, chunk, part), BF16),
            pltpu.VMEM((clips, 2, 3 * part), F32), pltpu.VMEM((clips - 1, 2, 3 * part), F32),
            dma((3, clips - 1)), dma((3, clips - 1)), dma((clips - 1,)), dma((clips - 1,)),
            pltpu.VMEM((peers, tokens + tokens // 2, LANES), BF16), dma((peers - 1,)), dma((peers - 1,)),
            pltpu.VMEM((2, clips // 2, peers, chunk, 3 * part), BF16), pltpu.VMEM((peers, 2, 3 * part), F32),
            dma((peers - 1,)), dma((peers - 1,)), dma((peers - 1,)), dma((peers - 1,)),
            dma((peers, clips // 2)), dma((peers, clips // 2)), dma((peers,)), dma((peers,)),
            pltpu.VMEM((NEAR, patch + TAIL, 3 * part), BF16), pltpu.VMEM((peers * tokens, 2 * LANES), BF16),
            pltpu.VMEM((2 * tokens, LANES), BF16), pltpu.VMEM((peers - NEAR, patch + TAIL, 3 * part), BF16),
            pltpu.VMEM((2, NEAR, tokens, part), BF16), dma((2 + peers,)),
            dma((peers - 1,)), dma((peers - 1,)),
        ],
        compiler_params=pltpu.CompilerParams(collective_id=0, has_side_effects=True),
        name="front",
    )(flow_times, source, features, enc, embed_cut, gain, weight, time_cut, noise, embed_weight, time_weight)
    output, output_t = attend(x, x_own, weights, near, peers * part)
    return output[None], output_t[None]


def solution(mesh):
    placed = (
        P("clip", None, "seq", None, None),
        P(),
        P("clip", None, "seq", None, None),
        P("clip", None),
        P(),
        P(),
        P(),
        P("clip", None, "seq"),
    )
    return jax.shard_map(
        local,
        mesh=mesh,
        in_specs=placed,
        out_specs=(P("clip", "seq", None), P("clip", "seq", None)),
        check_vma=False,
    )
```

```python
import functools

import jax
import jax.numpy as jnp
import numpy as np
from jax import lax
from jax.experimental import pallas as pl
from jax.experimental.pallas import tpu as pltpu
from jax.sharding import PartitionSpec as P

HD = 128
TFEAT = 256
TGRID = 1000
EPSILON = 1e-06
LANES = 128
TAIL = 16
NEAR = 1
LATE = (1, 2)
F32 = jnp.float32
BF16 = jnp.bfloat16


def split(value, parts):
    terms = []
    for _ in range(parts):
        term = value.astype(BF16)
        terms.append(term)
        value = value - term.astype(F32)
    return terms


def dot(a, b):
    return jnp.dot(a, b, preferred_element_type=F32)


def dot_nt(a, b):
    return lax.dot_general(a, b, (((1,), (1,)), ((), ())), preferred_element_type=F32)


def conv_part(features, weight, frames, width, chans):
    pixels = features.shape[1]
    taps = [dot_nt(weight[...], features[f]) for f in range(frames)]
    lane = lax.broadcasted_iota(jnp.int32, (chans, pixels), 1)
    column = lax.rem(lane, width)
    block = 9 * chans
    own, edge = [], []
    for f in range(frames):
        acc = taps[f][2 * block : 3 * block]
        if f >= 1:
            acc = acc + taps[f - 1][block : 2 * block]
        if f >= 2:
            acc = acc + taps[f - 2][:block]
        rows = []
        for b in range(3):
            part = [acc[(b * 3 + e) * chans : (b * 3 + e + 1) * chans] for e in range(3)]
            total = part[1]
            total = total + jnp.where(column > 0, pltpu.roll(part[0], 1, 1), 0.0)
            total = total + jnp.where(column < width - 1, pltpu.roll(part[2], pixels - 1, 1), 0.0)
            rows.append(total)
        down = pltpu.roll(rows[0], width, 1)
        up = pltpu.roll(rows[2], pixels - width, 1)
        here = rows[1] + jnp.where(lane >= width, down, 0.0)
        own.append(here + jnp.where(lane < pixels - width, up, 0.0))
        edge.append(jnp.where(lane < width, down, up))
    return jnp.concatenate(own, axis=1), jnp.concatenate(edge, axis=1)


def tokens_part(latent, edge, noise, pick, flow_t, chans):
    tokens = pick.shape[1] // 4
    terms = split(latent, 3) + split(noise, 3) + split(edge, 2)
    moved = dot(jnp.concatenate(terms, axis=0), pick)
    part = [moved[k * chans : (k + 1) * chans] for k in range(8)]
    lat, noi, rim = part[0] + part[1] + part[2], part[3] + part[4] + part[5], part[6] + part[7]
    noisy = (1.0 - flow_t) * lat + flow_t * noi
    velocity = noi - lat

    def flipped(*values):
        return jnp.concatenate([v[:, k * tokens : (k + 1) * tokens] for v in values for k in range(4)], axis=0).T

    rim = flipped(rim, jnp.zeros_like(rim))
    rim = rim[: tokens // 2] + pltpu.roll(rim[tokens // 2 :], 4 * chans, 1)
    return jnp.concatenate([flipped(noisy, velocity), rim], axis=0).astype(BF16)


def rim_of(block, tokens):
    rim = block[tokens:].astype(F32)
    return jnp.concatenate([rim, pltpu.roll(rim, LANES // 2, 1)], axis=0)


def joined(x_buf, p, flow_t, patch):
    tokens = x_buf.shape[1] * 2 // 3
    lane = lax.broadcasted_iota(jnp.int32, (tokens, LANES), 1)
    extra = jnp.zeros((tokens, LANES), F32)
    if p > 0:
        extra = jnp.where(lane < patch // 2, rim_of(x_buf[p - 1], tokens), extra)
    if p + 1 < x_buf.shape[0]:
        extra = jnp.where((lane >= patch // 2) & (lane < patch), rim_of(x_buf[p + 1], tokens), extra)
    return x_buf[p, :tokens].astype(F32) + (1.0 - flow_t) * extra - pltpu.roll(extra, patch, 1)


def norm_part(raw, gram_pair, depth, patch):
    tokens = raw.shape[0]
    lane = lax.broadcasted_iota(jnp.int32, (tokens, LANES), 1)
    noisy = jnp.where(lane < patch, raw, 0.0)
    velocity = jnp.where(lane < patch, pltpu.roll(raw, LANES - patch, 1), 0.0)
    ones = jnp.where((lane == patch) | (lane == patch + 1), 1.0, noisy)
    ones_t = jnp.where((lane == patch + 2) | (lane == patch + 3), 1.0, velocity)
    left = ones.astype(BF16)
    moved = dot(jnp.concatenate([left, left], axis=1), gram_pair)
    mean_sq = jnp.sum(moved * ones, axis=1, keepdims=True) / depth
    mean_cr = jnp.sum(moved * ones_t, axis=1, keepdims=True) / depth
    inv = lax.rsqrt(mean_sq + EPSILON)
    shift = -(inv * inv * inv) * mean_cr
    inv_hi, inv_lo = [v.astype(F32) for v in split(inv, 2)]
    sh_hi, sh_lo = [v.astype(F32) for v in split(shift, 2)]
    rows, rows_t = noisy * inv, velocity * inv + noisy * shift
    for index, column in enumerate([inv_hi, inv_lo, inv_hi]):
        rows = jnp.where(lane == patch + index, column, rows)
    for index, column in enumerate([sh_hi, sh_lo, sh_hi, inv_hi, inv_lo, inv_hi]):
        rows_t = jnp.where(lane == patch + index, column, rows_t)
    return rows.astype(BF16), rows_t.astype(BF16)


MESH = pl.DeviceIdType.MESH


def attend_heads(x_ref, own_ref, pieces, store):
    tokens = own_ref.shape[0] // 2
    fold = HD ** (-0.5) * np.log2(np.e).astype(np.float32)
    ln2 = np.log(2.0).astype(np.float32)
    zero = jnp.zeros((tokens, LANES), BF16)

    def tall(rows):
        return jnp.concatenate([rows, jnp.zeros((LANES - rows.shape[0], HD), BF16)], axis=0)

    inner = [(dot_nt(tall(q), tall(k)) * fold).astype(BF16) for q, k, _ in pieces]
    u = dot(own_ref[...], jnp.concatenate(inner, axis=1)).astype(BF16)
    ys = []
    for start in range(0, len(pieces), 2):
        group = range(start, min(start + 2, len(pieces)))
        left = []
        for h in group:
            at = slice(h * HD, (h + 1) * HD)
            left.append(jnp.concatenate([u[:tokens, at], zero], axis=1))
            left.append(jnp.concatenate([u[tokens:, at], u[:tokens, at]], axis=1))
        both = dot_nt(jnp.concatenate(left, axis=0), x_ref[...])
        left, invs = [], []
        for g in range(len(group)):
            scores, score_t = both[2 * g * tokens : (2 * g + 1) * tokens], both[(2 * g + 1) * tokens : (2 * g + 2) * tokens]
            expo = jnp.exp2(scores - jnp.max(scores, axis=1, keepdims=True))
            inv = 1.0 / jnp.sum(expo, axis=1, keepdims=True)
            mean = jnp.sum(expo * score_t, axis=1, keepdims=True) * inv
            left += [expo.astype(BF16), (expo * (score_t - mean)).astype(BF16)]
            invs.append(inv)
        both = dot(jnp.concatenate(left, axis=0), x_ref[...])
        for g, inv in enumerate(invs):
            p, pt = both[2 * g * tokens : (2 * g + 1) * tokens], both[(2 * g + 1) * tokens : (2 * g + 2) * tokens]
            y = p[:, :LANES] * inv
            yt = pt[:, :LANES] * (inv * ln2) + p[:, LANES:] * inv
            ys.append(jnp.concatenate(split(jnp.concatenate([y, yt], axis=0), 2), axis=1))
    for h, (_, _, v) in enumerate(pieces):
        both = dot(ys[h], jnp.concatenate([tall(v), tall(v)], axis=0))
        store(h, both[:tokens].astype(BF16), both[tokens:].astype(BF16))


def pieces_of(m_ref, k):
    part = m_ref.shape[2] // 3
    cols = [slice(h * HD, (h + 1) * HD) for h in range(3 * part // HD)]
    per = part // HD
    return [[m_ref[k, :, cols[g * per + h]] for g in range(3)] for h in range(per)]


def flip(index, bits):
    place = 1
    while place <= bits:
        if bits & place:
            index = index + place - 2 * place * lax.rem(index // place, 2)
        place *= 2
    return index


def front_kernel(
    dims,
    flow_ref, source_ref, f_hbm, enc_hbm, ecut_hbm, gcut_hbm, w_hbm, tcut_hbm, noise_hbm, embed_hbm, time_hbm,
    x_hbm, own_hbm, m_hbm, near_hbm,
    f_ref, enc_ref, ecut_ref, gcut_ref, w_ref, tcut_ref, noise_ref, embed_ref, time_ref, load_sem, feats_ref,
    feats_buf, feats_send, feats_recv,
    e_send, e_recv, tau_send, tau_recv, e_ss, e_rs, t_ss, t_rs,
    x_buf, x_ss, x_rs,
    g_buf, tau_buf, b_ss, b_rs, bt_ss, bt_rs, a_ss, a_rs, c_ss, c_rs, m_ref, x_out, x_own, m_out, near_out, out_sem,
    d_ss, d_rs,
):
    frames, width, chans, patch, peers, clips = dims
    seq, clip = lax.axis_index("seq"), lax.axis_index("clip")
    depth = embed_ref.shape[1]
    share = ecut_ref.shape[1]
    part = w_ref.shape[2]
    chunk = patch // clips
    on_seq = [{"seq": flip(seq, k)} for k in range(1, peers)]
    on_clip = [{"clip": flip(clip, k)} for k in range(1, clips)]
    mate = on_clip[0]
    core, chip = lax.rem(clip, 2), clip // 2

    barrier = pltpu.get_barrier_semaphore()
    for who in on_seq + on_clip:
        pl.semaphore_signal(barrier, inc=1, device_id=who, device_id_type=MESH)

    def cut(ref):
        if ref.shape[-1] == share:
            return ref
        return ref.at[:, pl.ds(pl.multiple_of(clip * share, share), share)]

    pairs = [(f_hbm, f_ref), (enc_hbm, enc_ref), (cut(ecut_hbm), ecut_ref), (cut(gcut_hbm), gcut_ref)]
    pairs += [(w_hbm.at[i], w_ref.at[i]) for i in range(3)]
    pairs += [
        (cut(tcut_hbm), tcut_ref), (noise_hbm, noise_ref), (embed_hbm, embed_ref.at[:patch]), (time_hbm, time_ref),
    ]
    loads = [pltpu.make_async_copy(src, dst, load_sem.at[k]) for k, (src, dst) in enumerate(pairs)]
    for load in loads:
        load.start()
    f_load, enc_load, ecut_load, gcut_load, w0, w1, w2, tcut_load, noise_load, embed_load, time_load = loads
    flow_r = flow_ref[0, 0].astype(F32) / TGRID
    flow_t = flow_ref[0, 1].astype(F32) / TGRID
    quarter = TFEAT // 4
    order = lax.broadcasted_iota(jnp.int32, (8, TFEAT), 1)
    line = lax.broadcasted_iota(jnp.int32, (8, TFEAT), 0)
    omega = 8.0 * jnp.exp(-np.float32(np.log(100.0)) * lax.rem(order, quarter).astype(F32) / quarter)
    angle = omega * jnp.where(order < 2 * quarter, flow_t, flow_t - flow_r)
    sine, cosine = jnp.sin(angle), jnp.cos(angle)
    first = lax.rem(order // quarter, 2) == 0
    feats_ref[...] = jnp.where(
        line == 0,
        jnp.where(first, sine, cosine),
        jnp.where(line == 1, jnp.where(first, omega * cosine, -omega * sine), 0.0),
    )
    sent = []

    def push(src, dst, ssem, rsem, who):
        copy = pltpu.make_async_remote_copy(
            src_ref=src, dst_ref=dst, send_sem=ssem, recv_sem=rsem, device_id=who, device_id_type=MESH
        )
        copy.start()
        sent.append(copy)
        return copy

    f_load.wait()
    enc_load.wait()
    own, edge = conv_part(f_ref, enc_ref, frames, width, chans)

    places = lax.broadcasted_iota(jnp.int32, (own.shape[1], source_ref.shape[1]), 0)
    pick = (places == source_ref[...]).astype(F32).astype(BF16)
    pl.semaphore_wait(barrier, len(on_seq) + len(on_clip))
    feats_in = [
        push(feats_ref, feats_buf.at[clip], feats_send.at[k], feats_recv.at[k], who) for k, who in enumerate(on_clip)
    ]
    feats_buf[clip] = feats_ref[...]

    ecut_load.wait()
    gcut_load.wait()
    gain = gcut_ref[...]
    left = jnp.concatenate(split(ecut_ref[...].astype(F32) * gain, 2), axis=0)
    e_in = []
    for i, load in enumerate((w0, w1, w2)):
        load.wait()
        both = dot(left, w_ref[i])
        both = both[:patch] + both[patch:]
        for c in range(clips):
            e_send[i, c] = both[c * chunk : (c + 1) * chunk].astype(BF16)
        e_in.append([
            push(e_send.at[i, flip(clip, k + 1)], e_recv.at[i, k], e_ss.at[i, k], e_rs.at[i, k], who)
            for k, who in enumerate(on_clip)
        ])
    noise_load.wait()
    noise = jnp.concatenate(
        [noise_ref[f, r] for f in range(frames) for r in range(noise_ref.shape[1])], axis=1
    )
    x_buf[seq] = tokens_part(own, edge, noise, pick, flow_t, chans)
    x_in = [push(x_buf.at[seq], x_buf.at[seq], x_ss.at[k], x_rs.at[k], who) for k, who in enumerate(on_seq)]


    for copy in feats_in:
        copy.wait_recv()
    tcut_load.wait()
    feats = jnp.concatenate([feats_buf[c, :2] for c in range(clips)], axis=0)
    both = dot(jnp.concatenate(split(feats, 2), axis=0), tcut_ref[...])
    left = jnp.concatenate(split((both[: clips * 2] + both[clips * 2 :]) * gain, 2), axis=0)
    for i in range(3):
        both = dot(left, w_ref[i])
        both = both[: clips * 2] + both[clips * 2 :]
        for c in range(clips):
            tau_send[c, :, i * part : (i + 1) * part] = both[c * 2 : c * 2 + 2]
    tau_in = [
        push(tau_send.at[flip(clip, k + 1)], tau_recv.at[k], t_ss.at[k], t_rs.at[k], who)
        for k, who in enumerate(on_clip)
    ]

    for i in range(3):
        for copy in e_in[i]:
            copy.wait_recv()
        total = e_send[i, clip].astype(F32)
        for k in range(clips - 1):
            total = total + e_recv[i, k].astype(F32)
        g_buf[core, chip, 0, :, i * part : (i + 1) * part] = total.astype(BF16)

    b_in = [
        push(g_buf.at[core, chip, 0], g_buf.at[core, chip, k + 1], b_ss.at[k], b_rs.at[k], who)
        for k, who in enumerate(on_seq)
    ]

    runs = [slice(k, k + 1) for k in range(peers)]
    a_in, c_in = [], []

    def spread(n):
        block = g_buf.at[core, chip, runs[n]]
        a_in.append([
            push(block, block, a_ss.at[n, j], a_rs.at[n, j], on_clip[2 * j + 1])
            for j in range(clips // 2 - 1 - (n in LATE))
        ])

    spread(0)
    time_load.wait()
    mine = jnp.concatenate(split(feats_ref[...], 2), axis=0)
    times = dot(mine, time_ref[...])
    times = times[:8] + times[8:]
    time_hi, time_lo = split(times, 2)
    filler = jnp.zeros((LANES - patch - 4, depth), BF16)
    rest = jnp.concatenate([time_hi[:1], time_lo[:1], time_hi[1:2], time_lo[1:2], filler], axis=0)
    embed_ref[patch:] = rest
    embed_load.wait()
    table = embed_ref[...]
    gram_pair = jnp.concatenate(split(dot_nt(table, table), 2), axis=0)

    far = flip(chip, clips // 2 - 1)
    d_in = {}

    def relay(n):
        for copy in a_in[n]:
            copy.wait_recv()
        if n == 0:
            for k in LATE:
                d_in[k] = push(
                    g_buf.at[core, far, 0], g_buf.at[core, far, k], d_ss.at[k - 1], d_rs.at[k - 1], on_seq[k - 1]
                )
        if n in d_in:
            d_in[n].wait_recv()
        block = g_buf.at[core, :, runs[n]]
        c_in.append(push(block, block, c_ss.at[n], c_rs.at[n], mate))

    def finish(k, whole, slot):
        if k:
            bt_in[k - 1].wait_recv()
        for c in range(clips):
            whole[slot, c * chunk : (c + 1) * chunk] = g_buf[c % 2, c // 2, k]
        hi = tau_buf[k].astype(BF16).astype(F32)
        lo = tau_buf[k] - hi
        extra = [hi[0:1], hi[0:1], lo[0:1], hi[1:2], hi[1:2], lo[1:2]]
        row = lax.broadcasted_iota(jnp.int32, (TAIL, 3 * part), 0)
        tail = jnp.zeros((TAIL, 3 * part), F32)
        for index, value in enumerate(extra):
            tail = jnp.where(row == index, value, tail)
        whole[slot, patch:] = tail.astype(BF16)

    relay(0)
    for n, run in list(enumerate(runs))[1:]:
        for copy in b_in[run.start - 1 : run.stop - 1]:
            copy.wait_recv()
        spread(n)
    for copy in x_in:
        copy.wait_recv()
    tokens = x_buf.shape[1] * 2 // 3
    for p in range(peers):
        rows, rows_t = norm_part(joined(x_buf, p, flow_t, patch), gram_pair, depth, patch)
        x_out[p * tokens : (p + 1) * tokens, :LANES] = rows
        x_out[p * tokens : (p + 1) * tokens, LANES:] = rows_t
    x_own[:tokens] = x_out[pl.ds(pl.multiple_of(seq * tokens, tokens), tokens), :LANES]
    x_own[tokens:] = x_out[pl.ds(pl.multiple_of(seq * tokens, tokens), tokens), LANES:]
    stores = []

    def save(src, dst):
        stores.append(pltpu.make_async_copy(src, dst, out_sem.at[len(stores)]))
        stores[-1].start()

    save(x_out, x_hbm)
    save(x_own, own_hbm)
    def near_part(k):
        c_in[k].wait_recv()
        finish(k, m_ref, k)

        def store(h, out, out_t):
            near_out[0, k, :, h * HD : (h + 1) * HD] = out
            near_out[1, k, :, h * HD : (h + 1) * HD] = out_t

        attend_heads(x_out, x_own, pieces_of(m_ref, k), store)
        save(near_out.at[:, k], near_hbm.at[:, k])

    def far_part(k):
        c_in[k].wait_recv()
        finish(k, m_out, k - NEAR)
        save(m_out.at[k - NEAR], m_hbm.at[k - NEAR])

    for copy in tau_in:
        copy.wait_recv()
    total = tau_send[clip]
    for k in range(clips - 1):
        total = total + tau_recv[k]
    tau_buf[0] = total
    bt_in = [
        push(tau_buf.at[0], tau_buf.at[k + 1], bt_ss.at[k], bt_rs.at[k], who) for k, who in enumerate(on_seq)
    ]
    near_part(0)
    for k in range(1, peers):
        relay(k)
    for k in range(1, peers):
        far_part(k)
    for move in stores:
        move.wait()
    for copy in sent:
        copy.wait_send()


def attend_kernel(x_ref, own_ref, m_ref, near_ref, out_hbm, out_t_hbm, far_ref, near_sem, far_sem):
    seq = lax.axis_index("seq")
    part = m_ref.shape[2] // 3
    per = part // HD
    outs = (out_hbm, out_t_hbm)

    def place(k):
        return pl.ds(pl.multiple_of(flip(seq, k) * part, part), part)

    moves = [
        pltpu.make_async_copy(near_ref.at[i, k], outs[i].at[:, place(k)], near_sem.at[i, k])
        for k in range(NEAR) for i in range(2)
    ]
    for move in moves:
        move.start()
    pieces = [piece for k in range(m_ref.shape[0]) for piece in pieces_of(m_ref, k)]

    def store(h, out, out_t):
        k, at = h // per, slice(h % per * HD, (h % per + 1) * HD)
        far_ref[0, k, :, at] = out
        far_ref[1, k, :, at] = out_t
        if h % per == per - 1:
            for i in range(2):
                moves.append(pltpu.make_async_copy(far_ref.at[i, k], outs[i].at[:, place(NEAR + k)], far_sem.at[i, k]))
                moves[-1].start()

    attend_heads(x_ref, own_ref, pieces, store)
    for move in moves:
        move.wait()


VMEM = pl.BlockSpec(memory_space=pltpu.VMEM)


def attend(rows, own, weights, near, inner):
    tokens, far, part = own.shape[0] // 2, weights.shape[0], weights.shape[2] // 3
    shape = jax.ShapeDtypeStruct((tokens, inner), BF16)
    anywhere = pl.BlockSpec(memory_space=pl.ANY)
    return pl.pallas_call(
        attend_kernel,
        out_shape=(shape, shape),
        in_specs=[VMEM, VMEM, VMEM, VMEM],
        out_specs=(anywhere, anywhere),
        scratch_shapes=[
            pltpu.VMEM((2, far, tokens, part), BF16),
            pltpu.SemaphoreType.DMA((2, NEAR)), pltpu.SemaphoreType.DMA((2, far)),
        ],
        name="attend",
    )(rows, own, weights, near)


def local(clip_features, enc_weight, noise_field, flow_times, embed_weight, time_weight, norm_gain, qkv_weight):
    _, frames, rows, width, depth_c = clip_features.shape
    chans = enc_weight.shape[4]
    patch, depth = embed_weight.shape
    peers, clips = lax.axis_size("seq"), lax.axis_size("clip")
    share = qkv_weight.shape[0]
    part = qkv_weight.shape[2]
    pixels = rows * width
    tokens = frames * pixels // 4

    gain, embed_cut, time_cut = norm_gain[None, :], embed_weight, time_weight
    if share % LANES:
        me = lax.axis_index("clip")
        gain, embed_cut, time_cut = (
            lax.dynamic_slice_in_dim(m, me * share, share, 1) for m in (gain, embed_weight, time_weight)
        )
    weight = qkv_weight.transpose(1, 0, 2)
    features = clip_features.reshape(frames, pixels, depth_c)
    enc = enc_weight.transpose(0, 1, 2, 4, 3).reshape(27 * chans, depth_c)
    noise = noise_field[0].transpose(0, 1, 3, 2)
    i, f, j = np.meshgrid(np.arange(rows // 2), np.arange(frames), np.arange(width // 2), indexing="ij")
    source = np.stack(
        [((f * rows + 2 * i + p) * width + 2 * j + q).reshape(-1) for p in range(2) for q in range(2)]
    ).reshape(1, -1)
    source = jnp.asarray(source.astype(np.int32))
    chunk = patch // clips
    dma = pltpu.SemaphoreType.DMA
    anywhere = pl.BlockSpec(memory_space=pl.ANY)
    x, x_own, weights, near = pl.pallas_call(
        functools.partial(front_kernel, (frames, width, chans, patch, peers, clips)),
        out_shape=(
            jax.ShapeDtypeStruct((peers * tokens, 2 * LANES), BF16),
            jax.ShapeDtypeStruct((2 * tokens, LANES), BF16),
            jax.ShapeDtypeStruct((peers - NEAR, patch + TAIL, 3 * part), BF16),
            jax.ShapeDtypeStruct((2, NEAR, tokens, part), BF16),
        ),
        in_specs=[pl.BlockSpec(memory_space=pltpu.SMEM), VMEM] + [anywhere] * 9,
        out_specs=(anywhere,) * 4,
        scratch_shapes=[
            pltpu.VMEM(features.shape, BF16), pltpu.VMEM(enc.shape, BF16), pltpu.VMEM((patch, share), BF16),
            pltpu.VMEM((1, share), F32), pltpu.VMEM(weight.shape, BF16), pltpu.VMEM((TFEAT, share), BF16),
            pltpu.VMEM(noise.shape, F32), pltpu.VMEM((LANES, depth), BF16), pltpu.VMEM(time_weight.shape, BF16),
            dma((11,)), pltpu.VMEM((8, TFEAT), F32),
            pltpu.VMEM((clips, 8, TFEAT), F32), dma((clips - 1,)), dma((clips - 1,)),
            pltpu.VMEM((3, clips, chunk, part), BF16), pltpu.VMEM((3, clips - 1, chunk, part), BF16),
            pltpu.VMEM((clips, 2, 3 * part), F32), pltpu.VMEM((clips - 1, 2, 3 * part), F32),
            dma((3, clips - 1)), dma((3, clips - 1)), dma((clips - 1,)), dma((clips - 1,)),
            pltpu.VMEM((peers, tokens + tokens // 2, LANES), BF16), dma((peers - 1,)), dma((peers - 1,)),
            pltpu.VMEM((2, clips // 2, peers, chunk, 3 * part), BF16), pltpu.VMEM((peers, 2, 3 * part), F32),
            dma((peers - 1,)), dma((peers - 1,)), dma((peers - 1,)), dma((peers - 1,)),
            dma((peers, clips // 2)), dma((peers, clips // 2)), dma((peers,)), dma((peers,)),
            pltpu.VMEM((NEAR, patch + TAIL, 3 * part), BF16), pltpu.VMEM((peers * tokens, 2 * LANES), BF16),
            pltpu.VMEM((2 * tokens, LANES), BF16), pltpu.VMEM((peers - NEAR, patch + TAIL, 3 * part), BF16),
            pltpu.VMEM((2, NEAR, tokens, part), BF16), dma((2 + peers,)),
            dma((peers - 1,)), dma((peers - 1,)),
        ],
        compiler_params=pltpu.CompilerParams(collective_id=0, has_side_effects=True),
        name="front",
    )(flow_times, source, features, enc, embed_cut, gain, weight, time_cut, noise, embed_weight, time_weight)
    output, output_t = attend(x, x_own, weights, near, peers * part)
    return output[None], output_t[None]


def solution(mesh):
    placed = (
        P("clip", None, "seq", None, None),
        P(),
        P("clip", None, "seq", None, None),
        P("clip", None),
        P(),
        P(),
        P(),
        P("clip", None, "seq"),
    )
    return jax.shard_map(
        local,
        mesh=mesh,
        in_specs=placed,
        out_specs=(P("clip", "seq", None), P("clip", "seq", None)),
        check_vma=False,
    )
```

```python
import functools

import jax
import jax.numpy as jnp
import numpy as np
from jax import lax
from jax.experimental import pallas as pl
from jax.experimental.pallas import tpu as pltpu
from jax.sharding import PartitionSpec as P

HD = 128
TFEAT = 256
TGRID = 1000
EPSILON = 1e-06
LANES = 128
TAIL = 16
NEAR = 1
LATE = (1, 2)
F32 = jnp.float32
BF16 = jnp.bfloat16


def split(value, parts):
    terms = []
    for _ in range(parts):
        term = value.astype(BF16)
        terms.append(term)
        value = value - term.astype(F32)
    return terms


def dot(a, b):
    return jnp.dot(a, b, preferred_element_type=F32)


def dot_nt(a, b):
    return lax.dot_general(a, b, (((1,), (1,)), ((), ())), preferred_element_type=F32)


def conv_part(features, weight, frames, width, chans):
    pixels = features.shape[1]
    taps = [dot_nt(weight[...], features[f]) for f in range(frames)]
    lane = lax.broadcasted_iota(jnp.int32, (chans, pixels), 1)
    column = lax.rem(lane, width)
    block = 9 * chans
    own, edge = [], []
    for f in range(frames):
        acc = taps[f][2 * block : 3 * block]
        if f >= 1:
            acc = acc + taps[f - 1][block : 2 * block]
        if f >= 2:
            acc = acc + taps[f - 2][:block]
        rows = []
        for b in range(3):
            part = [acc[(b * 3 + e) * chans : (b * 3 + e + 1) * chans] for e in range(3)]
            total = part[1]
            total = total + jnp.where(column > 0, pltpu.roll(part[0], 1, 1), 0.0)
            total = total + jnp.where(column < width - 1, pltpu.roll(part[2], pixels - 1, 1), 0.0)
            rows.append(total)
        down = pltpu.roll(rows[0], width, 1)
        up = pltpu.roll(rows[2], pixels - width, 1)
        here = rows[1] + jnp.where(lane >= width, down, 0.0)
        own.append(here + jnp.where(lane < pixels - width, up, 0.0))
        edge.append(jnp.where(lane < width, down, up))
    return jnp.concatenate(own, axis=1), jnp.concatenate(edge, axis=1)


def tokens_part(latent, edge, noise, pick, flow_t, chans):
    tokens = pick.shape[1] // 4
    terms = split(latent, 3) + split(noise, 3) + split(edge, 2)
    moved = dot(jnp.concatenate(terms, axis=0), pick)
    part = [moved[k * chans : (k + 1) * chans] for k in range(8)]
    lat, noi, rim = part[0] + part[1] + part[2], part[3] + part[4] + part[5], part[6] + part[7]
    noisy = (1.0 - flow_t) * lat + flow_t * noi
    velocity = noi - lat

    def flipped(*values):
        return jnp.concatenate([v[:, k * tokens : (k + 1) * tokens] for v in values for k in range(4)], axis=0).T

    rim = flipped(rim, jnp.zeros_like(rim))
    rim = rim[: tokens // 2] + pltpu.roll(rim[tokens // 2 :], 4 * chans, 1)
    return jnp.concatenate([flipped(noisy, velocity), rim], axis=0).astype(BF16)


def rim_of(block, tokens):
    rim = block[tokens:].astype(F32)
    return jnp.concatenate([rim, pltpu.roll(rim, LANES // 2, 1)], axis=0)


def joined(x_buf, p, flow_t, patch):
    tokens = x_buf.shape[1] * 2 // 3
    lane = lax.broadcasted_iota(jnp.int32, (tokens, LANES), 1)
    extra = jnp.zeros((tokens, LANES), F32)
    if p > 0:
        extra = jnp.where(lane < patch // 2, rim_of(x_buf[p - 1], tokens), extra)
    if p + 1 < x_buf.shape[0]:
        extra = jnp.where((lane >= patch // 2) & (lane < patch), rim_of(x_buf[p + 1], tokens), extra)
    return x_buf[p, :tokens].astype(F32) + (1.0 - flow_t) * extra - pltpu.roll(extra, patch, 1)


def norm_part(raw, gram_pair, depth, patch):
    tokens = raw.shape[0]
    lane = lax.broadcasted_iota(jnp.int32, (tokens, LANES), 1)
    noisy = jnp.where(lane < patch, raw, 0.0)
    velocity = jnp.where(lane < patch, pltpu.roll(raw, LANES - patch, 1), 0.0)
    ones = jnp.where((lane == patch) | (lane == patch + 1), 1.0, noisy)
    ones_t = jnp.where((lane == patch + 2) | (lane == patch + 3), 1.0, velocity)
    left = ones.astype(BF16)
    moved = dot(jnp.concatenate([left, left], axis=1), gram_pair)
    mean_sq = jnp.sum(moved * ones, axis=1, keepdims=True) / depth
    mean_cr = jnp.sum(moved * ones_t, axis=1, keepdims=True) / depth
    inv = lax.rsqrt(mean_sq + EPSILON)
    shift = -(inv * inv * inv) * mean_cr
    inv_hi, inv_lo = [v.astype(F32) for v in split(inv, 2)]
    sh_hi, sh_lo = [v.astype(F32) for v in split(shift, 2)]
    rows, rows_t = noisy * inv, velocity * inv + noisy * shift
    for index, column in enumerate([inv_hi, inv_lo, inv_hi]):
        rows = jnp.where(lane == patch + index, column, rows)
    for index, column in enumerate([sh_hi, sh_lo, sh_hi, inv_hi, inv_lo, inv_hi]):
        rows_t = jnp.where(lane == patch + index, column, rows_t)
    return rows.astype(BF16), rows_t.astype(BF16)


MESH = pl.DeviceIdType.MESH


def attend_heads(x_ref, own_ref, pieces, store):
    tokens = own_ref.shape[0] // 2
    fold = HD ** (-0.5) * np.log2(np.e).astype(np.float32)
    ln2 = np.log(2.0).astype(np.float32)
    zero = jnp.zeros((tokens, LANES), BF16)

    def tall(rows):
        return jnp.concatenate([rows, jnp.zeros((LANES - rows.shape[0], HD), BF16)], axis=0)

    inner = [(dot_nt(tall(q), tall(k)) * fold).astype(BF16) for q, k, _ in pieces]
    u = dot(own_ref[...], jnp.concatenate(inner, axis=1)).astype(BF16)
    ys = []
    for start in range(0, len(pieces), 2):
        group = range(start, min(start + 2, len(pieces)))
        left = []
        for h in group:
            at = slice(h * HD, (h + 1) * HD)
            left.append(jnp.concatenate([u[:tokens, at], zero], axis=1))
            left.append(jnp.concatenate([u[tokens:, at], u[:tokens, at]], axis=1))
        both = dot_nt(jnp.concatenate(left, axis=0), x_ref[...])
        left, invs = [], []
        for g in range(len(group)):
            scores, score_t = both[2 * g * tokens : (2 * g + 1) * tokens], both[(2 * g + 1) * tokens : (2 * g + 2) * tokens]
            expo = jnp.exp2(scores - jnp.max(scores, axis=1, keepdims=True))
            inv = 1.0 / jnp.sum(expo, axis=1, keepdims=True)
            mean = jnp.sum(expo * score_t, axis=1, keepdims=True) * inv
            left += [expo.astype(BF16), (expo * (score_t - mean)).astype(BF16)]
            invs.append(inv)
        both = dot(jnp.concatenate(left, axis=0), x_ref[...])
        for g, inv in enumerate(invs):
            p, pt = both[2 * g * tokens : (2 * g + 1) * tokens], both[(2 * g + 1) * tokens : (2 * g + 2) * tokens]
            y = p[:, :LANES] * inv
            yt = pt[:, :LANES] * (inv * ln2) + p[:, LANES:] * inv
            ys.append(jnp.concatenate(split(jnp.concatenate([y, yt], axis=0), 2), axis=1))
    for h, (_, _, v) in enumerate(pieces):
        both = dot(ys[h], jnp.concatenate([tall(v), tall(v)], axis=0))
        store(h, both[:tokens].astype(BF16), both[tokens:].astype(BF16))


def pieces_of(m_ref, k):
    part = m_ref.shape[2] // 3
    cols = [slice(h * HD, (h + 1) * HD) for h in range(3 * part // HD)]
    per = part // HD
    return [[m_ref[k, :, cols[g * per + h]] for g in range(3)] for h in range(per)]


def flip(index, bits):
    place = 1
    while place <= bits:
        if bits & place:
            index = index + place - 2 * place * lax.rem(index // place, 2)
        place *= 2
    return index


def front_kernel(
    dims,
    flow_ref, source_ref, f_hbm, enc_hbm, ecut_hbm, gcut_hbm, w_hbm, tcut_hbm, noise_hbm, embed_hbm, time_hbm,
    x_hbm, own_hbm, m_hbm, near_hbm,
    f_ref, enc_ref, ecut_ref, gcut_ref, w_ref, tcut_ref, noise_ref, embed_ref, time_ref, load_sem, feats_ref,
    feats_buf, feats_send, feats_recv,
    e_send, e_recv, tau_send, tau_recv, e_ss, e_rs, t_ss, t_rs,
    x_buf, x_ss, x_rs,
    g_buf, tau_buf, b_ss, b_rs, bt_ss, bt_rs, a_ss, a_rs, c_ss, c_rs, m_ref, x_out, x_own, m_out, near_out, out_sem,
    d_ss, d_rs,
):
    frames, width, chans, patch, peers, clips = dims
    seq, clip = lax.axis_index("seq"), lax.axis_index("clip")
    depth = embed_ref.shape[1]
    share = ecut_ref.shape[1]
    part = w_ref.shape[2]
    chunk = patch // clips
    on_seq = [{"seq": flip(seq, k)} for k in range(1, peers)]
    on_clip = [{"clip": flip(clip, k)} for k in range(1, clips)]
    mate = on_clip[0]
    core, chip = lax.rem(clip, 2), clip // 2

    barrier = pltpu.get_barrier_semaphore()
    for who in on_seq + on_clip:
        pl.semaphore_signal(barrier, inc=1, device_id=who, device_id_type=MESH)

    def cut(ref):
        if ref.shape[-1] == share:
            return ref
        return ref.at[:, pl.ds(pl.multiple_of(clip * share, share), share)]

    pairs = [(f_hbm, f_ref), (enc_hbm, enc_ref), (cut(ecut_hbm), ecut_ref), (cut(gcut_hbm), gcut_ref)]
    pairs += [(w_hbm.at[i], w_ref.at[i]) for i in range(3)]
    pairs += [
        (cut(tcut_hbm), tcut_ref), (noise_hbm, noise_ref), (embed_hbm, embed_ref.at[:patch]), (time_hbm, time_ref),
    ]
    loads = [pltpu.make_async_copy(src, dst, load_sem.at[k]) for k, (src, dst) in enumerate(pairs)]
    for load in loads:
        load.start()
    f_load, enc_load, ecut_load, gcut_load, w0, w1, w2, tcut_load, noise_load, embed_load, time_load = loads
    flow_r = flow_ref[0, 0].astype(F32) / TGRID
    flow_t = flow_ref[0, 1].astype(F32) / TGRID
    quarter = TFEAT // 4
    order = lax.broadcasted_iota(jnp.int32, (8, TFEAT), 1)
    line = lax.broadcasted_iota(jnp.int32, (8, TFEAT), 0)
    omega = 8.0 * jnp.exp(-np.float32(np.log(100.0)) * lax.rem(order, quarter).astype(F32) / quarter)
    angle = omega * jnp.where(order < 2 * quarter, flow_t, flow_t - flow_r)
    sine, cosine = jnp.sin(angle), jnp.cos(angle)
    first = lax.rem(order // quarter, 2) == 0
    feats_ref[...] = jnp.where(
        line == 0,
        jnp.where(first, sine, cosine),
        jnp.where(line == 1, jnp.where(first, omega * cosine, -omega * sine), 0.0),
    )
    sent = []

    def push(src, dst, ssem, rsem, who):
        copy = pltpu.make_async_remote_copy(
            src_ref=src, dst_ref=dst, send_sem=ssem, recv_sem=rsem, device_id=who, device_id_type=MESH
        )
        copy.start()
        sent.append(copy)
        return copy

    f_load.wait()
    enc_load.wait()
    own, edge = conv_part(f_ref, enc_ref, frames, width, chans)

    places = lax.broadcasted_iota(jnp.int32, (own.shape[1], source_ref.shape[1]), 0)
    pick = (places == source_ref[...]).astype(F32).astype(BF16)
    pl.semaphore_wait(barrier, len(on_seq) + len(on_clip))
    feats_in = [
        push(feats_ref, feats_buf.at[clip], feats_send.at[k], feats_recv.at[k], who) for k, who in enumerate(on_clip)
    ]
    feats_buf[clip] = feats_ref[...]

    ecut_load.wait()
    gcut_load.wait()
    gain = gcut_ref[...]
    left = jnp.concatenate(split(ecut_ref[...].astype(F32) * gain, 2), axis=0)
    e_in = []
    for i, load in enumerate((w0, w1, w2)):
        load.wait()
        both = dot(left, w_ref[i])
        both = both[:patch] + both[patch:]
        for c in range(clips):
            e_send[i, c] = both[c * chunk : (c + 1) * chunk].astype(BF16)
        e_in.append([
            push(e_send.at[i, flip(clip, k + 1)], e_recv.at[i, k], e_ss.at[i, k], e_rs.at[i, k], who)
            for k, who in enumerate(on_clip)
        ])
    noise_load.wait()
    noise = jnp.concatenate(
        [noise_ref[f, r] for f in range(frames) for r in range(noise_ref.shape[1])], axis=1
    )
    x_buf[seq] = tokens_part(own, edge, noise, pick, flow_t, chans)
    x_in = [push(x_buf.at[seq], x_buf.at[seq], x_ss.at[k], x_rs.at[k], who) for k, who in enumerate(on_seq)]


    for copy in feats_in:
        copy.wait_recv()
    tcut_load.wait()
    feats = jnp.concatenate([feats_buf[c, :2] for c in range(clips)], axis=0)
    both = dot(jnp.concatenate(split(feats, 2), axis=0), tcut_ref[...])
    left = jnp.concatenate(split((both[: clips * 2] + both[clips * 2 :]) * gain, 2), axis=0)
    for i in range(3):
        both = dot(left, w_ref[i])
        both = both[: clips * 2] + both[clips * 2 :]
        for c in range(clips):
            tau_send[c, :, i * part : (i + 1) * part] = both[c * 2 : c * 2 + 2]
    tau_in = [
        push(tau_send.at[flip(clip, k + 1)], tau_recv.at[k], t_ss.at[k], t_rs.at[k], who)
        for k, who in enumerate(on_clip)
    ]

    for i in range(3):
        for copy in e_in[i]:
            copy.wait_recv()
        total = e_send[i, clip].astype(F32)
        for k in range(clips - 1):
            total = total + e_recv[i, k].astype(F32)
        g_buf[core, chip, 0, :, i * part : (i + 1) * part] = total.astype(BF16)

    b_in = [
        push(g_buf.at[core, chip, 0], g_buf.at[core, chip, k + 1], b_ss.at[k], b_rs.at[k], who)
        for k, who in enumerate(on_seq)
    ]

    runs = [slice(k, k + 1) for k in range(peers)]
    a_in, c_in = [], []

    def spread(n):
        block = g_buf.at[core, chip, runs[n]]
        a_in.append([
            push(block, block, a_ss.at[n, j], a_rs.at[n, j], on_clip[2 * j + 1])
            for j in range(clips // 2 - 1 - (n in LATE))
        ])

    spread(0)
    time_load.wait()
    mine = jnp.concatenate(split(feats_ref[...], 2), axis=0)
    times = dot(mine, time_ref[...])
    times = times[:8] + times[8:]
    time_hi, time_lo = split(times, 2)
    filler = jnp.zeros((LANES - patch - 4, depth), BF16)
    rest = jnp.concatenate([time_hi[:1], time_lo[:1], time_hi[1:2], time_lo[1:2], filler], axis=0)
    embed_ref[patch:] = rest
    embed_load.wait()
    table = embed_ref[...]
    gram_pair = jnp.concatenate(split(dot_nt(table, table), 2), axis=0)

    far = flip(chip, clips // 2 - 1)
    d_in = {}

    def relay(n):
        for copy in a_in[n]:
            copy.wait_recv()
        if n == 0:
            for k in LATE:
                d_in[k] = push(
                    g_buf.at[core, far, 0], g_buf.at[core, far, k], d_ss.at[k - 1], d_rs.at[k - 1], on_seq[k - 1]
                )
        if n in d_in:
            d_in[n].wait_recv()
        block = g_buf.at[core, :, runs[n]]
        c_in.append(push(block, block, c_ss.at[n], c_rs.at[n], mate))

    def finish(k, whole, slot):
        if k:
            bt_in[k - 1].wait_recv()
        for c in range(clips):
            whole[slot, c * chunk : (c + 1) * chunk] = g_buf[c % 2, c // 2, k]
        hi = tau_buf[k].astype(BF16).astype(F32)
        lo = tau_buf[k] - hi
        extra = [hi[0:1], hi[0:1], lo[0:1], hi[1:2], hi[1:2], lo[1:2]]
        row = lax.broadcasted_iota(jnp.int32, (TAIL, 3 * part), 0)
        tail = jnp.zeros((TAIL, 3 * part), F32)
        for index, value in enumerate(extra):
            tail = jnp.where(row == index, value, tail)
        whole[slot, patch:] = tail.astype(BF16)

    relay(0)
    for n, run in list(enumerate(runs))[1:]:
        for copy in b_in[run.start - 1 : run.stop - 1]:
            copy.wait_recv()
        spread(n)
    for copy in x_in:
        copy.wait_recv()
    tokens = x_buf.shape[1] * 2 // 3
    for p in range(peers):
        rows, rows_t = norm_part(joined(x_buf, p, flow_t, patch), gram_pair, depth, patch)
        x_out[p * tokens : (p + 1) * tokens, :LANES] = rows
        x_out[p * tokens : (p + 1) * tokens, LANES:] = rows_t
    x_own[:tokens] = x_out[pl.ds(pl.multiple_of(seq * tokens, tokens), tokens), :LANES]
    x_own[tokens:] = x_out[pl.ds(pl.multiple_of(seq * tokens, tokens), tokens), LANES:]
    stores = []

    def save(src, dst):
        stores.append(pltpu.make_async_copy(src, dst, out_sem.at[len(stores)]))
        stores[-1].start()

    save(x_out, x_hbm)
    save(x_own, own_hbm)
    def near_part(k):
        c_in[k].wait_recv()
        finish(k, m_ref, k)

        def store(h, out, out_t):
            near_out[0, k, :, h * HD : (h + 1) * HD] = out
            near_out[1, k, :, h * HD : (h + 1) * HD] = out_t

        attend_heads(x_out, x_own, pieces_of(m_ref, k), store)
        save(near_out.at[:, k], near_hbm.at[:, k])

    def far_part(k):
        c_in[k].wait_recv()
        finish(k, m_out, k - NEAR)
        save(m_out.at[k - NEAR], m_hbm.at[k - NEAR])

    for copy in tau_in:
        copy.wait_recv()
    total = tau_send[clip]
    for k in range(clips - 1):
        total = total + tau_recv[k]
    tau_buf[0] = total
    bt_in = [
        push(tau_buf.at[0], tau_buf.at[k + 1], bt_ss.at[k], bt_rs.at[k], who) for k, who in enumerate(on_seq)
    ]
    near_part(0)
    for k in range(1, peers):
        relay(k)
        if k > 1:
            far_part(k - 1)
    far_part(peers - 1)
    for move in stores:
        move.wait()
    for copy in sent:
        copy.wait_send()


def attend_kernel(x_ref, own_ref, m_ref, near_ref, out_hbm, out_t_hbm, far_ref, near_sem, far_sem):
    seq = lax.axis_index("seq")
    part = m_ref.shape[2] // 3
    per = part // HD
    outs = (out_hbm, out_t_hbm)

    def place(k):
        return pl.ds(pl.multiple_of(flip(seq, k) * part, part), part)

    moves = [
        pltpu.make_async_copy(near_ref.at[i, k], outs[i].at[:, place(k)], near_sem.at[i, k])
        for k in range(NEAR) for i in range(2)
    ]
    for move in moves:
        move.start()
    pieces = [piece for k in range(m_ref.shape[0]) for piece in pieces_of(m_ref, k)]

    def store(h, out, out_t):
        k, at = h // per, slice(h % per * HD, (h % per + 1) * HD)
        far_ref[0, k, :, at] = out
        far_ref[1, k, :, at] = out_t
        if h % per == per - 1:
            for i in range(2):
                moves.append(pltpu.make_async_copy(far_ref.at[i, k], outs[i].at[:, place(NEAR + k)], far_sem.at[i, k]))
                moves[-1].start()

    attend_heads(x_ref, own_ref, pieces, store)
    for move in moves:
        move.wait()


VMEM = pl.BlockSpec(memory_space=pltpu.VMEM)


def attend(rows, own, weights, near, inner):
    tokens, far, part = own.shape[0] // 2, weights.shape[0], weights.shape[2] // 3
    shape = jax.ShapeDtypeStruct((tokens, inner), BF16)
    anywhere = pl.BlockSpec(memory_space=pl.ANY)
    return pl.pallas_call(
        attend_kernel,
        out_shape=(shape, shape),
        in_specs=[VMEM, VMEM, VMEM, VMEM],
        out_specs=(anywhere, anywhere),
        scratch_shapes=[
            pltpu.VMEM((2, far, tokens, part), BF16),
            pltpu.SemaphoreType.DMA((2, NEAR)), pltpu.SemaphoreType.DMA((2, far)),
        ],
        name="attend",
    )(rows, own, weights, near)


def local(clip_features, enc_weight, noise_field, flow_times, embed_weight, time_weight, norm_gain, qkv_weight):
    _, frames, rows, width, depth_c = clip_features.shape
    chans = enc_weight.shape[4]
    patch, depth = embed_weight.shape
    peers, clips = lax.axis_size("seq"), lax.axis_size("clip")
    share = qkv_weight.shape[0]
    part = qkv_weight.shape[2]
    pixels = rows * width
    tokens = frames * pixels // 4

    gain, embed_cut, time_cut = norm_gain[None, :], embed_weight, time_weight
    if share % LANES:
        me = lax.axis_index("clip")
        gain, embed_cut, time_cut = (
            lax.dynamic_slice_in_dim(m, me * share, share, 1) for m in (gain, embed_weight, time_weight)
        )
    weight = qkv_weight.transpose(1, 0, 2)
    features = clip_features.reshape(frames, pixels, depth_c)
    enc = enc_weight.transpose(0, 1, 2, 4, 3).reshape(27 * chans, depth_c)
    noise = noise_field[0].transpose(0, 1, 3, 2)
    i, f, j = np.meshgrid(np.arange(rows // 2), np.arange(frames), np.arange(width // 2), indexing="ij")
    source = np.stack(
        [((f * rows + 2 * i + p) * width + 2 * j + q).reshape(-1) for p in range(2) for q in range(2)]
    ).reshape(1, -1)
    source = jnp.asarray(source.astype(np.int32))
    chunk = patch // clips
    dma = pltpu.SemaphoreType.DMA
    anywhere = pl.BlockSpec(memory_space=pl.ANY)
    x, x_own, weights, near = pl.pallas_call(
        functools.partial(front_kernel, (frames, width, chans, patch, peers, clips)),
        out_shape=(
            jax.ShapeDtypeStruct((peers * tokens, 2 * LANES), BF16),
            jax.ShapeDtypeStruct((2 * tokens, LANES), BF16),
            jax.ShapeDtypeStruct((peers - NEAR, patch + TAIL, 3 * part), BF16),
            jax.ShapeDtypeStruct((2, NEAR, tokens, part), BF16),
        ),
        in_specs=[pl.BlockSpec(memory_space=pltpu.SMEM), VMEM] + [anywhere] * 9,
        out_specs=(anywhere,) * 4,
        scratch_shapes=[
            pltpu.VMEM(features.shape, BF16), pltpu.VMEM(enc.shape, BF16), pltpu.VMEM((patch, share), BF16),
            pltpu.VMEM((1, share), F32), pltpu.VMEM(weight.shape, BF16), pltpu.VMEM((TFEAT, share), BF16),
            pltpu.VMEM(noise.shape, F32), pltpu.VMEM((LANES, depth), BF16), pltpu.VMEM(time_weight.shape, BF16),
            dma((11,)), pltpu.VMEM((8, TFEAT), F32),
            pltpu.VMEM((clips, 8, TFEAT), F32), dma((clips - 1,)), dma((clips - 1,)),
            pltpu.VMEM((3, clips, chunk, part), BF16), pltpu.VMEM((3, clips - 1, chunk, part), BF16),
            pltpu.VMEM((clips, 2, 3 * part), F32), pltpu.VMEM((clips - 1, 2, 3 * part), F32),
            dma((3, clips - 1)), dma((3, clips - 1)), dma((clips - 1,)), dma((clips - 1,)),
            pltpu.VMEM((peers, tokens + tokens // 2, LANES), BF16), dma((peers - 1,)), dma((peers - 1,)),
            pltpu.VMEM((2, clips // 2, peers, chunk, 3 * part), BF16), pltpu.VMEM((peers, 2, 3 * part), F32),
            dma((peers - 1,)), dma((peers - 1,)), dma((peers - 1,)), dma((peers - 1,)),
            dma((peers, clips // 2)), dma((peers, clips // 2)), dma((peers,)), dma((peers,)),
            pltpu.VMEM((NEAR, patch + TAIL, 3 * part), BF16), pltpu.VMEM((peers * tokens, 2 * LANES), BF16),
            pltpu.VMEM((2 * tokens, LANES), BF16), pltpu.VMEM((peers - NEAR, patch + TAIL, 3 * part), BF16),
            pltpu.VMEM((2, NEAR, tokens, part), BF16), dma((2 + peers,)),
            dma((peers - 1,)), dma((peers - 1,)),
        ],
        compiler_params=pltpu.CompilerParams(collective_id=0, has_side_effects=True),
        name="front",
    )(flow_times, source, features, enc, embed_cut, gain, weight, time_cut, noise, embed_weight, time_weight)
    output, output_t = attend(x, x_own, weights, near, peers * part)
    return output[None], output_t[None]


def solution(mesh):
    placed = (
        P("clip", None, "seq", None, None),
        P(),
        P("clip", None, "seq", None, None),
        P("clip", None),
        P(),
        P(),
        P(),
        P("clip", None, "seq"),
    )
    return jax.shard_map(
        local,
        mesh=mesh,
        in_specs=placed,
        out_specs=(P("clip", "seq", None), P("clip", "seq", None)),
        check_vma=False,
    )
```
